32 devices in a mesh: section: 2 (over y), dp: 4 (over x, core), tensor: 4 (over z).
Axes of the slice: x: 2, y: 2, z: 4, core: 2. Of those that a mesh axis runs over, the one named last changes fastest.
Arguments:
- text_in: bfloat16 [8, 512, 768], P('dp'), may hold values from -6 to 6
- layout_in: bfloat16 [8, 512, 192], P('dp'), may hold values from -6 to 6
- token_mask: int32 [8, 512], P('dp'), may hold values 0 or 1
- text_cotangent: bfloat16 [8, 512, 768], P('dp'), may hold values from -6 to 6
- layout_cotangent: bfloat16 [8, 512, 192], P('dp'), may hold values from -6 to 6
- text_input_weight: float32 [2, 3, 768, 768], P('section', None, 'dp', 'tensor'), may hold values from -0.21875 to 0.21875
- text_head_bias: float32 [2, 2, 768], P('section', None, ('tensor', 'dp')), may hold values from -3 to 3
- text_output_weight: float32 [2, 768, 768], P('section', 'tensor', 'dp'), may hold values from -0.4375 to 0.4375
- text_gains: float32 [2, 2, 768], P('section', None, 'dp'), may hold values from 0.1 to 1.9
- text_shifts: float32 [2, 4, 768], P('section', None, 'dp'), may hold values from -3 to 3
- text_up_weight: float32 [2, 768, 3072], P('section', 'dp', 'tensor'), may hold values from -0.21875 to 0.21875
- text_up_bias: float32 [2, 3072], P('section', ('tensor', 'dp')), may hold values from -3 to 3
- text_down_weight: float32 [2, 3072, 768], P('section', 'tensor', 'dp'), may hold values from -0.109375 to 0.109375
- layout_input_weight: float32 [2, 3, 192, 192], P('section', None, 'dp', 'tensor'), may hold values from -0.4375 to 0.4375
- layout_head_bias: float32 [2, 2, 192], P('section', None, ('tensor', 'dp')), may hold values from -3 to 3
- layout_output_weight: float32 [2, 192, 192], P('section', 'tensor', 'dp'), may hold values from -0.875 to 0.875
- layout_gains: float32 [2, 2, 192], P('section', None, 'dp'), may hold values from 0.1 to 1.9
- layout_shifts: float32 [2, 4, 192], P('section', None, 'dp'), may hold values from -3 to 3
- layout_up_weight: float32 [2, 192, 768], P('section', 'dp', 'tensor'), may hold values from -0.4375 to 0.4375
- layout_up_bias: float32 [2, 768], P('section', ('tensor', 'dp')), may hold values from -3 to 3
- layout_down_weight: float32 [2, 768, 192], P('section', 'tensor', 'dp'), may hold values from -0.21875 to 0.21875
Outputs:
- text_result: bfloat16 [2, 8, 512, 768], P('section', 'dp')
- layout_result: bfloat16 [2, 8, 512, 192], P('section', 'dp')
- text_input_grad: bfloat16 [2, 8, 512, 768], P('section', 'dp')
- layout_input_grad: bfloat16 [2, 8, 512, 192], P('section', 'dp')
- grad_text_input_weight: float32 [2, 3, 768, 768], P('section', None, 'dp', 'tensor')
- grad_text_head_bias: float32 [2, 2, 768], P('section', None, ('tensor', 'dp'))
- grad_text_output_weight: float32 [2, 768, 768], P('section', 'tensor', 'dp')
- grad_text_gains: float32 [2, 2, 768], P('section', None, 'dp')
- grad_text_shifts: float32 [2, 4, 768], P('section', None, 'dp')
- grad_text_up_weight: float32 [2, 768, 3072], P('section', 'dp', 'tensor')
- grad_text_up_bias: float32 [2, 3072], P('section', ('tensor', 'dp'))
- grad_text_down_weight: float32 [2, 3072, 768], P('section', 'tensor', 'dp')
- grad_layout_input_weight: float32 [2, 3, 192, 192], P('section', None, 'dp', 'tensor')
- grad_layout_head_bias: float32 [2, 2, 192], P('section', None, ('tensor', 'dp'))
- grad_layout_output_weight: float32 [2, 192, 192], P('section', 'tensor', 'dp')
- grad_layout_gains: float32 [2, 2, 192], P('section', None, 'dp')
- grad_layout_shifts: float32 [2, 4, 192], P('section', None, 'dp')
- grad_layout_up_weight: float32 [2, 192, 768], P('section', 'dp', 'tensor')
- grad_layout_up_bias: float32 [2, 768], P('section', ('tensor', 'dp'))
- grad_layout_down_weight: float32 [2, 768, 192], P('section', 'tensor', 'dp')
The draws below stay inside these ranges and needn't reach their ends.
All inputs are finite; a program needn't handle non-finite values. No bound on the sum of `token_mask` on one device may be relied on, other than what follows from the above.
Results may differ from the reference program's by a relative error of at most 0.04.
Values may be sent and summed in bfloat16 or wider, within the bound.
No kernel may reach another device: no remote copies, remote signals or barrier semaphores. Data moves between devices by JAX's collectives and lax.ppermute only.
A program may use at most 192 MiB of HBM per device.

```python
import jax
import jax.numpy as jnp
from jax import lax

D = 768
HEADS = 12
HEAD = 64
FF = 3072
LD = 192
LHEAD = 16
LFF = 768
SEQ = 512
PAGES = 8
LAYERS = 2


def plant(values, stream_key, low, largest):
    shape = values.shape
    place = [jax.random.randint(jax.random.fold_in(stream_key, axis), (), 0, shape[axis]) for axis in range(len(shape))]
    values = values.at[tuple(place)].set(low)
    longest = shape.index(max(shape))
    place[longest] = (place[longest] + 1) % shape[longest]
    return values.at[tuple(place)].set(largest)


def level_of(own_key, dims, shards, least, top_value):
    loudness = 1.0
    for position, blocks in shards:
        heights = jax.random.uniform(jax.random.fold_in(jax.random.fold_in(own_key, 6), position), (blocks,), jnp.float32, least / len(shards), top_value / len(shards))
        loudness = loudness * jnp.repeat(jnp.exp(heights), dims[position] // blocks).reshape((-1,) + (1,) * (len(dims) - 1 - position))
    return loudness


def normal_values(rng, extent, width, most, shards=(), dtype=jnp.bfloat16):
    entries = jax.random.normal(rng, extent, jnp.float32) * width
    if len(shards) > 0:
        entries = level_of(rng, extent, shards, -0.22, 0.18) * entries
    return jnp.clip(entries, min=-most, max=most).astype(dtype)


def setup_inputs(seed: int = 0) -> dict:
    seeds = jax.random.split(jax.random.key(seed), 22)
    text_in = normal_values(seeds[0], (PAGES, SEQ, D), 1.0, 6.0, ((0, 4),))
    layout_in = normal_values(seeds[1], (PAGES, SEQ, LD), 1.0, 6.0, ((0, 4),))
    token_mask = plant((jax.random.randint(seeds[2], (PAGES, SEQ), 0, 8) < 7).astype(jnp.int32), jax.random.fold_in(seeds[2], 1), 0, 1)
    text_cotangent = normal_values(seeds[3], (PAGES, SEQ, D), 1.0, 6.0, ((0, 4),))
    layout_cotangent = normal_values(seeds[4], (PAGES, SEQ, LD), 1.0, 6.0, ((0, 4),))
    text_input_weight = normal_values(seeds[5], (LAYERS, 3, D, D), D ** -0.5, 0.21875, ((0, 2), (2, 4), (3, 4)), jnp.float32)
    text_head_bias = normal_values(seeds[6], (LAYERS, 2, D), 0.5, 3.0, ((0, 2), (2, 16)), jnp.float32)
    text_output_weight = normal_values(seeds[7], (LAYERS, D, D), (D // 4) ** -0.5, 0.4375, ((0, 2), (1, 4), (2, 4)), jnp.float32)
    text_gains = jnp.clip(1.0 + 0.18 * jax.random.normal(seeds[8], (LAYERS, 2, D), jnp.float32), 0.1, 1.9)
    text_shifts = normal_values(seeds[9], (LAYERS, 4, D), 0.5, 3.0, ((0, 2), (2, 4)), jnp.float32)
    text_up_weight = normal_values(seeds[10], (LAYERS, D, FF), D ** -0.5, 0.21875, ((0, 2), (1, 4), (2, 4)), jnp.float32)
    text_up_bias = normal_values(seeds[11], (LAYERS, FF), 0.5, 3.0, ((0, 2), (1, 16)), jnp.float32)
    text_down_weight = normal_values(seeds[12], (LAYERS, FF, D), FF ** -0.5, 0.109375, ((0, 2), (1, 4), (2, 4)), jnp.float32)
    layout_input_weight = normal_values(seeds[13], (LAYERS, 3, LD, LD), LD ** -0.5, 0.4375, ((0, 2), (2, 4), (3, 4)), jnp.float32)
    layout_head_bias = normal_values(seeds[14], (LAYERS, 2, LD), 0.5, 3.0, ((0, 2), (2, 16)), jnp.float32)
    layout_output_weight = normal_values(seeds[15], (LAYERS, LD, LD), (LD // 4) ** -0.5, 0.875, ((0, 2), (1, 4), (2, 4)), jnp.float32)
    layout_gains = jnp.clip(1.0 + 0.18 * jax.random.normal(seeds[16], (LAYERS, 2, LD), jnp.float32), 0.1, 1.9)
    layout_shifts = normal_values(seeds[17], (LAYERS, 4, LD), 0.5, 3.0, ((0, 2), (2, 4)), jnp.float32)
    layout_up_weight = normal_values(seeds[18], (LAYERS, LD, LFF), LD ** -0.5, 0.4375, ((0, 2), (1, 4), (2, 4)), jnp.float32)
    layout_up_bias = normal_values(seeds[19], (LAYERS, LFF), 0.5, 3.0, ((0, 2), (1, 16)), jnp.float32)
    layout_down_weight = normal_values(seeds[20], (LAYERS, LFF, LD), LFF ** -0.5, 0.21875, ((0, 2), (1, 4), (2, 4)), jnp.float32)
    return dict(text_in=text_in, layout_in=layout_in, token_mask=token_mask, text_cotangent=text_cotangent, layout_cotangent=layout_cotangent, text_input_weight=text_input_weight, text_head_bias=text_head_bias, text_output_weight=text_output_weight, text_gains=text_gains, text_shifts=text_shifts, text_up_weight=text_up_weight, text_up_bias=text_up_bias, text_down_weight=text_down_weight, layout_input_weight=layout_input_weight, layout_head_bias=layout_head_bias, layout_output_weight=layout_output_weight, layout_gains=layout_gains, layout_shifts=layout_shifts, layout_up_weight=layout_up_weight, layout_up_bias=layout_up_bias, layout_down_weight=layout_down_weight)


@jax.custom_vjp
def low(v):
    return lax.optimization_barrier(v.astype(jnp.bfloat16)).astype(jnp.float32)

@jax.custom_vjp
def low_back(v):
    return v

def low_keep(v):
    return (low(v), None)

def low_pass(kept, grad):
    return (grad,)

def back_keep(v):
    return (v, None)

def back_low(kept, grad):
    return (low(grad),)
low.defvjp(low_keep, low_pass)
low_back.defvjp(back_keep, back_low)

def rounded_both(value):
    return low_back(low(value))

def matmul(left, right):
    return jnp.dot(left, right, precision=lax.Precision.HIGHEST, preferred_element_type=jnp.float32)

def einsum_high(form, left, right):
    return jnp.einsum(form, left, right, precision=lax.Precision.HIGHEST, preferred_element_type=jnp.float32)

def normalize(resid, gain, shift):
    center = resid - lax.optimization_barrier(jnp.mean(resid, axis=-1, keepdims=True))
    spread = lax.optimization_barrier(jnp.mean(center * center, axis=-1, keepdims=True))
    return center * lax.rsqrt(spread + 1e-05) * gain + shift

def project(tokens, weights, heads):
    rows = tokens.reshape(-1, tokens.shape[-1])
    query = rounded_both(matmul(rows, weights[0][0]) + weights[1][0])
    key_part = rounded_both(matmul(rows, weights[0][1]))
    value = rounded_both(matmul(rows, weights[0][2]) + weights[1][1])
    split = (tokens.shape[0], tokens.shape[1], heads, -1)
    return (query.reshape(split), key_part.reshape(split), value.reshape(split))

def text_term(text, params):
    lowered = (low(params[0]), low(params[1]))
    text_query, text_key, unused_value = project(text, lowered, HEADS)
    return einsum_high('pshe,pthe->phst', text_query, text_key) * HEAD ** (-0.5)

def finish(tokens, context, weights):
    rows = tokens.reshape(-1, tokens.shape[-1])
    flat = context.reshape(rows.shape[0], -1)
    gains = weights[3]
    shifts = weights[4]
    attended = low_back(matmul(flat, weights[2]) + shifts[0])
    hidden = low(normalize(rows + attended, gains[0], shifts[1]))
    inner = low_back(matmul(hidden, weights[5]) + weights[6])
    active = low(jax.nn.gelu(inner, approximate=False))
    branch = low_back(matmul(active, weights[7]) + shifts[2])
    result = rounded_both(normalize(hidden + branch, gains[1], shifts[3]))
    return result.reshape(tokens.shape)

def layer(text, layout, mask, params, fixed_text):
    params = tuple((low(w) for w in params))
    text_weights = params[:8]
    layout_weights = params[8:]
    text_query, text_key, text_value = project(text, text_weights, HEADS)
    layout_query, layout_key, layout_value = project(layout, layout_weights, HEADS)
    text_part = einsum_high('pshe,pthe->phst', text_query, text_key) * HEAD ** (-0.5)
    layout_part = einsum_high('pshe,pthe->phst', layout_query, layout_key) * LHEAD ** (-0.5)
    present = mask[:, None, None, :] > 0
    text_scores = low_back(jnp.where(present, text_part + layout_part, -1000000000.0))
    layout_scores = low_back(jnp.where(present, layout_part + fixed_text, -1000000000.0))
    text_prob = low(jax.nn.softmax(text_scores, axis=-1))
    layout_prob = low(jax.nn.softmax(layout_scores, axis=-1))
    text_context = rounded_both(einsum_high('phst,pthe->pshe', text_prob, text_value))
    layout_context = rounded_both(einsum_high('phst,pthe->pshe', layout_prob, layout_value))
    return (finish(text, text_context, text_weights), finish(layout, layout_context, layout_weights))

def reference(text_in, layout_in, token_mask, text_cotangent, layout_cotangent, text_input_weight, text_head_bias, text_output_weight, text_gains, text_shifts, text_up_weight, text_up_bias, text_down_weight, layout_input_weight, layout_head_bias, layout_output_weight, layout_gains, layout_shifts, layout_up_weight, layout_up_bias, layout_down_weight):
    weights = (text_input_weight, text_head_bias, text_output_weight, text_gains, text_shifts, text_up_weight, text_up_bias, text_down_weight, layout_input_weight, layout_head_bias, layout_output_weight, layout_gains, layout_shifts, layout_up_weight, layout_up_bias, layout_down_weight)
    first = tuple((w[0].astype(jnp.float32) for w in weights))
    second = tuple((w[1].astype(jnp.float32) for w in weights))
    group = 4
    count = text_in.shape[0] // group

    def split(value):
        return value.reshape((count, group) + value.shape[1:])
    inputs = (split(text_in.astype(jnp.float32)), split(layout_in.astype(jnp.float32)), split(token_mask), split(text_cotangent.astype(jnp.float32)), split(layout_cotangent.astype(jnp.float32)))

    def step(totals, batch):
        text, layout, mask, text_grad, layout_grad = batch
        fixed_one = text_term(text, first)

        def single_one(left, right, params):
            return layer(left, right, mask, params, fixed_one)
        middle, back_one = jax.vjp(single_one, text, layout, first)
        fixed_two = text_term(middle[0], second)

        def single_two(left, right, params):
            return layer(left, right, mask, params, fixed_two)
        ending, back_two = jax.vjp(single_two, middle[0], middle[1], second)
        grad_mid_text, grad_mid_layout, grad_second = back_two((text_grad, layout_grad))
        grad_in_text, grad_in_layout, grad_first = back_one((grad_mid_text, grad_mid_layout))
        totals = (tuple((a + b for a, b in zip(totals[0], grad_first))), tuple((a + b for a, b in zip(totals[1], grad_second))))
        return (totals, (middle[0], ending[0], middle[1], ending[1], grad_in_text, grad_mid_text, grad_in_layout, grad_mid_layout))
    zeros = (tuple((jnp.zeros_like(w) for w in first)), tuple((jnp.zeros_like(w) for w in second)))
    totals, stacked = lax.scan(step, zeros, inputs)

    def merge(one, two):
        whole_one = one.reshape((count * group,) + one.shape[2:])
        whole_two = two.reshape((count * group,) + two.shape[2:])
        return jnp.stack([whole_one, whole_two]).astype(jnp.bfloat16)
    text_result = merge(stacked[0], stacked[1])
    layout_result = merge(stacked[2], stacked[3])
    text_grad_out = merge(stacked[4], stacked[5])
    layout_grad_out = merge(stacked[6], stacked[7])
    grads = tuple((jnp.stack([a, b]) for a, b in zip(totals[0], totals[1])))
    return (text_result, layout_result, text_grad_out, layout_grad_out, grads[0], grads[1], grads[2], grads[3], grads[4], grads[5], grads[6], grads[7], grads[8], grads[9], grads[10], grads[11], grads[12], grads[13], grads[14], grads[15])
```

```python
import functools

import jax
import jax.numpy as jnp
from jax import lax
from jax.experimental import pallas as pl
from jax.experimental.pallas import tpu as pltpu
from jax.sharding import Mesh, PartitionSpec as P

BF = jnp.bfloat16
F32 = jnp.float32
HEAD = 64
LHEAD = 16
SLOT = 128
GROUPS = 3
ALL = ("y", "x", "c", "h", "l")


def mm(a, b):
    return lax.dot_general(a, b, (((1,), (0,)), ((), ())), preferred_element_type=F32)


def mm_nt(a, b):
    return lax.dot_general(a, b, (((1,), (1,)), ((), ())), preferred_element_type=F32)


def mm_tn(a, b):
    return lax.dot_general(a, b, (((0,), (0,)), ((), ())), preferred_element_type=F32)


class Sizes:
    def __init__(self, text, layout, rd, ld, cols, lcols, dp):
        self.seq = text.shape[1]
        self.rows = self.seq // 2
        self.d = text.shape[2]
        self.ld = layout.shape[2]
        self.width = self.d + self.ld
        self.rd = rd
        self.lr = ld
        self.dp = dp
        self.quarter = cols
        self.lquarter = lcols
        self.heads = cols // HEAD
        self.block = rd + ld // GROUPS
        self.vblock = self.block + 16


def call(body, out_shapes, *args, scratch=(), flops=0):
    nbytes = sum(a.size * a.dtype.itemsize for a in args)
    nbytes += sum(s.size * s.dtype.itemsize for s in out_shapes)
    return pl.pallas_call(
        body,
        out_shape=list(out_shapes),
        in_specs=[pl.BlockSpec(memory_space=pltpu.VMEM)] * len(args),
        out_specs=[pl.BlockSpec(memory_space=pltpu.VMEM)] * len(out_shapes),
        scratch_shapes=list(scratch),
        compiler_params=pltpu.CompilerParams(vmem_limit_bytes=56 * 2**20),
        cost_estimate=pl.CostEstimate(flops=flops, bytes_accessed=nbytes, transcendentals=0),
    )(*args)


def sds(shape, dtype):
    return jax.ShapeDtypeStruct(shape, dtype)


def text_w(g_ref, h, z):
    return g_ref[h, :, : z.rd, :].reshape(z.dp * z.rd, g_ref.shape[-1])


def layout_w(g_ref, h, z):
    part = z.lr // GROUPS
    width = g_ref.shape[-1] // GROUPS
    pieces = []
    for d in range(z.dp):
        for k in range(GROUPS):
            pieces.append(g_ref[h, d, z.rd : z.rd + part, width * k : width * (k + 1)])
    return jnp.concatenate(pieces, axis=0)


def put_grads(g_ref, h, text, layout, z):
    part = z.lr // GROUPS
    width = g_ref.shape[-1] // GROUPS
    g_ref[h, :, : z.rd, :] = text.reshape(z.dp, z.rd, text.shape[-1]).astype(BF)
    pad = width - layout.shape[-1]
    low = layout.astype(BF)
    if pad:
        low = jnp.concatenate([low, jnp.zeros((low.shape[0], pad), BF)], axis=1)
    for d in range(z.dp):
        for k in range(GROUPS):
            base = z.lr * d + part * k
            g_ref[h, d, z.rd : z.rd + part, width * k : width * (k + 1)] = low[base : base + part]


def norm_stats(resid):
    center = resid - jnp.mean(resid, axis=-1, keepdims=True)
    factor = lax.rsqrt(jnp.mean(center * center, axis=-1, keepdims=True) + 1e-05)
    return center * factor, factor


def norm_both(resid, z):
    nt, ft = norm_stats(resid[:, : z.d])
    nl, fl = norm_stats(resid[:, z.d :])
    return jnp.concatenate([nt, nl], axis=1), ft, fl


def norm_back(grad, normed, factor, gain):
    scaled = grad * gain
    return factor * (
        scaled
        - jnp.mean(scaled, axis=-1, keepdims=True)
        - normed * jnp.mean(scaled * normed, axis=-1, keepdims=True)
    )


def norm_back_both(grad, normed, ft, fl, gain, z):
    gt = norm_back(grad[:, : z.d], normed[:, : z.d], ft, gain[:, : z.d])
    gl = norm_back(grad[:, z.d :], normed[:, z.d :], fl, gain[:, z.d :])
    return jnp.concatenate([gt, gl], axis=1)


def qkv_body(z, fused, *refs):
    if fused:
        hid_ref, own_ref, rec_ref, vec_ref, w_ref, bt_ref, bl_ref, r_ref, x_ref, q_ref, kv_ref = refs
        vec = vec_ref[...]
        resid = (
            hid_ref[...].astype(F32) + own_ref[...].astype(F32) + rec_ref[...].astype(F32) + vec[4:5]
        )
        r_ref[...] = resid
        normed, _, _ = norm_both(resid, z)
        x = (normed * vec[1:2] + vec[5:6]).astype(BF)
        x_ref[...] = x
    else:
        x_ref, w_ref, bt_ref, bl_ref, q_ref, kv_ref = refs
        x = x_ref[...]
    xt, xl = x[:, : z.d], x[:, z.d :]
    n, m = z.quarter, z.lquarter
    zeros = jnp.zeros((z.rows, SLOT - HEAD - LHEAD), BF)
    for h in range(2):
        yt = mm(xt, text_w(w_ref, h, z)[:, : 3 * n]) + bt_ref[h]
        yl = mm(xl, layout_w(w_ref, h, z)[:, : 3 * m]) + bl_ref[h]
        yt = yt.astype(BF)
        yl = yl.astype(BF)
        for s in range(3):
            for j in range(z.heads):
                a = yt[:, n * s + HEAD * j : n * s + HEAD * (j + 1)]
                b = yl[:, m * s + LHEAD * j : m * s + LHEAD * (j + 1)]
                if s == 0:
                    a = a * BF(HEAD**-0.5)
                    b = b * BF(LHEAD**-0.5)
                slot = jnp.concatenate([a, b, zeros], axis=1)
                head = z.heads * h + j
                if s == 0:
                    q_ref[head] = slot
                else:
                    kv_ref[2 * z.heads * (s - 1) + head] = slot


def attend_body(z, q_ref, own_ref, rec_ref, mask_ref, w_ref, a_ref, c_ref, p_ref, s_ref):
    count = 2 * z.heads
    m0 = mask_ref[0:1, : z.rows] > 0
    m1 = mask_ref[0:1, z.rows :] > 0

    def head(j, carry):
        q = q_ref[j]
        s0 = jnp.where(m0, mm_nt(q, own_ref[j]), -1000000000.0)
        s1 = jnp.where(m1, mm_nt(q, rec_ref[j]), -1000000000.0)
        top = jnp.maximum(
            jnp.max(s0, axis=-1, keepdims=True), jnp.max(s1, axis=-1, keepdims=True)
        )
        e0 = jnp.exp(s0 - top)
        e1 = jnp.exp(s1 - top)
        inv = 1.0 / (jnp.sum(e0, axis=-1, keepdims=True) + jnp.sum(e1, axis=-1, keepdims=True))
        p0 = (e0 * inv).astype(BF)
        p1 = (e1 * inv).astype(BF)
        p_ref[j, :, : z.rows] = p0
        p_ref[j, :, z.rows :] = p1
        s_ref[j] = (mm(p0, own_ref[count + j]) + mm(p1, rec_ref[count + j])).astype(BF)
        return carry

    lax.fori_loop(0, count, head, 0)
    n, m = z.quarter, z.lquarter
    at = al = None
    for h in range(2):
        heads = [s_ref[z.heads * h + j] for j in range(z.heads)]
        ct = jnp.concatenate([s[:, :HEAD] for s in heads], axis=1)
        cl = jnp.concatenate([s[:, HEAD : HEAD + LHEAD] for s in heads], axis=1)
        c_ref[h, :, :n] = ct
        c_ref[h, :, 2 * SLOT : 2 * SLOT + m] = cl
        pt = mm_nt(ct, text_w(w_ref, h, z)[:, 3 * n : 4 * n])
        pll = mm_nt(cl, layout_w(w_ref, h, z)[:, 3 * m : 4 * m])
        at = pt if at is None else at + pt
        al = pll if al is None else al + pll
    a_ref[:, : z.d] = at.astype(BF)
    a_ref[:, z.d :] = al.astype(BF)


def gelu_parts(u):
    cdf = 0.5 * (1.0 + lax.erf(u * 0.7071067811865476))
    slope = cdf + u * jnp.exp(-0.5 * u * u) * 0.3989422804014327
    return (u * cdf).astype(BF), slope.astype(BF)


def forward_body(
    z, x_ref, own_ref, rec_ref, vec_ref, up_ref, down_ref, bt_ref, bl_ref,
    r_ref, hid_ref, gt_ref, gl_ref, st_ref, sl_ref, f_ref,
):
    vec = vec_ref[...]
    resid = x_ref[...].astype(F32) + own_ref[...].astype(F32) + rec_ref[...].astype(F32) + vec[2:3]
    r_ref[...] = resid
    normed, _, _ = norm_both(resid, z)
    hid = (normed * vec[0:1] + vec[3:4]).astype(BF)
    hid_ref[...] = hid
    ht, hl = hid[:, : z.d], hid[:, z.d :]
    ft = fl = None
    for h in range(2):
        g, s = gelu_parts(mm(ht, text_w(up_ref, h, z)) + bt_ref[h])
        gt_ref[h] = g
        st_ref[h] = s
        p = mm_nt(g, text_w(down_ref, h, z))
        ft = p if ft is None else ft + p
        lw = 4 * z.lquarter
        g, s = gelu_parts(mm(hl, layout_w(up_ref, h, z)[:, :lw]) + bl_ref[h])
        gl_ref[h] = g
        sl_ref[h] = s
        p = mm_nt(g, layout_w(down_ref, h, z)[:, :lw])
        fl = p if fl is None else fl + p
    f_ref[:, : z.d] = ft.astype(BF)
    f_ref[:, z.d :] = fl.astype(BF)


def col_sum(value):
    return jnp.sum(value, axis=0, keepdims=True)


def tail_body(z, fused, *refs):
    if fused == "last":
        (hid_ref, own_ref, rec_ref, go_ref, vec_ref, up_ref, down_ref, st_ref, sl_ref,
         out_ref, d2_ref, df_ref, dut_ref, dul_ref, dh_ref, vg_ref, gbt_ref, gbl_ref) = refs
        vec = vec_ref[...]
        resid = (
            hid_ref[...].astype(F32) + own_ref[...].astype(F32) + rec_ref[...].astype(F32) + vec[4:5]
        )
        normed, ft, fl = norm_both(resid, z)
        out_ref[...] = (normed * vec[1:2] + vec[5:6]).astype(BF)
        go = go_ref[...].astype(F32)
    else:
        (r_ref, d1_ref, own_ref, rec_ref, vec_ref, up_ref, down_ref, st_ref, sl_ref,
         dx_ref, d2_ref, df_ref, dut_ref, dul_ref, dh_ref, vg_ref, gbt_ref, gbl_ref) = refs
        vec = vec_ref[...]
        normed, ft, fl = norm_both(r_ref[...], z)
        low = (d1_ref[...] + own_ref[...].astype(F32) + rec_ref[...].astype(F32)).astype(BF)
        dx_ref[...] = low
        go = low.astype(F32)
    d2 = norm_back_both(go, normed, ft, fl, vec[1:2], z)
    d2_ref[...] = d2
    df = d2.astype(BF)
    df_ref[...] = df
    vg_ref[0:1] = col_sum(go * normed)
    vg_ref[1:2] = col_sum(go)
    vg_ref[2:3] = col_sum(df.astype(F32))
    vg_ref[3:8] = jnp.zeros((5, z.width), F32)
    dft, dfl = df[:, : z.d], df[:, z.d :]
    ht = hl = None
    for h in range(2):
        du = (mm(dft, text_w(down_ref, h, z)) * st_ref[h].astype(F32)).astype(BF)
        dut_ref[h] = du
        gbt_ref[h] = col_sum(du.astype(F32))
        p = mm_nt(du, text_w(up_ref, h, z))
        ht = p if ht is None else ht + p
        lw = 4 * z.lquarter
        du = (mm(dfl, layout_w(down_ref, h, z)[:, :lw]) * sl_ref[h].astype(F32)).astype(BF)
        dul_ref[h] = du
        gbl_ref[h] = col_sum(du.astype(F32))
        p = mm_nt(du, layout_w(up_ref, h, z)[:, :lw])
        hl = p if hl is None else hl + p
    dh_ref[:, : z.d] = ht.astype(BF)
    dh_ref[:, z.d :] = hl.astype(BF)


def ffn_grads_body(z, hid_ref, df_ref, gt_ref, gl_ref, dut_ref, dul_ref, g1_ref, g2_ref):
    hid, df = hid_ref[...], df_ref[...]
    for h in range(2):
        put_grads(g1_ref, h, mm_tn(hid[:, : z.d], dut_ref[h]), mm_tn(hid[:, z.d :], dul_ref[h]), z)
        put_grads(g2_ref, h, mm_tn(df[:, : z.d], gt_ref[h]), mm_tn(df[:, z.d :], gl_ref[h]), z)


def attend_back_body(
    z, d2_ref, own_ref, rec_ref, r_ref, vec_ref, w_ref, c_ref, q_ref, kv_ref, kvr_ref, p_ref, mask_ref,
    d1_ref, da_ref, dq_ref, dkv_ref, dkvr_ref, vg_ref, dc_ref, dd_ref,
):
    count = 2 * z.heads
    vec = vec_ref[...]
    dh = d2_ref[...] + own_ref[...].astype(F32) + rec_ref[...].astype(F32)
    normed, ft, fl = norm_both(r_ref[...], z)
    d1 = norm_back_both(dh, normed, ft, fl, vec[0:1], z)
    d1_ref[...] = d1
    da = d1.astype(BF)
    da_ref[...] = da
    vg_ref[0:1] = col_sum(dh * normed)
    vg_ref[1:2] = col_sum(dh)
    vg_ref[2:3] = col_sum(da.astype(F32))
    vg_ref[3:8] = jnp.zeros((5, z.width), F32)
    n, m = z.quarter, z.lquarter
    zeros = jnp.zeros((z.rows, SLOT - HEAD - LHEAD), BF)
    for h in range(2):
        dct = mm(da[:, : z.d], text_w(w_ref, h, z)[:, 3 * n : 4 * n]).astype(BF)
        dcl = mm(da[:, z.d :], layout_w(w_ref, h, z)[:, 3 * m : 4 * m]).astype(BF)
        for j in range(z.heads):
            a = dct[:, HEAD * j : HEAD * (j + 1)]
            b = dcl[:, LHEAD * j : LHEAD * (j + 1)]
            dc_ref[z.heads * h + j] = jnp.concatenate([a, b, zeros], axis=1)
            ct = c_ref[h, :, HEAD * j : HEAD * (j + 1)].astype(F32)
            cl = c_ref[h, :, 2 * SLOT + LHEAD * j : 2 * SLOT + LHEAD * (j + 1)].astype(F32)
            dt = jnp.sum(a.astype(F32) * ct, axis=-1, keepdims=True)
            dl = jnp.sum(b.astype(F32) * cl, axis=-1, keepdims=True)
            dd_ref[z.heads * h + j, :, 0:1] = dt
            dd_ref[z.heads * h + j, :, 1:2] = dt + dl
    lane = lax.broadcasted_iota(jnp.int32, (z.rows, SLOT), 1)
    text_lane = lane < HEAD
    scale = jnp.where(text_lane, HEAD**-0.5, LHEAD**-0.5)
    mask = mask_ref[...]
    masks = (mask[:, : z.rows], mask[:, z.rows :])

    def head(j, carry):
        dc = dc_ref[j]
        dct = jnp.where(text_lane, dc, jnp.zeros_like(dc))
        q = q_ref[j]
        dt = dd_ref[j, :, 0:1]
        ds = dd_ref[j, :, 1:2]
        dq_t = dq_s = None
        for i, (k_ref, o_ref) in enumerate(((kv_ref, dkv_ref), (kvr_ref, dkvr_ref))):
            k = k_ref[j]
            v = k_ref[count + j]
            prob = p_ref[j, :, z.rows * i : z.rows * (i + 1)]
            pm = jnp.where(masks[i] > 0, prob.astype(F32), 0.0)
            st = (pm * (mm_nt(dct, v) - dt)).astype(BF)
            ss = (pm * (mm_nt(dc, v) - ds)).astype(BF)
            a = mm(st, k)
            b = mm(ss, k)
            dq_t = a if dq_t is None else dq_t + a
            dq_s = b if dq_s is None else dq_s + b
            dk = jnp.where(text_lane, mm_tn(st, q), mm_tn(ss, q))
            o_ref[j] = dk.astype(BF)
            o_ref[count + j] = mm_tn(prob, dc).astype(BF)
        dq_ref[j] = (jnp.where(text_lane, dq_t, dq_s) * scale).astype(BF)
        return carry

    lax.fori_loop(0, count, head, 0)


def input_back_body(z, dq_ref, dkv_ref, rec_ref, w_ref, yt_ref, yl_ref, dx_ref, gbt_ref, gbl_ref):
    count = 2 * z.heads
    n, m = z.quarter, z.lquarter
    xt = xl = None
    for h in range(2):
        ts, ls = [], []
        for s in range(3):
            for j in range(z.heads):
                head = z.heads * h + j
                if s == 0:
                    slot = dq_ref[head]
                else:
                    at = count * (s - 1) + head
                    slot = (dkv_ref[at].astype(F32) + rec_ref[at].astype(F32)).astype(BF)
                ts.append(slot[:, :HEAD])
                ls.append(slot[:, HEAD : HEAD + LHEAD])
        yt = jnp.concatenate(ts, axis=1)
        yl = jnp.concatenate(ls, axis=1)
        yt_ref[h] = yt
        yl_ref[h] = yl
        gbt_ref[h] = col_sum(yt.astype(F32))
        gbl_ref[h] = col_sum(yl.astype(F32))
        p = mm_nt(yt, text_w(w_ref, h, z)[:, : 3 * n])
        xt = p if xt is None else xt + p
        p = mm_nt(yl, layout_w(w_ref, h, z)[:, : 3 * m])
        xl = p if xl is None else xl + p
    dx_ref[:, : z.d] = xt.astype(BF)
    dx_ref[:, z.d :] = xl.astype(BF)


def input_grads_body(
    z, x_ref, da_ref, c_ref, yt_ref, yl_ref, va_ref, vb_ref, bt_ref, bl_ref, ut_ref, ul_ref, g_ref
):
    x, da = x_ref[...], da_ref[...]
    n, m = z.quarter, z.lquarter
    va, vb = va_ref[...], vb_ref[...]
    rows = (vb[0:1], va[0:1], vb[2:3], vb[1:2], va[2:3], va[1:2])
    for h in range(2):
        ct = c_ref[h, :, :n]
        cl = c_ref[h, :, 2 * SLOT : 2 * SLOT + m]
        text = jnp.concatenate(
            [mm_tn(x[:, : z.d], yt_ref[h]), mm_tn(da[:, : z.d], ct)], axis=1
        )
        layout = jnp.concatenate(
            [mm_tn(x[:, z.d :], yl_ref[h]), mm_tn(da[:, z.d :], cl)], axis=1
        )
        put_grads(g_ref, h, text, layout, z)
        bt, bl, ut, ul = bt_ref[h], bl_ref[h], ut_ref[h], ul_ref[h]
        hb, hl = n // z.dp, m // z.dp
        ub, ulb = 4 * n // z.dp, 4 * m // z.dp
        for d in range(z.dp):
            g_ref[h, d, z.block : z.vblock, :] = jnp.zeros((16, g_ref.shape[-1]), BF)
            for i, row in enumerate(rows):
                at = z.block + i
                g_ref[h, d, at : at + 1, : z.rd] = row[:, z.rd * d : z.rd * (d + 1)].astype(BF)
                g_ref[h, d, at : at + 1, 2 * SLOT : 2 * SLOT + z.lr] = row[
                    :, z.d + z.lr * d : z.d + z.lr * (d + 1)
                ].astype(BF)
            for i, s in enumerate((0, 2)):
                at = z.block + 6 + i
                g_ref[h, d, at : at + 1, :hb] = bt[:, n * s + hb * d : n * s + hb * (d + 1)].astype(BF)
                g_ref[h, d, at : at + 1, 2 * SLOT : 2 * SLOT + hl] = bl[
                    :, m * s + hl * d : m * s + hl * (d + 1)
                ].astype(BF)
            at = z.block + 8
            g_ref[h, d, at : at + 1, :ub] = ut[:, ub * d : ub * (d + 1)].astype(BF)
            g_ref[h, d, at : at + 1, 2 * SLOT : 2 * SLOT + ulb] = ul[
                :, ulb * d : ulb * (d + 1)
            ].astype(BF)


def swap(value, axis):
    return lax.ppermute(value, axis, [(0, 1), (1, 0)])


def gather_blocks(own, x_size):
    if x_size == 2:
        x = lax.axis_index("x")
        other = swap(own, "x")
        both = jnp.where(
            x == 0, jnp.stack([own, other], axis=1), jnp.stack([other, own], axis=1)
        )
    else:
        both = lax.all_gather(own, "x", axis=1)
    c = lax.axis_index("c")
    other = swap(both, "c")
    out = jnp.where(
        c == 0, jnp.stack([both, other], axis=2), jnp.stack([other, both], axis=2)
    )
    return out.reshape((2, 2 * x_size) + own.shape[1:])


def pick(value, index, axis):
    return lax.dynamic_index_in_dim(value, index, axis, keepdims=False)


def add_low(a, b):
    return (a.astype(F32) + b.astype(F32)).astype(BF)


def scatter_blocks(grads, x_size):
    c = lax.axis_index("c")
    parts = grads.reshape((2, x_size, 2) + grads.shape[2:])
    got = swap(pick(parts, 1 - c, 2), "c")
    parts = add_low(pick(parts, c, 2), got)
    if x_size == 2:
        x = lax.axis_index("x")
        got = swap(pick(parts, 1 - x, 1), "x")
        parts = add_low(pick(parts, x, 1), got)
    else:
        parts = lax.psum_scatter(parts, "x", scatter_dimension=1, tiled=False)
    got = swap(parts[1], "h")
    return add_low(parts[0], got)


def pack_layout(value):
    lead, rows, cols = value.shape[:-2], value.shape[-2], value.shape[-1]
    value = jnp.pad(value, [(0, 0)] * (len(lead) + 1) + [(0, 256 - cols)])
    value = value.reshape(lead + (GROUPS, rows // GROUPS, 256))
    return jnp.moveaxis(value, -3, -2).reshape(lead + (rows // GROUPS, GROUPS * 256))


def unpack_layout(value, cols):
    lead, rows = value.shape[:-2], value.shape[-2]
    value = jnp.moveaxis(value.reshape(lead + (rows, GROUPS, 256)), -2, -3)
    return value.reshape(lead + (GROUPS * rows, 256))[..., :cols]


def per_device(
    text_in, layout_in, token_mask, text_cotangent, layout_cotangent,
    t_in, t_hb, t_out, t_gain, t_shift, t_up, t_ub, t_down,
    l_in, l_hb, l_out, l_gain, l_shift, l_up, l_ub, l_down,
):
    x_size = lax.axis_size("x")
    y, x, c, h = (lax.axis_index(a) for a in ("y", "x", "c", "h"))
    rd, ld = t_in.shape[2], l_in.shape[2]
    z = Sizes(text_in, layout_in, rd, ld, t_in.shape[3], l_in.shape[3], 2 * x_size)
    low = lambda v: v[0].astype(BF)

    text = [
        jnp.concatenate([low(t_in)[0], low(t_in)[1], low(t_in)[2], low(t_out).T], axis=1),
        low(t_up),
        low(t_down).T,
    ]
    layout = [
        jnp.concatenate([low(l_in)[0], low(l_in)[1], low(l_in)[2], low(l_out).T], axis=1),
        low(l_up),
        low(l_down).T,
    ]
    raw = [jnp.concatenate([a, pack_layout(b)], axis=0) for a, b in zip(text, layout)]

    layers = ([], [])
    for piece in raw:
        other = swap(piece, "y")
        first = jnp.where(y == 0, piece, other)
        second = jnp.where(y == 0, other, piece)
        for index, value in enumerate((first, second)):
            layers[index].append(value)
    weights = [
        [gather_blocks(jnp.stack([v, swap(v, "h")]), x_size) for v in pieces] for pieces in layers
    ]

    rows = jnp.zeros((16, 512), F32)
    small = (
        (t_gain[0], l_gain[0], 0), (t_shift[0], l_shift[0], 2),
        (t_hb[0], l_hb[0], 6), (t_ub, l_ub, 8),
    )
    for a, b, at in small:
        rows = rows.at[at : at + a.shape[0], : a.shape[1]].set(a)
        rows = rows.at[at : at + b.shape[0], 256 : 256 + b.shape[1]].set(b)
    every = lax.all_gather(rows.astype(BF), ("y", "h", "x", "c"), axis=0)
    every = every.reshape(2, 2, z.dp, 16, 512).astype(F32)
    every = jnp.where(h == 0, every, every[:, ::-1])

    def joined(value, at, width):
        value = value[:, :, at : at + width]
        return jnp.moveaxis(value, 0, 1).reshape(value.shape[1], -1)

    vecs, biases = [], []
    for index in range(2):
        part = every[index]
        vec = jnp.concatenate(
            [joined(part[0, :, 0:6], 0, rd), joined(part[0, :, 0:6], 256, ld)], axis=1
        )
        vecs.append(jnp.pad(vec, ((0, 2), (0, 0))))
        bt, bl, ut, ul = [], [], [], []
        for q in range(2):
            hb = joined(part[q, :, 6:8], 0, t_hb.shape[2])
            lb = joined(part[q, :, 6:8], 256, l_hb.shape[2])
            bt.append(jnp.concatenate([hb[0], jnp.zeros_like(hb[0]), hb[1]])[None])
            bl.append(jnp.concatenate([lb[0], jnp.zeros_like(lb[0]), lb[1]])[None])
            ut.append(joined(part[q, :, 8:9], 0, t_ub.shape[1]))
            ul.append(joined(part[q, :, 8:9], 256, l_ub.shape[1]))
        biases.append([jnp.stack(v) for v in (bt, bl, ut, ul)])

    both = jnp.concatenate([text_in, layout_in, text_cotangent, layout_cotangent], axis=2)
    page = pick(both, y, 0)
    half = lambda i: lax.dynamic_slice_in_dim(page, i * z.rows, z.rows, 0)
    moved = swap(half(1 - c), "c")
    mine = jnp.where(c == h, half(c), moved)
    x0, cot = mine[:, : z.width], mine[:, z.width :]
    mask = pick(token_mask, y, 0)[None].astype(F32)
    mask = jnp.where(c == h, mask, swap(mask, "c"))
    mask = jnp.where(c == 0, mask, jnp.concatenate([mask[:, z.rows :], mask[:, : z.rows]], axis=1))
    mask = jnp.broadcast_to(mask, (8, z.seq))[0:1]

    R, W, Q, M = z.rows, z.width, 4 * z.quarter, 4 * z.lquarter
    nh = 2 * z.heads
    q_shapes = [sds((nh, R, SLOT), BF), sds((2 * nh, R, SLOT), BF)]
    saved = []
    result = []
    inner = x0
    for index in range(2):
        w0, w1, w2 = weights[index]
        vec = vecs[index]
        bt, bl, ut, ul = biases[index]
        if index == 0:
            q, kv = call(functools.partial(qkv_body, z, False), q_shapes, x0, w0, bt, bl, flops=10**9)
            xin = x0
        else:
            hid, own, got = inner
            r2, xin, q, kv = call(
                functools.partial(qkv_body, z, True),
                [sds((R, W), F32), sds((R, W), BF)] + q_shapes,
                hid, own, got, vecs[0], w0, bt, bl, flops=10**9,
            )
            saved[0]["r2"] = r2
            result.append(xin)
        kvr = swap(kv, "c")
        a, ctx, prob = call(
            functools.partial(attend_body, z),
            [sds((R, W), BF), sds((2, R, 3 * SLOT), BF), sds((nh, R, z.seq), BF)],
            q, kv, kvr, mask, w0, scratch=[pltpu.VMEM((nh, R, SLOT), BF)], flops=10**9,
        )
        ar = swap(a, "l")
        r1, hid, gt, gl, st, sl, f = call(
            functools.partial(forward_body, z),
            [sds((R, W), F32), sds((R, W), BF), sds((2, R, Q), BF), sds((2, R, M), BF),
             sds((2, R, Q), BF), sds((2, R, M), BF), sds((R, W), BF)],
            xin, a, ar, vec, w1, w2, ut, ul, flops=2 * 10**9,
        )
        fr = swap(f, "l")
        inner = (hid, f, fr)
        saved.append(dict(x=xin, q=q, kv=kv, kvr=kvr, ctx=ctx, prob=prob, r1=r1, hid=hid, gt=gt,
                          gl=gl, st=st, sl=sl))

    reduced = [None, None]
    grads_x = [None, None]
    for index in (1, 0):
        w0, w1, w2 = weights[index]
        vec = vecs[index]
        keep = saved[index]
        tail_shapes = [sds((R, W), BF), sds((R, W), F32), sds((R, W), BF), sds((2, R, Q), BF),
                       sds((2, R, M), BF), sds((R, W), BF), sds((8, W), F32), sds((2, 1, Q), F32),
                       sds((2, 1, M), F32)]
        if index == 1:
            out, d2, df, dut, dul, dh, va, gut, gul = call(
                functools.partial(tail_body, z, "last"), tail_shapes,
                *inner, cot, vec, w1, w2, keep["st"], keep["sl"], flops=2 * 10**9,
            )
            result.append(out)
        else:
            dx, d2, df, dut, dul, dh, va, gut, gul = call(
                functools.partial(tail_body, z, "mid"), tail_shapes,
                keep["r2"], d1, dxp, dxr, vec, w1, w2, keep["st"], keep["sl"], flops=2 * 10**9,
            )
            grads_x[1] = dx
        dhr = swap(dh, "l")
        gshape = sds((2, z.dp, z.block, 768), BF)
        g1, g2 = call(
            functools.partial(ffn_grads_body, z), [gshape, gshape],
            keep["hid"], df, keep["gt"], keep["gl"], dut, dul, flops=2 * 10**9,
        )
        d1, da, dq, dkv, dkvr, vb = call(
            functools.partial(attend_back_body, z),
            [sds((R, W), F32), sds((R, W), BF), q_shapes[0], q_shapes[1], q_shapes[1], sds((8, W), F32)],
            d2, dh, dhr, keep["r1"], vec, w0, keep["ctx"], keep["q"], keep["kv"], keep["kvr"],
            keep["prob"], mask,
            scratch=[pltpu.VMEM((nh, R, SLOT), BF), pltpu.VMEM((nh, R, SLOT), F32)],
            flops=2 * 10**9,
        )
        back = swap(dkvr, "c")
        yt, yl, dxp, gbt, gbl = call(
            functools.partial(input_back_body, z),
            [sds((2, R, 3 * z.quarter), BF), sds((2, R, 3 * z.lquarter), BF), sds((R, W), BF),
             sds((2, 1, 3 * z.quarter), F32), sds((2, 1, 3 * z.lquarter), F32)],
            dq, dkv, back, w0, flops=10**9,
        )
        dxr = swap(dxp, "l")
        (g0,) = call(
            functools.partial(input_grads_body, z), [sds((2, z.dp, z.vblock, 768), BF)],
            keep["x"], da, keep["ctx"], yt, yl, va, vb, gbt, gbl, gut, gul, flops=10**9,
        )
        reduced[index] = [scatter_blocks(g, x_size) for g in (g0, g1, g2)]
    grads_x[0] = (d1 + dxp.astype(F32) + dxr.astype(F32)).astype(BF)

    final = []
    for p in range(3):
        here = jnp.where(y == 0, reduced[0][p], reduced[1][p])
        there = jnp.where(y == 0, reduced[1][p], reduced[0][p])
        final.append(here.astype(F32) + swap(there, "y").astype(F32))
    f0, f1, f2 = final
    n, m = z.quarter, z.lquarter
    lay = [unpack_layout(f[rd : z.block], 4 * m) for f in final]
    v = f0[z.block :]
    g_t_in = jnp.stack([f0[:rd, n * s : n * (s + 1)] for s in range(3)])[None]
    g_l_in = jnp.stack([lay[0][:, m * s : m * (s + 1)] for s in range(3)])[None]
    small_out = lambda at, count, width, lane: v[at : at + count, lane : lane + width]
    gt = (
        g_t_in,
        small_out(6, 2, t_hb.shape[2], 0)[None],
        f0[:rd, 3 * n :].T[None],
        small_out(0, 2, rd, 0)[None],
        small_out(2, 4, rd, 0)[None],
        f1[:rd][None],
        small_out(8, 1, t_ub.shape[1], 0),
        f2[:rd].T[None],
    )
    glay = (
        g_l_in,
        small_out(6, 2, l_hb.shape[2], 256)[None],
        lay[0][:, 3 * m :].T[None],
        small_out(0, 2, ld, 256)[None],
        small_out(2, 4, ld, 256)[None],
        lay[1][None],
        small_out(8, 1, l_ub.shape[1], 256),
        lay[2].T[None],
    )

    def spread(pair):
        here = jnp.where(y == 0, pair[0], pair[1])
        there = jnp.where(y == 0, pair[1], pair[0])
        got = swap(there, "y")
        rows2 = jnp.where(y == 0, jnp.stack([here, got]), jnp.stack([got, here]))
        mate = swap(rows2, "c")
        full = jnp.where(
            c == 0, jnp.concatenate([rows2, mate], axis=1), jnp.concatenate([mate, rows2], axis=1)
        )
        return jnp.where(c == h, full, swap(full, "h"))

    result_all = spread(result)
    grad_all = spread(grads_x)
    return (
        result_all[None, :, :, : z.d], result_all[None, :, :, z.d :],
        grad_all[None, :, :, : z.d], grad_all[None, :, :, z.d :],
    ) + gt + glay


def solution(mesh):
    section, dp, tensor = (mesh.shape[a] for a in ("section", "dp", "tensor"))
    fine = Mesh(mesh.devices.reshape(section, dp // 2, 2, 2, tensor // 2), ALL)
    d, t = ("x", "c"), ("h", "l")
    weights = (
        P("y", None, d, t),
        P("y", None, t + d),
        P("y", t, d),
        P("y", None, d),
        P("y", None, d),
        P("y", d, t),
        P("y", t + d),
        P("y", t, d),
    ) * 2
    pages = (P(d, None, None), P(d, None, None))
    return jax.shard_map(
        per_device,
        mesh=fine,
        in_specs=pages + (P(d, None),) + pages + weights,
        out_specs=(P("y", d, None, None),) * 4 + weights,
        check_vma=False,
    )
```

```python
import functools

import jax
import jax.numpy as jnp
from jax import lax
from jax.experimental import pallas as pl
from jax.experimental.pallas import tpu as pltpu
from jax.sharding import Mesh, PartitionSpec as P

BF = jnp.bfloat16
F32 = jnp.float32
HEAD = 64
LHEAD = 16
SLOT = 128
GROUPS = 3
ALL = ("y", "x", "c", "h", "l")


def mm(a, b):
    return lax.dot_general(a, b, (((1,), (0,)), ((), ())), preferred_element_type=F32)


def mm_nt(a, b):
    return lax.dot_general(a, b, (((1,), (1,)), ((), ())), preferred_element_type=F32)


def mm_tn(a, b):
    return lax.dot_general(a, b, (((0,), (0,)), ((), ())), preferred_element_type=F32)


class Sizes:
    def __init__(self, text, layout, rd, ld, cols, lcols, dp):
        self.seq = text.shape[1]
        self.rows = self.seq // 2
        self.d = text.shape[2]
        self.ld = layout.shape[2]
        self.width = self.d + self.ld
        self.rd = rd
        self.lr = ld
        self.dp = dp
        self.quarter = cols
        self.lquarter = lcols
        self.heads = cols // HEAD
        self.block = rd + ld // GROUPS
        self.vblock = self.block + 16
        self.part = ld // GROUPS
        self.xs = dp // 2
        self.masks = 4 if self.xs == 2 else 2


def call(body, out_shapes, *args, scratch=(), meta=None, us=4):
    places = [pl.BlockSpec(memory_space=pltpu.VMEM)] * len(args)
    if meta is not None:
        args = (meta,) + args
        places = [pl.BlockSpec(memory_space=pltpu.SMEM)] + places
    return pl.pallas_call(
        body,
        out_shape=list(out_shapes),
        in_specs=places,
        out_specs=[pl.BlockSpec(memory_space=pltpu.VMEM)] * len(out_shapes),
        scratch_shapes=list(scratch),
        compiler_params=pltpu.CompilerParams(vmem_limit_bytes=56 * 2**20),
        cost_estimate=pl.CostEstimate(flops=int(us * 2.3e9), bytes_accessed=1000, transcendentals=0),
    )(*args)


def sds(shape, dtype):
    return jax.ShapeDtypeStruct(shape, dtype)


def text_w(w, h, z, lo=0, hi=None):
    return jnp.concatenate(
        [w[r % 2][r // 2, w[2](h), : z.rd, lo:hi] for r in range(z.dp)], axis=0
    )


def layout_w(w, h, z, lo=0, hi=None):
    width = w[0].shape[-1] // GROUPS
    hi = width if hi is None else hi
    pieces = []
    for r in range(z.dp):
        for k in range(GROUPS):
            rows = slice(z.rd, z.rd + z.part)
            pieces.append(w[r % 2][r // 2, w[2](h), rows, width * k + lo : width * k + hi])
    return jnp.concatenate(pieces, axis=0)


def alone(h):
    return h


def first_of_two(h):
    return 2 * h


def second_of_two(h):
    return 2 * h + 1


def feed_forward(refs):
    if len(refs) == 4:
        return (refs[0], refs[1], alone), (refs[2], refs[3], alone)
    return (refs[0], refs[1], first_of_two), (refs[0], refs[1], second_of_two)


def put_grads(g, h, text, layout, z):
    width = g[0].shape[-1] // GROUPS
    low = layout.astype(BF)
    pad = width - low.shape[-1]
    low = jnp.concatenate([low, jnp.zeros((low.shape[0], pad), BF)], axis=1)
    text = text.astype(BF)
    at = g[2](h)
    for r in range(z.dp):
        ref, x = g[r % 2], r // 2
        ref[x, at, : z.rd, :] = text[z.rd * r : z.rd * (r + 1)]
        for k in range(GROUPS):
            base = z.lr * r + z.part * k
            ref[x, at, z.rd : z.block, width * k : width * (k + 1)] = low[base : base + z.part]


def natural(pieces, m, z):
    out = []
    for d in range(z.dp):
        value = pieces[d]
        for other in range(1, z.masks):
            value = jnp.where(m == other, pieces[d ^ other], value)
        out.append(value)
    return jnp.concatenate(out, axis=1)


def norm_stats(resid):
    center = resid - jnp.mean(resid, axis=-1, keepdims=True)
    factor = lax.rsqrt(jnp.mean(center * center, axis=-1, keepdims=True) + 1e-05)
    return center * factor, factor


def norm_both(resid, z):
    nt, ft = norm_stats(resid[:, : z.d])
    nl, fl = norm_stats(resid[:, z.d :])
    return jnp.concatenate([nt, nl], axis=1), ft, fl


def norm_back(grad, normed, factor, gain):
    scaled = grad * gain
    return factor * (
        scaled
        - jnp.mean(scaled, axis=-1, keepdims=True)
        - normed * jnp.mean(scaled * normed, axis=-1, keepdims=True)
    )


def norm_back_both(grad, normed, ft, fl, gain, z):
    gt = norm_back(grad[:, : z.d], normed[:, : z.d], ft, gain[:, : z.d])
    gl = norm_back(grad[:, z.d :], normed[:, z.d :], fl, gain[:, z.d :])
    return jnp.concatenate([gt, gl], axis=1)


def small_rows(w, h, z):
    return [w[r % 2][r // 2, h, z.block : z.vblock, :].astype(F32) for r in range(z.dp)]


def qkv_body(z, fused, meta_ref, *refs):
    if fused:
        (hid_ref, own_ref, rec_ref, prev_ref, ws_ref, wc_ref,
         r_ref, x_ref, q_ref, kv_ref, vec_ref, ut_ref, ul_ref) = refs
        vec = prev_ref[...]
        resid = (
            hid_ref[...].astype(F32) + own_ref[...].astype(F32) + rec_ref[...].astype(F32) + vec[4:5]
        )
        r_ref[...] = resid
        normed, _, _ = norm_both(resid, z)
        x = (normed * vec[1:2] + vec[5:6]).astype(BF)
        x_ref[...] = x
    else:
        x_ref, ws_ref, wc_ref, q_ref, kv_ref, vec_ref, ut_ref, ul_ref = refs
        x = x_ref[...]
    w = (ws_ref, wc_ref, alone)
    mask = meta_ref[1]
    lane = 4 * SLOT
    small = small_rows(w, 0, z)
    vec_ref[:, : z.d] = jnp.concatenate([s[:, : z.rd] for s in small], axis=1)
    vec_ref[:, z.d :] = jnp.concatenate([s[:, lane : lane + z.lr] for s in small], axis=1)
    xt, xl = x[:, : z.d], x[:, z.d :]
    n, m = z.quarter, z.lquarter
    zeros = jnp.zeros((z.rows, SLOT - HEAD - LHEAD), BF)
    hb, lb, ub, vb = n // z.dp, m // z.dp, 4 * n // z.dp, 4 * m // z.dp
    for h in range(2):
        small = small_rows(w, h, z)
        rows = lambda i, lo, size: natural([s[i : i + 1, lo : lo + size] for s in small], mask, z)
        ut_ref[h] = rows(8, 0, ub)
        ul_ref[h] = rows(8, lane, vb)
        bt = jnp.concatenate([rows(6, 0, hb), jnp.zeros((1, n), F32), rows(7, 0, hb)], axis=1)
        bl = jnp.concatenate(
            [rows(6, lane, lb), jnp.zeros((1, m), F32), rows(7, lane, lb)], axis=1
        )
        yt = mm(xt, text_w(w, h, z, 0, 3 * n)) + bt
        yl = mm(xl, layout_w(w, h, z, 0, 3 * m)) + bl
        yt = yt.astype(BF)
        yl = yl.astype(BF)
        for s in range(3):
            for j in range(z.heads):
                a = yt[:, n * s + HEAD * j : n * s + HEAD * (j + 1)]
                b = yl[:, m * s + LHEAD * j : m * s + LHEAD * (j + 1)]
                if s == 0:
                    a = a * BF(HEAD**-0.5)
                    b = b * BF(LHEAD**-0.5)
                slot = jnp.concatenate([a, b, zeros], axis=1)
                head = z.heads * h + j
                if s == 0:
                    q_ref[head] = slot
                else:
                    kv_ref[2 * z.heads * (s - 1) + head] = slot


def attend_body(z, q_ref, own_ref, rec_ref, mask_ref, ws_ref, wc_ref, a_ref, c_ref, p_ref, s_ref):
    w = (ws_ref, wc_ref, alone)
    count = 2 * z.heads
    m0 = mask_ref[0:1, : z.rows] > 0
    m1 = mask_ref[0:1, z.rows :] > 0

    def head(j, carry):
        q = q_ref[j]
        s0 = jnp.where(m0, mm_nt(q, own_ref[j]), -1000000000.0)
        s1 = jnp.where(m1, mm_nt(q, rec_ref[j]), -1000000000.0)
        top = jnp.maximum(
            jnp.max(s0, axis=-1, keepdims=True), jnp.max(s1, axis=-1, keepdims=True)
        )
        e0 = jnp.exp(s0 - top)
        e1 = jnp.exp(s1 - top)
        inv = 1.0 / (jnp.sum(e0, axis=-1, keepdims=True) + jnp.sum(e1, axis=-1, keepdims=True))
        p0 = (e0 * inv).astype(BF)
        p1 = (e1 * inv).astype(BF)
        p_ref[j, :, : z.rows] = p0
        p_ref[j, :, z.rows :] = p1
        s_ref[j] = (mm(p0, own_ref[count + j]) + mm(p1, rec_ref[count + j])).astype(BF)
        return carry

    lax.fori_loop(0, count, head, 0)
    n, m = z.quarter, z.lquarter
    at = al = None
    for h in range(2):
        heads = [s_ref[z.heads * h + j] for j in range(z.heads)]
        ct = jnp.concatenate([s[:, :HEAD] for s in heads], axis=1)
        cl = jnp.concatenate([s[:, HEAD : HEAD + LHEAD] for s in heads], axis=1)
        c_ref[h, :, :n] = ct
        c_ref[h, :, 2 * SLOT : 2 * SLOT + m] = cl
        pt = mm_nt(ct, text_w(w, h, z, 3 * n, 4 * n))
        pll = mm_nt(cl, layout_w(w, h, z, 3 * m, 4 * m))
        at = pt if at is None else at + pt
        al = pll if al is None else al + pll
    a_ref[:, : z.d] = at.astype(BF)
    a_ref[:, z.d :] = al.astype(BF)


def gelu_parts(u):
    cdf = 0.5 * (1.0 + lax.erf(u * 0.7071067811865476))
    slope = cdf + u * jnp.exp(-0.5 * u * u) * 0.3989422804014327
    return (u * cdf).astype(BF), slope.astype(BF)


def forward_body(
    z, x_ref, own_ref, rec_ref, vec_ref, bt_ref, bl_ref, *refs
):
    r_ref, hid_ref, gt_ref, gl_ref, st_ref, sl_ref, f_ref = refs[-7:]
    up, down = feed_forward(refs[:-7])
    lw = 4 * z.lquarter
    vec = vec_ref[...]
    resid = x_ref[...].astype(F32) + own_ref[...].astype(F32) + rec_ref[...].astype(F32) + vec[2:3]
    r_ref[...] = resid
    normed, _, _ = norm_both(resid, z)
    hid = (normed * vec[0:1] + vec[3:4]).astype(BF)
    hid_ref[...] = hid
    ht, hl = hid[:, : z.d], hid[:, z.d :]
    ft = fl = None
    for h in range(2):
        g, s = gelu_parts(mm(ht, text_w(up, h, z)) + bt_ref[h])
        gt_ref[h] = g
        st_ref[h] = s
        p = mm_nt(g, text_w(down, h, z))
        ft = p if ft is None else ft + p
        g, s = gelu_parts(mm(hl, layout_w(up, h, z, 0, lw)) + bl_ref[h])
        gl_ref[h] = g
        sl_ref[h] = s
        p = mm_nt(g, layout_w(down, h, z, 0, lw))
        fl = p if fl is None else fl + p
    f_ref[:, : z.d] = ft.astype(BF)
    f_ref[:, z.d :] = fl.astype(BF)


def col_sum(value):
    return jnp.sum(value, axis=0, keepdims=True)


def tail_body(z, fused, *refs):
    if fused == "last":
        hid_ref, own_ref, rec_ref, go_ref, vec_ref, st_ref, sl_ref = refs[:7]
        ws = refs[7:-9]
        out_ref, d2_ref, df_ref, dut_ref, dul_ref, dh_ref, vg_ref, gbt_ref, gbl_ref = refs[-9:]
        vec = vec_ref[...]
        resid = (
            hid_ref[...].astype(F32) + own_ref[...].astype(F32) + rec_ref[...].astype(F32) + vec[4:5]
        )
        normed, ft, fl = norm_both(resid, z)
        out_ref[...] = (normed * vec[1:2] + vec[5:6]).astype(BF)
        go = go_ref[...].astype(F32)
    else:
        r_ref, d1_ref, own_ref, rec_ref, vec_ref, st_ref, sl_ref = refs[:7]
        ws = refs[7:-9]
        dx_ref, d2_ref, df_ref, dut_ref, dul_ref, dh_ref, vg_ref, gbt_ref, gbl_ref = refs[-9:]
        vec = vec_ref[...]
        normed, ft, fl = norm_both(r_ref[...], z)
        low = (d1_ref[...] + own_ref[...].astype(F32) + rec_ref[...].astype(F32)).astype(BF)
        dx_ref[...] = low
        go = low.astype(F32)
    up, down = feed_forward(ws)
    lw = 4 * z.lquarter
    d2 = norm_back_both(go, normed, ft, fl, vec[1:2], z)
    d2_ref[...] = d2
    df = d2.astype(BF)
    df_ref[...] = df
    vg_ref[0:1] = col_sum(go * normed)
    vg_ref[1:2] = col_sum(go)
    vg_ref[2:3] = col_sum(df.astype(F32))
    vg_ref[3:8] = jnp.zeros((5, z.width), F32)
    dft, dfl = df[:, : z.d], df[:, z.d :]
    ht = hl = None
    for h in range(2):
        du = (mm(dft, text_w(down, h, z)) * st_ref[h].astype(F32)).astype(BF)
        dut_ref[h] = du
        gbt_ref[h] = col_sum(du.astype(F32))
        p = mm_nt(du, text_w(up, h, z))
        ht = p if ht is None else ht + p
        du = (mm(dfl, layout_w(down, h, z, 0, lw)) * sl_ref[h].astype(F32)).astype(BF)
        dul_ref[h] = du
        gbl_ref[h] = col_sum(du.astype(F32))
        p = mm_nt(du, layout_w(up, h, z, 0, lw))
        hl = p if hl is None else hl + p
    dh_ref[:, : z.d] = ht.astype(BF)
    dh_ref[:, z.d :] = hl.astype(BF)


def ffn_grads_body(z, hid_ref, df_ref, gt_ref, gl_ref, dut_ref, dul_ref, g_ref, h_ref):
    one, two = (g_ref, h_ref, first_of_two), (g_ref, h_ref, second_of_two)
    hid, df = hid_ref[...], df_ref[...]
    for h in range(2):
        put_grads(one, h, mm_tn(hid[:, : z.d], dut_ref[h]), mm_tn(hid[:, z.d :], dul_ref[h]), z)
        put_grads(two, h, mm_tn(df[:, : z.d], gt_ref[h]), mm_tn(df[:, z.d :], gl_ref[h]), z)


def attend_back_body(
    z, d2_ref, own_ref, rec_ref, r_ref, vec_ref, ws_ref, wc_ref, c_ref, q_ref, kv_ref, kvr_ref, p_ref, mask_ref,
    d1_ref, da_ref, dq_ref, dkv_ref, dkvr_ref, vg_ref, dc_ref, dd_ref,
):
    count = 2 * z.heads
    w = (ws_ref, wc_ref, alone)
    vec = vec_ref[...]
    dh = d2_ref[...] + own_ref[...].astype(F32) + rec_ref[...].astype(F32)
    normed, ft, fl = norm_both(r_ref[...], z)
    d1 = norm_back_both(dh, normed, ft, fl, vec[0:1], z)
    d1_ref[...] = d1
    da = d1.astype(BF)
    da_ref[...] = da
    vg_ref[0:1] = col_sum(dh * normed)
    vg_ref[1:2] = col_sum(dh)
    vg_ref[2:3] = col_sum(da.astype(F32))
    vg_ref[3:8] = jnp.zeros((5, z.width), F32)
    n, m = z.quarter, z.lquarter
    zeros = jnp.zeros((z.rows, SLOT - HEAD - LHEAD), BF)
    for h in range(2):
        dct = mm(da[:, : z.d], text_w(w, h, z, 3 * n, 4 * n)).astype(BF)
        dcl = mm(da[:, z.d :], layout_w(w, h, z, 3 * m, 4 * m)).astype(BF)
        for j in range(z.heads):
            a = dct[:, HEAD * j : HEAD * (j + 1)]
            b = dcl[:, LHEAD * j : LHEAD * (j + 1)]
            dc_ref[z.heads * h + j] = jnp.concatenate([a, b, zeros], axis=1)
            ct = c_ref[h, :, HEAD * j : HEAD * (j + 1)].astype(F32)
            cl = c_ref[h, :, 2 * SLOT + LHEAD * j : 2 * SLOT + LHEAD * (j + 1)].astype(F32)
            dt = jnp.sum(a.astype(F32) * ct, axis=-1, keepdims=True)
            dl = jnp.sum(b.astype(F32) * cl, axis=-1, keepdims=True)
            dd_ref[z.heads * h + j, :, 0:1] = dt
            dd_ref[z.heads * h + j, :, 1:2] = dt + dl
    lane = lax.broadcasted_iota(jnp.int32, (z.rows, SLOT), 1)
    text_lane = lane < HEAD
    scale = jnp.where(text_lane, HEAD**-0.5, LHEAD**-0.5)
    mask = mask_ref[...]
    masks = (mask[:, : z.rows], mask[:, z.rows :])

    def head(j, carry):
        dc = dc_ref[j]
        dct = jnp.where(text_lane, dc, jnp.zeros_like(dc))
        q = q_ref[j]
        dt = dd_ref[j, :, 0:1]
        ds = dd_ref[j, :, 1:2]
        dq_t = dq_s = None
        for i, (k_ref, o_ref) in enumerate(((kv_ref, dkv_ref), (kvr_ref, dkvr_ref))):
            k = k_ref[j]
            v = k_ref[count + j]
            prob = p_ref[j, :, z.rows * i : z.rows * (i + 1)]
            pm = jnp.where(masks[i] > 0, prob.astype(F32), 0.0)
            st = (pm * (mm_nt(dct, v) - dt)).astype(BF)
            ss = (pm * (mm_nt(dc, v) - ds)).astype(BF)
            a = mm(st, k)
            b = mm(ss, k)
            dq_t = a if dq_t is None else dq_t + a
            dq_s = b if dq_s is None else dq_s + b
            dk = jnp.where(text_lane, mm_tn(st, q), mm_tn(ss, q))
            o_ref[j] = dk.astype(BF)
            o_ref[count + j] = mm_tn(prob, dc).astype(BF)
        dq_ref[j] = (jnp.where(text_lane, dq_t, dq_s) * scale).astype(BF)
        return carry

    lax.fori_loop(0, count, head, 0)


def input_back_body(z, dq_ref, dkv_ref, rec_ref, ws_ref, wc_ref, yt_ref, yl_ref, dx_ref, gbt_ref, gbl_ref):
    count = 2 * z.heads
    w = (ws_ref, wc_ref, alone)
    n, m = z.quarter, z.lquarter
    xt = xl = None
    for h in range(2):
        ts, ls = [], []
        for s in range(3):
            for j in range(z.heads):
                head = z.heads * h + j
                if s == 0:
                    slot = dq_ref[head]
                else:
                    at = count * (s - 1) + head
                    slot = (dkv_ref[at].astype(F32) + rec_ref[at].astype(F32)).astype(BF)
                ts.append(slot[:, :HEAD])
                ls.append(slot[:, HEAD : HEAD + LHEAD])
        yt = jnp.concatenate(ts, axis=1)
        yl = jnp.concatenate(ls, axis=1)
        yt_ref[h] = yt
        yl_ref[h] = yl
        gbt_ref[h] = col_sum(yt.astype(F32))
        gbl_ref[h] = col_sum(yl.astype(F32))
        p = mm_nt(yt, text_w(w, h, z, 0, 3 * n))
        xt = p if xt is None else xt + p
        p = mm_nt(yl, layout_w(w, h, z, 0, 3 * m))
        xl = p if xl is None else xl + p
    dx_ref[:, : z.d] = xt.astype(BF)
    dx_ref[:, z.d :] = xl.astype(BF)


def input_grads_body(
    z, meta_ref, x_ref, da_ref, c_ref, yt_ref, yl_ref, va_ref, vb_ref, bt_ref, bl_ref, ut_ref, ul_ref,
    g_ref, h_ref, s_ref,
):
    g = (g_ref, h_ref, alone)
    x, da = x_ref[...], da_ref[...]
    n, m = z.quarter, z.lquarter
    va, vb = va_ref[...], vb_ref[...]
    mask = meta_ref[1]
    rows = (vb[0:1], va[0:1], vb[2:3], vb[1:2], va[2:3], va[1:2])
    lane = 4 * SLOT
    s_ref[...] = jnp.zeros_like(s_ref)

    def relative(value, size):
        parts = [value[:, size * d : size * (d + 1)] for d in range(z.dp)]
        out = []
        for r in range(z.dp):
            v = parts[r]
            for other in range(1, z.masks):
                v = jnp.where(mask == other, parts[r ^ other], v)
            out.append(v)
        return out

    for h in range(2):
        ct = c_ref[h, :, :n]
        cl = c_ref[h, :, 2 * SLOT : 2 * SLOT + m]
        text = jnp.concatenate(
            [mm_tn(x[:, : z.d], yt_ref[h]), mm_tn(da[:, : z.d], ct)], axis=1
        )
        layout = jnp.concatenate(
            [mm_tn(x[:, z.d :], yl_ref[h]), mm_tn(da[:, z.d :], cl)], axis=1
        )
        put_grads(g, h, text, layout, z)
        bt, bl, ut, ul = bt_ref[h], bl_ref[h], ut_ref[h], ul_ref[h]
        entries = [
            (6, 0, relative(bt[:, :n], n // z.dp)),
            (7, 0, relative(bt[:, 2 * n :], n // z.dp)),
            (6, lane, relative(bl[:, :m], m // z.dp)),
            (7, lane, relative(bl[:, 2 * m :], m // z.dp)),
            (8, 0, relative(ut, 4 * n // z.dp)),
            (8, lane, relative(ul, 4 * m // z.dp)),
        ]
        for r in range(z.dp):
            for i, row in enumerate(rows):
                s_ref[i : i + 1, : z.rd] = row[:, z.rd * r : z.rd * (r + 1)]
                s_ref[i : i + 1, lane : lane + z.lr] = row[
                    :, z.d + z.lr * r : z.d + z.lr * (r + 1)
                ]
            for at, lo, values in entries:
                s_ref[at : at + 1, lo : lo + values[r].shape[1]] = values[r]
            g[r % 2][r // 2, h, z.block : z.vblock, :] = s_ref[...].astype(BF)


def put_pack(out_ref, text, layout, z):
    out_ref[: z.rd, :] = text.astype(BF)
    width = out_ref.shape[-1] // GROUPS
    low = layout.astype(BF)
    low = jnp.concatenate([low, jnp.zeros((low.shape[0], width - low.shape[1]), BF)], axis=1)
    for k in range(GROUPS):
        out_ref[z.rd : z.block, width * k : width * (k + 1)] = low[z.part * k : z.part * (k + 1)]


def pack_first_body(
    z, ti_ref, to_ref, li_ref, lo_ref, tg_ref, lg_ref, ts_ref, ls_ref, tb_ref, lb_ref, tu_ref, lu_ref,
    out_ref, s_ref,
):
    text = jnp.concatenate([ti_ref[0, 0], ti_ref[0, 1], ti_ref[0, 2], to_ref[0].T], axis=1)
    layout = jnp.concatenate([li_ref[0, 0], li_ref[0, 1], li_ref[0, 2], lo_ref[0].T], axis=1)
    put_pack(out_ref, text, layout, z)
    s_ref[...] = jnp.zeros_like(s_ref)
    for lane, refs in ((0, (tg_ref, ts_ref, tb_ref)), (4 * SLOT, (lg_ref, ls_ref, lb_ref))):
        at = 0
        for ref in refs:
            count, width = ref.shape[1], ref.shape[2]
            s_ref[at : at + count, lane : lane + width] = ref[0]
            at += count
    s_ref[8:9, : tu_ref.shape[1]] = tu_ref[...]
    s_ref[8:9, 4 * SLOT : 4 * SLOT + lu_ref.shape[1]] = lu_ref[...]
    out_ref[z.block : z.vblock, :] = s_ref[...].astype(BF)


def pack_rest_body(z, tu_ref, lu_ref, td_ref, ld_ref, out_ref):
    put_pack(out_ref.at[0], tu_ref[0], lu_ref[0], z)
    put_pack(out_ref.at[1], td_ref[0], ld_ref[0], z)


def take_layout(total, cols, z):
    width = total.shape[-1] // GROUPS
    return jnp.concatenate(
        [total[z.rd : z.block, width * k : width * k + cols] for k in range(GROUPS)], axis=0
    )


def final_sum(refs):
    return sum(r[...].astype(F32) for r in refs)


def finish_first_body(z, *refs):
    (ti_ref, tb_ref, to_ref, tg_ref, ts_ref, tu_ref,
     li_ref, lb_ref, lo_ref, lg_ref, ls_ref, lu_ref) = refs[2:]
    total = final_sum(refs[:2])[0]
    n, m = z.quarter, z.lquarter
    layout = take_layout(total, 4 * m, z)
    for s in range(3):
        ti_ref[0, s] = total[: z.rd, n * s : n * (s + 1)]
        li_ref[0, s] = layout[:, m * s : m * (s + 1)]
    to_ref[0] = total[: z.rd, 3 * n :].T
    lo_ref[0] = layout[:, 3 * m :].T
    rows = total[z.block : z.vblock]
    for lane, group in ((0, (tg_ref, ts_ref, tb_ref)), (4 * SLOT, (lg_ref, ls_ref, lb_ref))):
        at = 0
        for ref in group:
            count, width = ref.shape[1], ref.shape[2]
            ref[0] = rows[at : at + count, lane : lane + width]
            at += count
    tu_ref[...] = rows[8:9, : tu_ref.shape[1]]
    lu_ref[...] = rows[8:9, 4 * SLOT : 4 * SLOT + lu_ref.shape[1]]


def finish_body(z, *refs):
    total = final_sum(refs[:2])
    for p in range(2):
        t_ref, l_ref = refs[2 + 2 * p : 4 + 2 * p]
        t_ref[0] = total[p, : z.rd]
        l_ref[0] = take_layout(total[p], 4 * z.lquarter, z)


def entry_body(z, meta_ref, t_ref, l_ref, tc_ref, lc_ref, mask_ref, own_ref, send_ref):
    y, c = meta_ref[0], meta_ref[2]
    for ref, half in ((own_ref, c), (send_ref, 1 - c)):
        rows = pl.ds(pl.multiple_of(half * z.rows, z.rows), z.rows)
        at = 0
        for source, flip in ((t_ref, False), (l_ref, True), (tc_ref, False), (lc_ref, True)):
            if flip:
                value = source[y, :, rows].astype(F32).T.astype(BF)
            else:
                value = source[y, rows, :]
            ref[: z.rows, at : at + value.shape[1]] = value
            at += value.shape[1]
        row = jnp.where(y == 0, mask_ref[0:1, :], mask_ref[1:2, :]).astype(F32)
        ref[z.rows :, : z.seq] = jnp.broadcast_to(row, (16, z.seq)).astype(BF)
        ref[z.rows :, z.seq :] = jnp.zeros((16, ref.shape[1] - z.seq), BF)


def ordered(value, m, z):
    text = [value[:, z.rd * r : z.rd * (r + 1)] for r in range(z.dp)]
    layout = [value[:, z.d + z.lr * r : z.d + z.lr * (r + 1)] for r in range(z.dp)]
    return jnp.concatenate([natural(text, m, z), natural(layout, m, z)], axis=1)


def settle_body(z, meta_ref, own_ref, got_ref, x_ref, cot_ref, out_ref):
    mine = meta_ref[3] == 1
    mask, c = meta_ref[1], meta_ref[2]
    value = jnp.where(mine, own_ref[: z.rows], got_ref[: z.rows])
    x_ref[...] = ordered(value[:, : z.width], mask, z)
    cot_ref[...] = ordered(value[:, z.width :], mask, z)
    row = jnp.where(mine, own_ref[z.rows :, : z.seq], got_ref[z.rows :, : z.seq]).astype(F32)[0:1]
    left, right = row[:, : z.rows], row[:, z.rows :]
    out_ref[:, : z.rows] = jnp.where(c == 0, left, right)
    out_ref[:, z.rows :] = jnp.where(c == 0, right, left)


def exit_body(z, summed, meta_ref, *refs):
    if summed:
        d_ref, own_ref, rec_ref, b_ref, here_ref, part_ref, send_ref = refs
        one = (d_ref[...] + own_ref[...].astype(F32) + rec_ref[...].astype(F32)).astype(BF)
    else:
        a_ref, b_ref, here_ref, part_ref, send_ref = refs
        one = a_ref[...]
    first = meta_ref[0] == 0
    low = meta_ref[4] == 0
    mask = meta_ref[1]
    two = b_ref[...]
    half = z.rows // 2
    here = ordered(jnp.where(first, one, two), mask, z)
    here_ref[...] = here
    part_ref[...] = jnp.where(low, here[:half], here[half:])
    there = jnp.where(first, two, one)
    send_ref[...] = ordered(jnp.where(low, there[:half], there[half:]), mask, z)


def sort_body(z, meta_ref, here_ref, a_ref, bd_ref, far_ref, keep_ref, send_ref):
    mine = meta_ref[3] == 1
    low = meta_ref[4] == 0
    half = z.rows // 2
    b_ref, d_ref = (bd_ref.at[half * i : half * (i + 1)] for i in range(2))
    ao_ref, bo_ref, do_ref = (far_ref.at[half * i : half * (i + 1)] for i in range(3))
    for i, (left, right) in enumerate(((b_ref, bo_ref), (d_ref, do_ref))):
        for k in range(2):
            rows = slice(half * k, half * (k + 1))
            other = jnp.where(low == (k == 0), left[...], right[...])
            if i == 0:
                same = here_ref[rows, :]
            else:
                same = jnp.where(low == (k == 0), a_ref[...], ao_ref[...])
            rows = slice(z.rows * i + half * k, z.rows * i + half * (k + 1))
            keep_ref[rows, :] = jnp.where(mine, same, other)
            send_ref[rows, :] = jnp.where(mine, other, same)


def place_body(z, meta_ref, keep_ref, got_ref, t_ref, l_ref):
    y, c = meta_ref[0], meta_ref[2]
    for i in range(2):
        page = y if i == 0 else 1 - y
        for ref, half in ((keep_ref, c), (got_ref, 1 - c)):
            rows = pl.ds(pl.multiple_of(half * z.rows, z.rows), z.rows)
            value = ref[z.rows * i : z.rows * (i + 1), :]
            t_ref[0, page, rows, :] = value[:, : z.d]
            l_ref[0, page, :, rows] = value[:, z.d :].astype(F32).T.astype(BF)


def swap(value, axis):
    return lax.ppermute(value, axis, [(0, 1), (1, 0)])


def after(value, *others):
    return lax.optimization_barrier((value,) + others)[0]


def gather_blocks(parts, x_size, *token):
    if x_size == 2:
        got = [after(swap(v, "x"), *token) for v in parts]
        own = jnp.stack([jnp.concatenate(parts), jnp.concatenate(got)])
    else:
        own = lax.all_gather(jnp.concatenate(parts), "x", axis=0)
    return own, swap(own, "c")


def add_low(*terms):
    total = terms[0].astype(F32)
    for term in terms[1:]:
        total = total + term.astype(F32)
    return total.astype(BF)


class Reduce:
    def __init__(self, keep, send, x_size):
        self.keep, self.x_size = keep, x_size
        half = keep.shape[1] // 2
        self.rows = (slice(half, None), slice(0, half), slice(None))
        self.got = swap(send, "c")
        self.far = {}

    def x_step(self, part, *token):
        got, rows = after(self.got, *token), self.rows[part]
        if self.x_size == 2:
            total = add_low(self.keep[1, rows], got[1, rows])
            self.far[part] = swap(total, "x")
        else:
            total = add_low(self.keep[:, rows], got[:, rows])
            self.far[part] = lax.psum_scatter(total, "x", scatter_dimension=0, tiled=False)
        return total

    def near(self, part, *token):
        rows = self.rows[part]
        if part in self.far:
            far = after(self.far[part], *token)
        else:
            far = after(self.far[2], *token)[rows]
        if self.x_size == 2:
            far = add_low(self.keep[0, rows], self.got[0, rows], far)
        return far


class Finish:
    def __init__(self, y):
        self.y, self.here, self.cross = y, {}, {}

    def y_step(self, part, first, second):
        self.here[part] = jnp.where(self.y == 0, first, second)
        self.cross[part] = swap(jnp.where(self.y == 0, second, first), "y")
        return self.here[part]

    def h_step(self, *token):
        other = add_low(self.here[0], after(self.cross[0], *token))
        self.last = swap(other, "h")
        return other

    def close(self, *token):
        self.own = add_low(self.here[1], after(self.cross[1], *token))
        return self.own

    def terms(self, *token):
        return (self.own, after(self.last, *token))


def per_device(
    text_in, layout_in, token_mask, text_cotangent, layout_cotangent,
    t_in, t_hb, t_out, t_gain, t_shift, t_up, t_ub, t_down,
    l_in, l_hb, l_out, l_gain, l_shift, l_up, l_ub, l_down,
):
    x_size = lax.axis_size("x")
    y, x, c, h, l = (lax.axis_index(a) for a in ALL)
    z = Sizes(
        text_in, layout_in, t_in.shape[2], l_in.shape[2], t_in.shape[3], l_in.shape[3], 2 * x_size
    )
    order = 2 * x + c if x_size == 2 else c
    meta = jnp.stack([y, order, c, (c == h).astype(jnp.int32), l, 0 * y, 0 * y, 0 * y])
    bind = functools.partial
    cols = t_up.shape[2]

    R, W, Q, M = z.rows, z.width, 4 * z.quarter, 4 * z.lquarter
    nh = 2 * z.heads
    flip = lambda v: jnp.swapaxes(v, -1, -2)

    (first,) = call(
        bind(pack_first_body, z), [sds((z.vblock, cols), BF)],
        t_in, t_out, l_in, l_out, t_gain, l_gain, t_shift, l_shift, t_hb, l_hb, t_ub, l_ub,
        scratch=[pltpu.VMEM((16, cols), F32)],
    )
    (rest,) = call(
        bind(pack_rest_body, z), [sds((2, z.block, cols), BF)],
        after(t_up, first), l_up, flip(t_down), flip(l_down), us=10,
    )
    own, send = call(
        bind(entry_body, z), [sds((R + 16, 2 * W), BF)] * 2,
        after(text_in, rest), flip(layout_in), text_cotangent, flip(layout_cotangent), token_mask,
        meta=meta, us=10,
    )
    first = first[None]

    first_h, rest_h = swap(first, "h"), swap(rest, "h")
    first_y = after(swap(first, "y"), rest, own)
    pick = lambda index, mine, across: jnp.where(y == index, mine, across)
    a0 = pick(0, first, first_y)
    got = after(swap(send, "c"), a0)
    x0, cot, mask = call(
        bind(settle_body, z), [sds((R, W), BF)] * 2 + [sds((1, z.seq), F32)], own, got, meta=meta, us=10,
    )
    first_h = after(first_h, x0)
    first_hy = swap(first_h, "y")
    rest_y = swap(after(rest, first_h), "y")
    rest_h = after(rest_h, first_h)
    a1 = pick(0, first_h, after(first_hy, rest_h))
    parts_hy = [swap(rest_h[p : p + 1], "y") for p in range(2)]
    f0 = pick(0, rest, after(rest_y, a1))
    weights = [[gather_blocks([a0, a1], x_size, f0)], []]

    q_shapes = [sds((nh, R, SLOT), BF), sds((2 * nh, R, SLOT), BF)]
    v_shapes = [sds((16, W), F32), sds((2, 1, Q), F32), sds((2, 1, M), F32)]
    saved = []
    inner = None
    for index in range(2):
        w0 = weights[index][0]
        if index == 0:
            q, kv, vec, ut, ul = call(
                bind(qkv_body, z, False), q_shapes + v_shapes, x0, *w0, meta=meta
            )
            xin = x0
        else:
            r2, xin, q, kv, vec, ut, ul = call(
                bind(qkv_body, z, True),
                [sds((R, W), F32), sds((R, W), BF)] + q_shapes + v_shapes,
                *inner, saved[0]["vec"], *w0, meta=meta,
            )
            saved[0]["r2"] = r2
        kvr = swap(kv, "c")
        if index == 0:
            parts_hy[0] = after(parts_hy[0], kv)
            f1 = pick(0, rest_h[0:1], parts_hy[0])
            kvr = after(kvr, f1)
        a, ctx, prob = call(
            bind(attend_body, z),
            [sds((R, W), BF), sds((2, R, 3 * SLOT), BF), sds((nh, R, z.seq), BF)],
            q, kv, kvr, mask, *w0, scratch=[pltpu.VMEM((nh, R, SLOT), BF)], us=8,
        )
        ar = swap(a, "l")
        if index == 0:
            parts_hy[1] = after(parts_hy[1], a)
            f2 = pick(0, rest_h[1:2], parts_hy[1])
            weights[0].append(gather_blocks([f0, f1, f2], x_size, f2))
            second = jnp.concatenate([pick(1, first, first_y), pick(1, after(first_h, f2), first_hy)])
            second_rest = jnp.concatenate(
                [pick(1, rest, rest_y)]
                + [pick(1, after(rest_h, f2)[p : p + 1], parts_hy[p]) for p in range(2)]
            )
            ar = after(ar, second, second_rest)
        r1, hid, gt, gl, st, sl, f = call(
            bind(forward_body, z),
            [sds((R, W), F32), sds((R, W), BF), sds((2, R, Q), BF), sds((2, R, M), BF),
             sds((2, R, Q), BF), sds((2, R, M), BF), sds((R, W), BF)],
            xin, a, ar, vec, ut, ul, *weights[index][1], us=6,
        )
        fr = swap(f, "l")
        if index == 0:
            weights[1].append(gather_blocks([second], x_size, hid))
            fr = after(fr, weights[1][0][0])
        inner = (hid, f, fr)
        saved.append(dict(x=xin, q=q, kv=kv, kvr=kvr, ctx=ctx, prob=prob, r1=r1, hid=hid, gt=gt,
                          gl=gl, st=st, sl=sl, vec=vec))
        if index == 0:
            weights[1].append(gather_blocks([second_rest], x_size, inner[2]))

    gshape = sds((x_size, 4, z.block, cols), BF)
    vshape = sds((x_size, 2, z.vblock, cols), BF)

    def tail(index, *args):
        keep = saved[index]
        shapes = [sds((R, W), BF), sds((R, W), F32), sds((R, W), BF), sds((2, R, Q), BF),
                  sds((2, R, M), BF), sds((R, W), BF), sds((8, W), F32), sds((2, 1, Q), F32),
                  sds((2, 1, M), F32)]
        return call(
            bind(tail_body, z, "last" if index == 1 else "mid"), shapes,
            *args, keep["vec"], keep["st"], keep["sl"], *weights[index][1], us=7,
        )

    def ffn_grads(index, df, dut, dul):
        keep = saved[index]
        g, s = call(
            bind(ffn_grads_body, z), [gshape] * 2,
            keep["hid"], df, keep["gt"], keep["gl"], dut, dul, us=6,
        )
        return Reduce(g, s, x_size)

    def attend_back(index, d2, dh, dhr):
        keep = saved[index]
        return call(
            bind(attend_back_body, z),
            [sds((R, W), F32), sds((R, W), BF), q_shapes[0], q_shapes[1], q_shapes[1], sds((8, W), F32)],
            d2, dh, dhr, keep["r1"], keep["vec"], *weights[index][0], keep["ctx"], keep["q"],
            keep["kv"], keep["kvr"], keep["prob"], mask,
            scratch=[pltpu.VMEM((nh, R, SLOT), BF), pltpu.VMEM((nh, R, SLOT), F32)], us=14,
        )

    def input_back(index, dq, dkv, back):
        return call(
            bind(input_back_body, z),
            [sds((2, R, 3 * z.quarter), BF), sds((2, R, 3 * z.lquarter), BF), sds((R, W), BF),
             sds((2, 1, 3 * z.quarter), F32), sds((2, 1, 3 * z.lquarter), F32)],
            dq, dkv, back, *weights[index][0],
        )

    def input_grads(index, *args):
        keep = saved[index]
        g0, s0 = call(
            bind(input_grads_body, z), [vshape] * 2, keep["x"], args[0], keep["ctx"], *args[1:],
            scratch=[pltpu.VMEM((16, cols), F32)], meta=meta,
        )
        return Reduce(g0, s0, x_size)

    def leave(summed, *args):
        return call(
            bind(exit_body, z, summed), [sds((R, W), BF)] + [sds((R // 2, W), BF)] * 2, *args, meta=meta
        )

    out, d2, df, dut, dul, dh, va, gut, gul = tail(1, *inner, cot)
    dhr = swap(dh, "l")
    r1f = ffn_grads(1, df, dut, dul)
    here, part, send = leave(False, xin, after(out, r1f.keep))
    d1, da, dq, dkv, dkvr, vb = attend_back(1, d2, dh, after(dhr, r1f.keep, here))
    back = swap(dkvr, "c")
    back = after(back, r1f.x_step(2, vb))
    got = swap(send, "y")
    yt, yl, dxp, gbt, gbl = input_back(1, dq, dkv, back)
    dxr = swap(dxp, "l")
    r10 = input_grads(1, da, yt, yl, va, vb, gbt, gbl, gut, gul)

    dx1, d2, df, dut, dul, dh, va, gut, gul = tail(
        0, saved[0]["r2"], d1, dxp, after(dxr, r10.keep)
    )
    dhr = swap(dh, "l")
    r0f = ffn_grads(0, df, dut, dul)
    got = after(got, r0f.keep)
    s0 = r0f.x_step(0, got)
    s1 = r0f.x_step(1, s0)
    cross = swap(jnp.concatenate([part, got], axis=0), "h")
    d1, da, dq, dkv, dkvr, vb = attend_back(0, d2, dh, after(dhr, r0f.keep, s0, s1))
    back = swap(dkvr, "c")
    rest, first = Finish(y), Finish(y)
    y0 = rest.y_step(0, r0f.near(0, vb), r1f.near(0, vb))
    cross = after(cross, y0)
    s10 = r10.x_step(2, y0)
    yt, yl, dxp, gbt, gbl = input_back(0, dq, dkv, after(back, s10, cross))
    dxr = swap(dxp, "l")
    y1 = rest.y_step(1, r0f.near(1, dxp), r1f.near(1, dxp))
    r00 = input_grads(0, da, yt, yl, va, vb, gbt, gbl, gut, gul)

    def sort(here, got, cross, low):
        kept, sent = call(
            bind(sort_body, z), [sds((2 * R, W), BF)] * 2, here, got, cross, low, meta=meta,
        )
        return kept, swap(sent, "c")

    def place(kept, sent):
        shape = layout_in.shape
        t, l_ = call(
            bind(place_body, z),
            [sds((1,) + text_in.shape, BF), sds((1, shape[0], shape[2], shape[1]), BF)],
            kept, sent, meta=meta,
        )
        return t, flip(l_)

    dhere, dpart, dsend = leave(True, d1, dxp, after(dxr, r00.keep, y1), dx1)
    dgot = swap(dsend, "y")
    h0 = rest.h_step(dhere)
    s0 = r00.x_step(0, h0)
    s1 = r00.x_step(1, s0)
    dgot = after(dgot, s1)
    dcross = swap(jnp.concatenate([dpart, dgot], axis=0), "h")
    low = swap(jnp.concatenate([got, cross], axis=0), "l")
    own1 = rest.close(dgot)
    y0 = first.y_step(0, r00.near(0, own1), r10.near(0, own1))
    y1 = first.y_step(1, r00.near(1, y0), r10.near(1, y0))
    kept, sent = sort(here, got, cross, after(low, y1))
    h1 = first.h_step(kept)
    own1 = first.close(h1)
    like = lambda *arrays: [sds(v.shape, F32) for v in arrays]
    g_tup, g_lup, g_tdn, g_ldn = call(
        bind(finish_body, z), like(t_up, l_up, flip(t_down), flip(l_down)), *rest.terms(own1)
    )
    res_t, res_l = place(kept, after(sent, g_tup))
    dcross = after(dcross, res_t)
    dlow = swap(jnp.concatenate([dgot, dcross], axis=0), "l")
    g_ti, g_tb, g_to, g_tg, g_ts, g_tu, g_li, g_lb, g_lo, g_lg, g_ls, g_lu = call(
        bind(finish_first_body, z),
        like(t_in, t_hb, t_out, t_gain, t_shift, t_ub, l_in, l_hb, l_out, l_gain, l_shift, l_ub),
        *first.terms(dcross),
    )
    dkept, dsent = sort(dhere, dgot, dcross, after(dlow, g_ti))
    dx_t, dx_l = place(dkept, dsent)
    return (
        res_t, res_l, dx_t, dx_l,
        g_ti, g_tb, g_to, g_tg, g_ts, g_tup, g_tu, flip(g_tdn),
        g_li, g_lb, g_lo, g_lg, g_ls, g_lup, g_lu, flip(g_ldn),
    )


def solution(mesh):
    section, dp, tensor = (mesh.shape[a] for a in ("section", "dp", "tensor"))
    fine = Mesh(mesh.devices.reshape(section, dp // 2, 2, 2, tensor // 2), ALL)
    d, t = ("x", "c"), ("h", "l")
    weights = (
        P("y", None, d, t),
        P("y", None, t + d),
        P("y", t, d),
        P("y", None, d),
        P("y", None, d),
        P("y", d, t),
        P("y", t + d),
        P("y", t, d),
    ) * 2
    pages = (P(d, None, None), P(d, None, None))
    return jax.shard_map(
        per_device,
        mesh=fine,
        in_specs=pages + (P(d, None),) + pages + weights,
        out_specs=(P("y", d, None, None),) * 4 + weights,
        check_vma=False,
    )
```

```python
import functools

import jax
import jax.numpy as jnp
from jax import lax
from jax.experimental import pallas as pl
from jax.experimental.pallas import tpu as pltpu
from jax.sharding import Mesh, PartitionSpec as P

BF = jnp.bfloat16
F32 = jnp.float32
HEAD = 64
LHEAD = 16
SLOT = 128
GROUPS = 3
ALL = ("y", "x", "c", "h", "l")


def mm(a, b):
    return lax.dot_general(a, b, (((1,), (0,)), ((), ())), preferred_element_type=F32)


def mm_nt(a, b):
    return lax.dot_general(a, b, (((1,), (1,)), ((), ())), preferred_element_type=F32)


def mm_tn(a, b):
    return lax.dot_general(a, b, (((0,), (0,)), ((), ())), preferred_element_type=F32)


class Sizes:
    def __init__(self, text, layout, rd, ld, cols, lcols, dp):
        self.seq = text.shape[1]
        self.rows = self.seq // 2
        self.d = text.shape[2]
        self.ld = layout.shape[2]
        self.width = self.d + self.ld
        self.rd = rd
        self.lr = ld
        self.dp = dp
        self.quarter = cols
        self.lquarter = lcols
        self.heads = cols // HEAD
        self.block = rd + ld // GROUPS
        self.vblock = self.block + 16
        self.part = ld // GROUPS
        self.xs = dp // 2
        self.masks = 4 if self.xs == 2 else 2


def call(body, out_shapes, *args, scratch=(), meta=None, us=4):
    places = [pl.BlockSpec(memory_space=pltpu.VMEM)] * len(args)
    if meta is not None:
        args = (meta,) + args
        places = [pl.BlockSpec(memory_space=pltpu.SMEM)] + places
    return pl.pallas_call(
        body,
        out_shape=list(out_shapes),
        in_specs=places,
        out_specs=[pl.BlockSpec(memory_space=pltpu.VMEM)] * len(out_shapes),
        scratch_shapes=list(scratch),
        compiler_params=pltpu.CompilerParams(vmem_limit_bytes=56 * 2**20),
        cost_estimate=pl.CostEstimate(flops=int(us * 2.3e9), bytes_accessed=1000, transcendentals=0),
    )(*args)


def sds(shape, dtype):
    return jax.ShapeDtypeStruct(shape, dtype)


def text_w(w, h, z, lo=0, hi=None):
    return jnp.concatenate(
        [w[r % 2][r // 2, w[2](h), : z.rd, lo:hi] for r in range(z.dp)], axis=0
    )


def layout_w(w, h, z, lo=0, hi=None):
    width = w[0].shape[-1] // GROUPS
    hi = width if hi is None else hi
    pieces = []
    for r in range(z.dp):
        for k in range(GROUPS):
            rows = slice(z.rd, z.rd + z.part)
            pieces.append(w[r % 2][r // 2, w[2](h), rows, width * k + lo : width * k + hi])
    return jnp.concatenate(pieces, axis=0)


def alone(h):
    return h


def first_of_two(h):
    return 2 * h


def second_of_two(h):
    return 2 * h + 1


def feed_forward(refs):
    if len(refs) == 4:
        return (refs[0], refs[1], alone), (refs[2], refs[3], alone)
    return (refs[0], refs[1], first_of_two), (refs[0], refs[1], second_of_two)


def put_grads(g, h, text, layout, z):
    width = g[0].shape[-1] // GROUPS
    low = layout.astype(BF)
    pad = width - low.shape[-1]
    low = jnp.concatenate([low, jnp.zeros((low.shape[0], pad), BF)], axis=1)
    text = text.astype(BF)
    at = g[2](h)
    for r in range(z.dp):
        ref, x = g[r % 2], r // 2
        ref[x, at, : z.rd, :] = text[z.rd * r : z.rd * (r + 1)]
        for k in range(GROUPS):
            base = z.lr * r + z.part * k
            ref[x, at, z.rd : z.block, width * k : width * (k + 1)] = low[base : base + z.part]


def natural(pieces, m, z):
    out = []
    for d in range(z.dp):
        value = pieces[d]
        for other in range(1, z.masks):
            value = jnp.where(m == other, pieces[d ^ other], value)
        out.append(value)
    return jnp.concatenate(out, axis=1)


def norm_stats(resid):
    center = resid - jnp.mean(resid, axis=-1, keepdims=True)
    factor = lax.rsqrt(jnp.mean(center * center, axis=-1, keepdims=True) + 1e-05)
    return center * factor, factor


def norm_both(resid, z):
    nt, ft = norm_stats(resid[:, : z.d])
    nl, fl = norm_stats(resid[:, z.d :])
    return jnp.concatenate([nt, nl], axis=1), ft, fl


def norm_back(grad, normed, factor, gain):
    scaled = grad * gain
    return factor * (
        scaled
        - jnp.mean(scaled, axis=-1, keepdims=True)
        - normed * jnp.mean(scaled * normed, axis=-1, keepdims=True)
    )


def norm_back_both(grad, normed, ft, fl, gain, z):
    gt = norm_back(grad[:, : z.d], normed[:, : z.d], ft, gain[:, : z.d])
    gl = norm_back(grad[:, z.d :], normed[:, z.d :], fl, gain[:, z.d :])
    return jnp.concatenate([gt, gl], axis=1)


def small_rows(w, h, z):
    return [w[r % 2][r // 2, h, z.block : z.vblock, :].astype(F32) for r in range(z.dp)]


def qkv_body(z, fused, meta_ref, *refs):
    if fused:
        (hid_ref, own_ref, rec_ref, prev_ref, ws_ref, wc_ref,
         r_ref, x_ref, q_ref, kv_ref, vec_ref, ut_ref, ul_ref) = refs
        vec = prev_ref[...]
        resid = (
            hid_ref[...].astype(F32) + own_ref[...].astype(F32) + rec_ref[...].astype(F32) + vec[4:5]
        )
        r_ref[...] = resid
        normed, _, _ = norm_both(resid, z)
        x = (normed * vec[1:2] + vec[5:6]).astype(BF)
        x_ref[...] = x
    else:
        x_ref, far_ref, ws_ref, wc_ref, q_ref, kv_ref, kvr_ref, vec_ref, ut_ref, ul_ref = refs
        x = x_ref[...]
    w = (ws_ref, wc_ref, alone)
    mask = meta_ref[1]
    lane = 4 * SLOT
    small = small_rows(w, 0, z)
    vec_ref[:, : z.d] = jnp.concatenate([s[:, : z.rd] for s in small], axis=1)
    vec_ref[:, z.d :] = jnp.concatenate([s[:, lane : lane + z.lr] for s in small], axis=1)
    xt, xl = x[:, : z.d], x[:, z.d :]
    n, m = z.quarter, z.lquarter
    zeros = jnp.zeros((z.rows, SLOT - HEAD - LHEAD), BF)
    hb, lb, ub, vb = n // z.dp, m // z.dp, 4 * n // z.dp, 4 * m // z.dp

    def project(xt, xl, first, out_ref):
        yt = mm(xt, text_w(w, h, z, n * first, 3 * n)) + bt[:, n * first :]
        yl = mm(xl, layout_w(w, h, z, m * first, 3 * m)) + bl[:, m * first :]
        yt = yt.astype(BF)
        yl = yl.astype(BF)
        for s in range(first, 3):
            for j in range(z.heads):
                lo, llo = n * (s - first) + HEAD * j, m * (s - first) + LHEAD * j
                a = yt[:, lo : lo + HEAD]
                b = yl[:, llo : llo + LHEAD]
                if s == 0:
                    a = a * BF(HEAD**-0.5)
                    b = b * BF(LHEAD**-0.5)
                slot = jnp.concatenate([a, b, zeros], axis=1)
                head = z.heads * h + j
                if s == 0:
                    q_ref[head] = slot
                else:
                    out_ref[2 * z.heads * (s - 1) + head] = slot

    for h in range(2):
        small = small_rows(w, h, z)
        rows = lambda i, lo, size: natural([s[i : i + 1, lo : lo + size] for s in small], mask, z)
        ut_ref[h] = rows(8, 0, ub)
        ul_ref[h] = rows(8, lane, vb)
        bt = jnp.concatenate([rows(6, 0, hb), jnp.zeros((1, n), F32), rows(7, 0, hb)], axis=1)
        bl = jnp.concatenate(
            [rows(6, lane, lb), jnp.zeros((1, m), F32), rows(7, lane, lb)], axis=1
        )
        project(xt, xl, 0, kv_ref)
        if not fused:
            far = far_ref[...]
            project(far[:, : z.d], far[:, z.d :], 1, kvr_ref)


def attend_body(z, q_ref, own_ref, rec_ref, mask_ref, ws_ref, wc_ref, a_ref, c_ref, p_ref, s_ref):
    w = (ws_ref, wc_ref, alone)
    count = 2 * z.heads
    m0 = mask_ref[0:1, : z.rows] > 0
    m1 = mask_ref[0:1, z.rows :] > 0

    def head(j, carry):
        q = q_ref[j]
        s0 = jnp.where(m0, mm_nt(q, own_ref[j]), -1000000000.0)
        s1 = jnp.where(m1, mm_nt(q, rec_ref[j]), -1000000000.0)
        top = jnp.maximum(
            jnp.max(s0, axis=-1, keepdims=True), jnp.max(s1, axis=-1, keepdims=True)
        )
        e0 = jnp.exp(s0 - top)
        e1 = jnp.exp(s1 - top)
        inv = 1.0 / (jnp.sum(e0, axis=-1, keepdims=True) + jnp.sum(e1, axis=-1, keepdims=True))
        p0 = (e0 * inv).astype(BF)
        p1 = (e1 * inv).astype(BF)
        p_ref[j, :, : z.rows] = p0
        p_ref[j, :, z.rows :] = p1
        s_ref[j] = (mm(p0, own_ref[count + j]) + mm(p1, rec_ref[count + j])).astype(BF)
        return carry

    lax.fori_loop(0, count, head, 0)
    n, m = z.quarter, z.lquarter
    at = al = None
    for h in range(2):
        heads = [s_ref[z.heads * h + j] for j in range(z.heads)]
        ct = jnp.concatenate([s[:, :HEAD] for s in heads], axis=1)
        cl = jnp.concatenate([s[:, HEAD : HEAD + LHEAD] for s in heads], axis=1)
        c_ref[h, :, :n] = ct
        c_ref[h, :, 2 * SLOT : 2 * SLOT + m] = cl
        pt = mm_nt(ct, text_w(w, h, z, 3 * n, 4 * n))
        pll = mm_nt(cl, layout_w(w, h, z, 3 * m, 4 * m))
        at = pt if at is None else at + pt
        al = pll if al is None else al + pll
    a_ref[:, : z.d] = at.astype(BF)
    a_ref[:, z.d :] = al.astype(BF)


def gelu_parts(u):
    cdf = 0.5 * (1.0 + lax.erf(u * 0.7071067811865476))
    slope = cdf + u * jnp.exp(-0.5 * u * u) * 0.3989422804014327
    return (u * cdf).astype(BF), slope.astype(BF)


def forward_body(
    z, x_ref, own_ref, rec_ref, vec_ref, bt_ref, bl_ref, *refs
):
    r_ref, hid_ref, gt_ref, gl_ref, st_ref, sl_ref, f_ref = refs[-7:]
    up, down = feed_forward(refs[:-7])
    lw = 4 * z.lquarter
    vec = vec_ref[...]
    resid = x_ref[...].astype(F32) + own_ref[...].astype(F32) + rec_ref[...].astype(F32) + vec[2:3]
    r_ref[...] = resid
    normed, _, _ = norm_both(resid, z)
    hid = (normed * vec[0:1] + vec[3:4]).astype(BF)
    hid_ref[...] = hid
    ht, hl = hid[:, : z.d], hid[:, z.d :]
    ft = fl = None
    for h in range(2):
        g, s = gelu_parts(mm(ht, text_w(up, h, z)) + bt_ref[h])
        gt_ref[h] = g
        st_ref[h] = s
        p = mm_nt(g, text_w(down, h, z))
        ft = p if ft is None else ft + p
        g, s = gelu_parts(mm(hl, layout_w(up, h, z, 0, lw)) + bl_ref[h])
        gl_ref[h] = g
        sl_ref[h] = s
        p = mm_nt(g, layout_w(down, h, z, 0, lw))
        fl = p if fl is None else fl + p
    f_ref[:, : z.d] = ft.astype(BF)
    f_ref[:, z.d :] = fl.astype(BF)


def col_sum(value):
    return jnp.sum(value, axis=0, keepdims=True)


def tail_body(z, fused, *refs):
    if fused == "last":
        hid_ref, own_ref, rec_ref, go_ref, vec_ref, st_ref, sl_ref = refs[:7]
        ws = refs[7:-9]
        out_ref, d2_ref, df_ref, dut_ref, dul_ref, dh_ref, vg_ref, gbt_ref, gbl_ref = refs[-9:]
        vec = vec_ref[...]
        resid = (
            hid_ref[...].astype(F32) + own_ref[...].astype(F32) + rec_ref[...].astype(F32) + vec[4:5]
        )
        normed, ft, fl = norm_both(resid, z)
        out_ref[...] = (normed * vec[1:2] + vec[5:6]).astype(BF)
        go = go_ref[...].astype(F32)
    else:
        r_ref, d1_ref, own_ref, rec_ref, vec_ref, st_ref, sl_ref = refs[:7]
        ws = refs[7:-9]
        dx_ref, d2_ref, df_ref, dut_ref, dul_ref, dh_ref, vg_ref, gbt_ref, gbl_ref = refs[-9:]
        vec = vec_ref[...]
        normed, ft, fl = norm_both(r_ref[...], z)
        low = (d1_ref[...] + own_ref[...].astype(F32) + rec_ref[...].astype(F32)).astype(BF)
        dx_ref[...] = low
        go = low.astype(F32)
    up, down = feed_forward(ws)
    lw = 4 * z.lquarter
    d2 = norm_back_both(go, normed, ft, fl, vec[1:2], z)
    d2_ref[...] = d2
    df = d2.astype(BF)
    df_ref[...] = df
    vg_ref[0:1] = col_sum(go * normed)
    vg_ref[1:2] = col_sum(go)
    vg_ref[2:3] = col_sum(df.astype(F32))
    vg_ref[3:8] = jnp.zeros((5, z.width), F32)
    dft, dfl = df[:, : z.d], df[:, z.d :]
    ht = hl = None
    for h in range(2):
        du = (mm(dft, text_w(down, h, z)) * st_ref[h].astype(F32)).astype(BF)
        dut_ref[h] = du
        gbt_ref[h] = col_sum(du.astype(F32))
        p = mm_nt(du, text_w(up, h, z))
        ht = p if ht is None else ht + p
        du = (mm(dfl, layout_w(down, h, z, 0, lw)) * sl_ref[h].astype(F32)).astype(BF)
        dul_ref[h] = du
        gbl_ref[h] = col_sum(du.astype(F32))
        p = mm_nt(du, layout_w(up, h, z, 0, lw))
        hl = p if hl is None else hl + p
    dh_ref[:, : z.d] = ht.astype(BF)
    dh_ref[:, z.d :] = hl.astype(BF)


def ffn_grads_body(z, hid_ref, df_ref, gt_ref, gl_ref, dut_ref, dul_ref, g_ref, h_ref):
    one, two = (g_ref, h_ref, first_of_two), (g_ref, h_ref, second_of_two)
    hid, df = hid_ref[...], df_ref[...]
    for h in range(2):
        put_grads(one, h, mm_tn(hid[:, : z.d], dut_ref[h]), mm_tn(hid[:, z.d :], dul_ref[h]), z)
        put_grads(two, h, mm_tn(df[:, : z.d], gt_ref[h]), mm_tn(df[:, z.d :], gl_ref[h]), z)


def attend_back_body(
    z, d2_ref, own_ref, rec_ref, r_ref, vec_ref, ws_ref, wc_ref, c_ref, q_ref, kv_ref, kvr_ref, p_ref, mask_ref,
    d1_ref, da_ref, dq_ref, dkv_ref, dkvr_ref, vg_ref, dc_ref, dd_ref,
):
    count = 2 * z.heads
    w = (ws_ref, wc_ref, alone)
    vec = vec_ref[...]
    dh = d2_ref[...] + own_ref[...].astype(F32) + rec_ref[...].astype(F32)
    normed, ft, fl = norm_both(r_ref[...], z)
    d1 = norm_back_both(dh, normed, ft, fl, vec[0:1], z)
    d1_ref[...] = d1
    da = d1.astype(BF)
    da_ref[...] = da
    vg_ref[0:1] = col_sum(dh * normed)
    vg_ref[1:2] = col_sum(dh)
    vg_ref[2:3] = col_sum(da.astype(F32))
    vg_ref[3:8] = jnp.zeros((5, z.width), F32)
    n, m = z.quarter, z.lquarter
    zeros = jnp.zeros((z.rows, SLOT - HEAD - LHEAD), BF)
    for h in range(2):
        dct = mm(da[:, : z.d], text_w(w, h, z, 3 * n, 4 * n)).astype(BF)
        dcl = mm(da[:, z.d :], layout_w(w, h, z, 3 * m, 4 * m)).astype(BF)
        for j in range(z.heads):
            a = dct[:, HEAD * j : HEAD * (j + 1)]
            b = dcl[:, LHEAD * j : LHEAD * (j + 1)]
            dc_ref[z.heads * h + j] = jnp.concatenate([a, b, zeros], axis=1)
            ct = c_ref[h, :, HEAD * j : HEAD * (j + 1)].astype(F32)
            cl = c_ref[h, :, 2 * SLOT + LHEAD * j : 2 * SLOT + LHEAD * (j + 1)].astype(F32)
            dt = jnp.sum(a.astype(F32) * ct, axis=-1, keepdims=True)
            dl = jnp.sum(b.astype(F32) * cl, axis=-1, keepdims=True)
            dd_ref[z.heads * h + j, :, 0:1] = dt
            dd_ref[z.heads * h + j, :, 1:2] = dt + dl
    lane = lax.broadcasted_iota(jnp.int32, (z.rows, SLOT), 1)
    text_lane = lane < HEAD
    scale = jnp.where(text_lane, HEAD**-0.5, LHEAD**-0.5)
    mask = mask_ref[...]
    masks = (mask[:, : z.rows], mask[:, z.rows :])

    def head(j, carry):
        dc = dc_ref[j]
        dct = jnp.where(text_lane, dc, jnp.zeros_like(dc))
        q = q_ref[j]
        dt = dd_ref[j, :, 0:1]
        ds = dd_ref[j, :, 1:2]
        dq_t = dq_s = None
        for i, (k_ref, o_ref) in enumerate(((kv_ref, dkv_ref), (kvr_ref, dkvr_ref))):
            k = k_ref[j]
            v = k_ref[count + j]
            prob = p_ref[j, :, z.rows * i : z.rows * (i + 1)]
            pm = jnp.where(masks[i] > 0, prob.astype(F32), 0.0)
            st = (pm * (mm_nt(dct, v) - dt)).astype(BF)
            ss = (pm * (mm_nt(dc, v) - ds)).astype(BF)
            a = mm(st, k)
            b = mm(ss, k)
            dq_t = a if dq_t is None else dq_t + a
            dq_s = b if dq_s is None else dq_s + b
            dk = jnp.where(text_lane, mm_tn(st, q), mm_tn(ss, q))
            o_ref[j] = dk.astype(BF)
            o_ref[count + j] = mm_tn(prob, dc).astype(BF)
        dq_ref[j] = (jnp.where(text_lane, dq_t, dq_s) * scale).astype(BF)
        return carry

    lax.fori_loop(0, count, head, 0)


def input_back_body(z, dq_ref, dkv_ref, rec_ref, ws_ref, wc_ref, yt_ref, yl_ref, dx_ref, gbt_ref, gbl_ref):
    count = 2 * z.heads
    w = (ws_ref, wc_ref, alone)
    n, m = z.quarter, z.lquarter
    xt = xl = None
    for h in range(2):
        ts, ls = [], []
        for s in range(3):
            for j in range(z.heads):
                head = z.heads * h + j
                if s == 0:
                    slot = dq_ref[head]
                else:
                    at = count * (s - 1) + head
                    slot = (dkv_ref[at].astype(F32) + rec_ref[at].astype(F32)).astype(BF)
                ts.append(slot[:, :HEAD])
                ls.append(slot[:, HEAD : HEAD + LHEAD])
        yt = jnp.concatenate(ts, axis=1)
        yl = jnp.concatenate(ls, axis=1)
        yt_ref[h] = yt
        yl_ref[h] = yl
        gbt_ref[h] = col_sum(yt.astype(F32))
        gbl_ref[h] = col_sum(yl.astype(F32))
        p = mm_nt(yt, text_w(w, h, z, 0, 3 * n))
        xt = p if xt is None else xt + p
        p = mm_nt(yl, layout_w(w, h, z, 0, 3 * m))
        xl = p if xl is None else xl + p
    dx_ref[:, : z.d] = xt.astype(BF)
    dx_ref[:, z.d :] = xl.astype(BF)


def input_grads_body(
    z, meta_ref, x_ref, da_ref, c_ref, yt_ref, yl_ref, va_ref, vb_ref, bt_ref, bl_ref, ut_ref, ul_ref,
    g_ref, h_ref, s_ref,
):
    g = (g_ref, h_ref, alone)
    x, da = x_ref[...], da_ref[...]
    n, m = z.quarter, z.lquarter
    va, vb = va_ref[...], vb_ref[...]
    mask = meta_ref[1]
    rows = (vb[0:1], va[0:1], vb[2:3], vb[1:2], va[2:3], va[1:2])
    lane = 4 * SLOT
    s_ref[...] = jnp.zeros_like(s_ref)

    def relative(value, size):
        parts = [value[:, size * d : size * (d + 1)] for d in range(z.dp)]
        out = []
        for r in range(z.dp):
            v = parts[r]
            for other in range(1, z.masks):
                v = jnp.where(mask == other, parts[r ^ other], v)
            out.append(v)
        return out

    for h in range(2):
        ct = c_ref[h, :, :n]
        cl = c_ref[h, :, 2 * SLOT : 2 * SLOT + m]
        text = jnp.concatenate(
            [mm_tn(x[:, : z.d], yt_ref[h]), mm_tn(da[:, : z.d], ct)], axis=1
        )
        layout = jnp.concatenate(
            [mm_tn(x[:, z.d :], yl_ref[h]), mm_tn(da[:, z.d :], cl)], axis=1
        )
        put_grads(g, h, text, layout, z)
        bt, bl, ut, ul = bt_ref[h], bl_ref[h], ut_ref[h], ul_ref[h]
        entries = [
            (6, 0, relative(bt[:, :n], n // z.dp)),
            (7, 0, relative(bt[:, 2 * n :], n // z.dp)),
            (6, lane, relative(bl[:, :m], m // z.dp)),
            (7, lane, relative(bl[:, 2 * m :], m // z.dp)),
            (8, 0, relative(ut, 4 * n // z.dp)),
            (8, lane, relative(ul, 4 * m // z.dp)),
        ]
        for r in range(z.dp):
            for i, row in enumerate(rows):
                s_ref[i : i + 1, : z.rd] = row[:, z.rd * r : z.rd * (r + 1)]
                s_ref[i : i + 1, lane : lane + z.lr] = row[
                    :, z.d + z.lr * r : z.d + z.lr * (r + 1)
                ]
            for at, lo, values in entries:
                s_ref[at : at + 1, lo : lo + values[r].shape[1]] = values[r]
            g[r % 2][r // 2, h, z.block : z.vblock, :] = s_ref[...].astype(BF)


def put_pack(out_ref, text, layout, z):
    out_ref[: z.rd, :] = text.astype(BF)
    width = out_ref.shape[-1] // GROUPS
    low = layout.astype(BF)
    low = jnp.concatenate([low, jnp.zeros((low.shape[0], width - low.shape[1]), BF)], axis=1)
    for k in range(GROUPS):
        out_ref[z.rd : z.block, width * k : width * (k + 1)] = low[z.part * k : z.part * (k + 1)]


def pack_first_body(
    z, ti_ref, to_ref, li_ref, lo_ref, tg_ref, lg_ref, ts_ref, ls_ref, tb_ref, lb_ref, tu_ref, lu_ref,
    out_ref, s_ref,
):
    text = jnp.concatenate([ti_ref[0, 0], ti_ref[0, 1], ti_ref[0, 2], to_ref[0].T], axis=1)
    layout = jnp.concatenate([li_ref[0, 0], li_ref[0, 1], li_ref[0, 2], lo_ref[0].T], axis=1)
    put_pack(out_ref, text, layout, z)
    s_ref[...] = jnp.zeros_like(s_ref)
    for lane, refs in ((0, (tg_ref, ts_ref, tb_ref)), (4 * SLOT, (lg_ref, ls_ref, lb_ref))):
        at = 0
        for ref in refs:
            count, width = ref.shape[1], ref.shape[2]
            s_ref[at : at + count, lane : lane + width] = ref[0]
            at += count
    s_ref[8:9, : tu_ref.shape[1]] = tu_ref[...]
    s_ref[8:9, 4 * SLOT : 4 * SLOT + lu_ref.shape[1]] = lu_ref[...]
    out_ref[z.block : z.vblock, :] = s_ref[...].astype(BF)


def pack_rest_body(z, tu_ref, lu_ref, td_ref, ld_ref, out_ref):
    put_pack(out_ref.at[0], tu_ref[0], lu_ref[0], z)
    put_pack(out_ref.at[1], td_ref[0], ld_ref[0], z)


def take_layout(total, cols, z):
    width = total.shape[-1] // GROUPS
    return jnp.concatenate(
        [total[z.rd : z.block, width * k : width * k + cols] for k in range(GROUPS)], axis=0
    )


def final_sum(refs):
    return sum(r[...].astype(F32) for r in refs)


def finish_first_body(z, *refs):
    (ti_ref, tb_ref, to_ref, tg_ref, ts_ref, tu_ref,
     li_ref, lb_ref, lo_ref, lg_ref, ls_ref, lu_ref) = refs[2:]
    total = final_sum(refs[:2])[0]
    n, m = z.quarter, z.lquarter
    layout = take_layout(total, 4 * m, z)
    for s in range(3):
        ti_ref[0, s] = total[: z.rd, n * s : n * (s + 1)]
        li_ref[0, s] = layout[:, m * s : m * (s + 1)]
    to_ref[0] = total[: z.rd, 3 * n :].T
    lo_ref[0] = layout[:, 3 * m :].T
    rows = total[z.block : z.vblock]
    for lane, group in ((0, (tg_ref, ts_ref, tb_ref)), (4 * SLOT, (lg_ref, ls_ref, lb_ref))):
        at = 0
        for ref in group:
            count, width = ref.shape[1], ref.shape[2]
            ref[0] = rows[at : at + count, lane : lane + width]
            at += count
    tu_ref[...] = rows[8:9, : tu_ref.shape[1]]
    lu_ref[...] = rows[8:9, 4 * SLOT : 4 * SLOT + lu_ref.shape[1]]


def finish_body(z, *refs):
    total = final_sum(refs[:2])
    for p in range(2):
        t_ref, l_ref = refs[2 + 2 * p : 4 + 2 * p]
        t_ref[0] = total[p, : z.rd]
        l_ref[0] = take_layout(total[p], 4 * z.lquarter, z)


def entry_body(z, meta_ref, t_ref, l_ref, tc_ref, lc_ref, mask_ref, own_ref, send_ref):
    y, c = meta_ref[0], meta_ref[2]
    row = jnp.where(y == 0, mask_ref[0:1, :], mask_ref[1:2, :]).astype(F32)
    left, right = row[:, : z.rows], row[:, z.rows :]
    for ref, half in ((own_ref, c), (send_ref, 1 - c)):
        for i, (text, layout) in enumerate(((t_ref, l_ref), (t_ref, l_ref), (tc_ref, lc_ref))):
            part = 1 - half if i == 1 else half
            rows = pl.ds(pl.multiple_of(part * z.rows, z.rows), z.rows)
            out = slice(z.rows * i, z.rows * (i + 1))
            ref[out, : z.d] = text[y, rows, :]
            ref[out, z.d :] = layout[y, :, rows].astype(F32).T.astype(BF)
        near = jnp.where(half == 0, left, right)
        far = jnp.where(half == 0, right, left)
        low = jnp.concatenate([near, far, jnp.zeros((1, z.width - z.seq), F32)], axis=1)
        ref[3 * z.rows :, :] = jnp.broadcast_to(low, (16, z.width)).astype(BF)


def ordered(value, m, z):
    text = [value[:, z.rd * r : z.rd * (r + 1)] for r in range(z.dp)]
    layout = [value[:, z.d + z.lr * r : z.d + z.lr * (r + 1)] for r in range(z.dp)]
    return jnp.concatenate([natural(text, m, z), natural(layout, m, z)], axis=1)


def settle_body(z, meta_ref, own_ref, got_ref, x_ref, far_ref, cot_ref, out_ref):
    mine = meta_ref[3] == 1
    mask = meta_ref[1]
    for i, ref in enumerate((x_ref, far_ref, cot_ref)):
        rows = slice(z.rows * i, z.rows * (i + 1))
        ref[...] = ordered(jnp.where(mine, own_ref[rows, :], got_ref[rows, :]), mask, z)
    last = slice(3 * z.rows, 3 * z.rows + 16)
    row = jnp.where(mine, own_ref[last, : z.seq], got_ref[last, : z.seq])
    out_ref[...] = row.astype(F32)[0:1]


def exit_body(z, summed, meta_ref, *refs):
    if summed:
        d_ref, own_ref, rec_ref, b_ref, here_ref, part_ref, send_ref, far_ref = refs
        one = (d_ref[...] + own_ref[...].astype(F32) + rec_ref[...].astype(F32)).astype(BF)
    else:
        a_ref, b_ref, here_ref, part_ref, send_ref, far_ref = refs
        one = a_ref[...]
    first = meta_ref[0] == 0
    low = meta_ref[4] == 0
    mask = meta_ref[1]
    two = b_ref[...]
    half = z.rows // 2
    here = ordered(jnp.where(first, one, two), mask, z)
    here_ref[...] = here
    part_ref[...] = jnp.where(low, here[:half], here[half:])
    there = ordered(jnp.where(first, two, one), mask, z)
    send_ref[...] = there
    far_ref[...] = jnp.where(low, there[:half], there[half:])


def sort_body(z, meta_ref, here_ref, got_ref, b_ref, d_ref, far_ref, keep_ref, send_ref):
    mine = meta_ref[3] == 1
    low = meta_ref[4] == 0
    half = z.rows // 2
    for i, (same_ref, near_ref) in enumerate(((here_ref, b_ref), (got_ref, d_ref))):
        beyond = far_ref[half * i : half * (i + 1), :]
        for k in range(2):
            rows = slice(half * k, half * (k + 1))
            other = jnp.where(low == (k == 0), near_ref[...], beyond)
            same = same_ref[rows, :]
            rows = slice(z.rows * i + half * k, z.rows * i + half * (k + 1))
            keep_ref[rows, :] = jnp.where(mine, same, other)
            send_ref[rows, :] = jnp.where(mine, other, same)
    send_ref[2 * z.rows :, :] = jnp.zeros((16, z.width), BF)


def place_body(z, meta_ref, keep_ref, got_ref, t_ref, l_ref):
    y, c = meta_ref[0], meta_ref[2]
    for i in range(2):
        page = y if i == 0 else 1 - y
        for ref, half in ((keep_ref, c), (got_ref, 1 - c)):
            rows = pl.ds(pl.multiple_of(half * z.rows, z.rows), z.rows)
            value = ref[z.rows * i : z.rows * (i + 1), :]
            t_ref[0, page, rows, :] = value[:, : z.d]
            l_ref[0, page, :, rows] = value[:, z.d :].astype(F32).T.astype(BF)


def swap(value, axis):
    return lax.ppermute(value, axis, [(0, 1), (1, 0)])


def after(value, *others):
    return lax.optimization_barrier((value,) + others)[0]


def swap_both(value):
    return lax.ppermute(value, ("y", "h"), [(0, 3), (1, 2), (2, 1), (3, 0)])


def join_rows(*parts):
    return jnp.concatenate(parts + (jnp.zeros((16, parts[0].shape[1]), BF),), axis=0)


def join_blocks(parts, got):
    own = jnp.stack([jnp.concatenate(parts), jnp.concatenate(got)])
    return own, swap(own, "c")


def gather_blocks(parts, x_size, *token):
    if x_size == 2:
        return join_blocks(parts, [after(swap(v, "x"), *token) for v in parts])
    else:
        own = lax.all_gather(jnp.concatenate(parts), "x", axis=0)
    return own, swap(own, "c")


def add_low(*terms):
    total = terms[0].astype(F32)
    for term in terms[1:]:
        total = total + term.astype(F32)
    return total.astype(BF)


class Reduce:
    def __init__(self, keep, send, x_size, *token):
        self.keep, self.x_size = keep, x_size
        half = keep.shape[1] // 2
        self.rows = (slice(half, None), slice(0, half), slice(None))
        self.got = swap(after(send, *token) if token else send, "c")
        self.far = {}

    def x_step(self, part, *token):
        got, rows = after(self.got, *token), self.rows[part]
        if self.x_size == 2:
            total = add_low(self.keep[1, rows], got[1, rows])
            self.far[part] = swap(total, "x")
        else:
            total = add_low(self.keep[:, rows], got[:, rows])
            self.far[part] = lax.psum_scatter(total, "x", scatter_dimension=0, tiled=False)
        return total

    def near(self, part, *token):
        rows = self.rows[part]
        if part in self.far:
            far = after(self.far[part], *token)
        else:
            far = after(self.far[2], *token)[rows]
        if self.x_size == 2:
            far = add_low(self.keep[0, rows], self.got[0, rows], far)
        return far


class Finish:
    def __init__(self, y):
        self.y, self.here, self.cross = y, {}, {}

    def y_step(self, part, first, second):
        self.here[part] = jnp.where(self.y == 0, first, second)
        self.cross[part] = swap(jnp.where(self.y == 0, second, first), "y")
        return self.here[part]

    def sum_of(self, part, *token):
        if part in self.here:
            return add_low(self.here[part], after(self.cross[part], *token))
        half = self.here[2].shape[0] // 2
        rows = slice(half, None) if part == 0 else slice(0, half)
        return add_low(self.here[2][rows], after(self.cross[2], *token)[rows])

    def h_step(self, *token):
        other = self.sum_of(0, *token)
        self.last = swap(other, "h")
        return other

    def close(self, *token):
        self.own = self.sum_of(1, *token)
        return self.own

    def terms(self, *token):
        return (self.own, after(self.last, *token))


def per_device(
    text_in, layout_in, token_mask, text_cotangent, layout_cotangent,
    t_in, t_hb, t_out, t_gain, t_shift, t_up, t_ub, t_down,
    l_in, l_hb, l_out, l_gain, l_shift, l_up, l_ub, l_down,
):
    x_size = lax.axis_size("x")
    y, x, c, h, l = (lax.axis_index(a) for a in ALL)
    z = Sizes(
        text_in, layout_in, t_in.shape[2], l_in.shape[2], t_in.shape[3], l_in.shape[3], 2 * x_size
    )
    order = 2 * x + c if x_size == 2 else c
    meta = jnp.stack([y, order, c, (c == h).astype(jnp.int32), l, 0 * y, 0 * y, 0 * y])
    bind = functools.partial
    cols = t_up.shape[2]

    R, W, Q, M = z.rows, z.width, 4 * z.quarter, 4 * z.lquarter
    nh = 2 * z.heads
    flip = lambda v: jnp.swapaxes(v, -1, -2)

    (first,) = call(
        bind(pack_first_body, z), [sds((z.vblock, cols), BF)],
        t_in, t_out, l_in, l_out, t_gain, l_gain, t_shift, l_shift, t_hb, l_hb, t_ub, l_ub,
        scratch=[pltpu.VMEM((16, cols), F32)],
    )
    (rest,) = call(
        bind(pack_rest_body, z), [sds((2, z.block, cols), BF)],
        after(t_up, first), l_up, flip(t_down), flip(l_down), us=10,
    )
    own, send = call(
        bind(entry_body, z), [sds((3 * R + 16, W), BF)] * 2,
        after(text_in, rest), flip(layout_in), text_cotangent, flip(layout_cotangent), token_mask,
        meta=meta, us=10,
    )
    first = first[None]

    first_h, rest_h = swap(first, "h"), swap(rest, "h")
    first_y = after(swap(first, "y"), rest, own)
    pick = lambda index, mine, across: jnp.where(y == index, mine, across)
    a0 = pick(0, first, first_y)
    got = after(swap(send, "c"), a0)
    x0, far0, cot, mask = call(
        bind(settle_body, z), [sds((R, W), BF)] * 3 + [sds((1, z.seq), F32)], own, got, meta=meta, us=10,
    )
    first_h = after(first_h, x0)
    rest_y = after(swap(rest, "y"), first_h)
    f0 = pick(0, rest, rest_y)
    first_hy = swap(first_h, "y")
    rest_h = after(rest_h, first_h, f0)
    a1 = pick(0, first_h, after(first_hy, rest_h))
    parts_hy = [swap(rest_h[p : p + 1], "y") for p in range(2)]
    if x_size == 2:
        far_a = [swap(a0, "x"), swap(a1, "x")]
        far_f0 = swap(f0, "x")
        far_a[0] = after(far_a[0], far_a[1], far_f0, *parts_hy)
        weights = [[join_blocks([a0, a1], far_a)], []]
    else:
        weights = [[gather_blocks([a0, a1], x_size)], []]
    tokens = weights[0][0][0]
    f1 = pick(0, rest_h[0:1], after(parts_hy[0], tokens))
    f2 = pick(0, rest_h[1:2], after(parts_hy[1], tokens))
    x0 = after(x0, f1, f2)

    q_shapes = [sds((nh, R, SLOT), BF), sds((2 * nh, R, SLOT), BF)]
    v_shapes = [sds((16, W), F32), sds((2, 1, Q), F32), sds((2, 1, M), F32)]
    saved = []
    inner = None
    for index in range(2):
        w0 = weights[index][0]
        if index == 0:
            q, kv, kvr, vec, ut, ul = call(
                bind(qkv_body, z, False), q_shapes + q_shapes[1:] + v_shapes, x0, far0, *w0, meta=meta
            )
            xin = x0
        else:
            r2, xin, q, kv, vec, ut, ul = call(
                bind(qkv_body, z, True),
                [sds((R, W), F32), sds((R, W), BF)] + q_shapes + v_shapes,
                *inner, saved[0]["vec"], *w0, meta=meta,
            )
            saved[0]["r2"] = r2
            kvr = swap(kv, "c")
        a, ctx, prob = call(
            bind(attend_body, z),
            [sds((R, W), BF), sds((2, R, 3 * SLOT), BF), sds((nh, R, z.seq), BF)],
            q, kv, kvr, mask, *w0, scratch=[pltpu.VMEM((nh, R, SLOT), BF)], us=8,
        )
        ar = swap(a, "l")
        if index == 0:
            if x_size == 2:
                got = [after(swap(v, "x"), a) for v in (f1, f2)]
                weights[0].append(join_blocks([f0, f1, f2], [far_f0] + got))
            else:
                weights[0].append(gather_blocks([f0, f1, f2], x_size))
            token = weights[0][1][0]
            second = jnp.concatenate([pick(1, first, first_y), pick(1, after(first_h, token), first_hy)])
            got = swap(second, "x") if x_size == 2 else None
            if x_size == 2:
                ar = after(ar, got)
                weights[1].append(join_blocks([second], [got]))
            else:
                weights[1].append(gather_blocks([second], x_size))
            halves = [
                pick(1, after(rest, token), rest_y),
                jnp.concatenate(
                    [pick(1, after(rest_h, token)[p : p + 1], parts_hy[p]) for p in range(2)]
                ),
            ]
        if index == 1:
            if x_size == 2:
                far1 = after(swap(halves[1], "x"), a)
                weights[1].append(join_blocks(halves, [far_half, far1]))
            else:
                weights[1].append(gather_blocks(halves, x_size))
        r1, hid, gt, gl, st, sl, f = call(
            bind(forward_body, z),
            [sds((R, W), F32), sds((R, W), BF), sds((2, R, Q), BF), sds((2, R, M), BF),
             sds((2, R, Q), BF), sds((2, R, M), BF), sds((R, W), BF)],
            xin, a, ar, vec, ut, ul, *weights[index][1], us=6,
        )
        fr = swap(f, "l")
        if index == 0 and x_size == 2:
            far_half = swap(after(halves[0], ar), "x")
            fr = after(fr, far_half)
        inner = (hid, f, fr)
        saved.append(dict(x=xin, q=q, kv=kv, kvr=kvr, ctx=ctx, prob=prob, r1=r1, hid=hid, gt=gt,
                          gl=gl, st=st, sl=sl, vec=vec))

    gshape = sds((x_size, 4, z.block, cols), BF)
    vshape = sds((x_size, 2, z.vblock, cols), BF)

    def tail(index, *args):
        keep = saved[index]
        shapes = [sds((R, W), BF), sds((R, W), F32), sds((R, W), BF), sds((2, R, Q), BF),
                  sds((2, R, M), BF), sds((R, W), BF), sds((8, W), F32), sds((2, 1, Q), F32),
                  sds((2, 1, M), F32)]
        return call(
            bind(tail_body, z, "last" if index == 1 else "mid"), shapes,
            *args, keep["vec"], keep["st"], keep["sl"], *weights[index][1], us=7,
        )

    def ffn_grads(index, df, dut, dul, *token):
        keep = saved[index]
        g, s = call(
            bind(ffn_grads_body, z), [gshape] * 2,
            keep["hid"], df, keep["gt"], keep["gl"], dut, dul, us=6,
        )
        return Reduce(g, s, x_size, *token)

    def attend_back(index, d2, dh, dhr):
        keep = saved[index]
        return call(
            bind(attend_back_body, z),
            [sds((R, W), F32), sds((R, W), BF), q_shapes[0], q_shapes[1], q_shapes[1], sds((8, W), F32)],
            d2, dh, dhr, keep["r1"], keep["vec"], *weights[index][0], keep["ctx"], keep["q"],
            keep["kv"], keep["kvr"], keep["prob"], mask,
            scratch=[pltpu.VMEM((nh, R, SLOT), BF), pltpu.VMEM((nh, R, SLOT), F32)], us=14,
        )

    def input_back(index, dq, dkv, back):
        return call(
            bind(input_back_body, z),
            [sds((2, R, 3 * z.quarter), BF), sds((2, R, 3 * z.lquarter), BF), sds((R, W), BF),
             sds((2, 1, 3 * z.quarter), F32), sds((2, 1, 3 * z.lquarter), F32)],
            dq, dkv, back, *weights[index][0],
        )

    def input_grads(index, *args):
        keep = saved[index]
        g0, s0 = call(
            bind(input_grads_body, z), [vshape] * 2, keep["x"], args[0], keep["ctx"], *args[1:],
            scratch=[pltpu.VMEM((16, cols), F32)], meta=meta,
        )
        return Reduce(g0, s0, x_size)

    def leave(summed, *args):
        return call(
            bind(exit_body, z, summed),
            [sds((R, W), BF), sds((R // 2, W), BF), sds((R, W), BF), sds((R // 2, W), BF)], *args,
            meta=meta,
        )

    out, d2, df, dut, dul, dh, va, gut, gul = tail(1, *inner, cot)
    dhr = swap(dh, "l")
    r1f = ffn_grads(1, df, dut, dul, dhr)
    here, part, send, send_far = leave(False, xin, after(out, r1f.keep))
    d1, da, dq, dkv, dkvr, vb = attend_back(1, d2, dh, after(dhr, r1f.keep, here))
    back = swap(dkvr, "c")
    s0 = r1f.x_step(0, vb)
    yt, yl, dxp, gbt, gbl = input_back(1, dq, dkv, after(back, s0))
    dxr = swap(dxp, "l")
    r10 = input_grads(1, da, yt, yl, va, vb, gbt, gbl, gut, gul)
    got, near = swap(after(send, dxp), "y"), swap(after(part, dxp), "h")
    n0 = r1f.near(0, r10.keep)
    s1 = r1f.x_step(1, n0)
    near = after(near, s1)
    got = after(got, near)

    dx1, d2, df, dut, dul, dh, va, gut, gul = tail(
        0, saved[0]["r2"], d1, dxp, after(dxr, r10.keep, n0, s1, got)
    )
    dhr = swap(dh, "l")
    r0f = ffn_grads(0, df, dut, dul)
    n1 = r1f.near(1, r0f.keep)
    s10 = r10.x_step(2, n1)
    d1, da, dq, dkv, dkvr, vb = attend_back(0, d2, dh, after(dhr, r0f.keep, s10, n1))
    back = swap(dkvr, "c")
    n10 = r10.near(2, vb)
    s0 = r0f.x_step(0, n10)
    yt, yl, dxp, gbt, gbl = input_back(0, dq, dkv, after(back, s0))
    dxr = swap(dxp, "l")
    far = swap_both(after(send_far, dxp))
    r00 = input_grads(0, da, yt, yl, va, vb, gbt, gbl, gut, gul)
    rest, first = Finish(y), Finish(y)
    y0 = rest.y_step(0, r0f.near(0, r00.keep), n0)
    dxr = after(dxr, far, y0)

    def sort(here, got, near, far, low):
        kept, sent = call(
            bind(sort_body, z), [sds((2 * R, W), BF), sds((2 * R + 16, W), BF)],
            here, got, near, far, low, meta=meta,
        )
        return kept, swap(sent, "c")

    def place(kept, sent):
        shape = layout_in.shape
        t, l_ = call(
            bind(place_body, z),
            [sds((1,) + text_in.shape, BF), sds((1, shape[0], shape[2], shape[1]), BF)],
            kept, sent, meta=meta,
        )
        return t, flip(l_)

    low = swap(join_rows(near, after(far, dxr)), "l")
    dhere, dpart, dsend, dsend_far = leave(True, d1, dxp, after(dxr, r00.keep), dx1)
    dgot, dnear, dfar = swap(dsend, "y"), swap(dpart, "h"), swap_both(dsend_far)
    h0 = rest.h_step(dhere)
    s0 = r00.x_step(2, h0)
    dnear, dfar, low = after(dnear, s0), after(dfar, s0), after(low, s0)
    dlow = swap(join_rows(dnear, dfar), "l")
    dgot = after(dgot, dnear)
    kept, sent = sort(here, got, near, far, after(low, dgot))
    s1 = r0f.x_step(1, dgot)
    y1 = first.y_step(2, r00.near(2, s1), n10)
    dlow = after(dlow, y1, kept)
    dkept, dsent = sort(dhere, dgot, dnear, dfar, dlow)
    yf = rest.y_step(1, r0f.near(1, dkept), n1)
    h1 = first.h_step(yf)
    own1 = first.close(h1)
    res_t, res_l = place(kept, after(sent, own1))
    dx_t, dx_l = place(dkept, after(dsent, res_t))
    own2 = rest.close(dx_t)
    like = lambda *arrays: [sds(v.shape, F32) for v in arrays]
    g_tup, g_lup, g_tdn, g_ldn = call(
        bind(finish_body, z), like(t_up, l_up, flip(t_down), flip(l_down)), *rest.terms(own2)
    )
    g_ti, g_tb, g_to, g_tg, g_ts, g_tu, g_li, g_lb, g_lo, g_lg, g_ls, g_lu = call(
        bind(finish_first_body, z),
        like(t_in, t_hb, t_out, t_gain, t_shift, t_ub, l_in, l_hb, l_out, l_gain, l_shift, l_ub),
        *first.terms(g_tup),
    )
    return (
        res_t, res_l, dx_t, dx_l,
        g_ti, g_tb, g_to, g_tg, g_ts, g_tup, g_tu, flip(g_tdn),
        g_li, g_lb, g_lo, g_lg, g_ls, g_lup, g_lu, flip(g_ldn),
    )


def solution(mesh):
    section, dp, tensor = (mesh.shape[a] for a in ("section", "dp", "tensor"))
    fine = Mesh(mesh.devices.reshape(section, dp // 2, 2, 2, tensor // 2), ALL)
    d, t = ("x", "c"), ("h", "l")
    weights = (
        P("y", None, d, t),
        P("y", None, t + d),
        P("y", t, d),
        P("y", None, d),
        P("y", None, d),
        P("y", d, t),
        P("y", t + d),
        P("y", t, d),
    ) * 2
    pages = (P(d, None, None), P(d, None, None))
    return jax.shard_map(
        per_device,
        mesh=fine,
        in_specs=pages + (P(d, None),) + pages + weights,
        out_specs=(P("y", d, None, None),) * 4 + weights,
        check_vma=False,
    )
```

```python
import functools

import jax
import jax.numpy as jnp
from jax import lax
from jax.experimental import pallas as pl
from jax.experimental.pallas import tpu as pltpu
from jax.sharding import Mesh, PartitionSpec as P

BF = jnp.bfloat16
F32 = jnp.float32
HEAD = 64
LHEAD = 16
SLOT = 128
GROUPS = 3
ALL = ("y", "x", "c", "h", "l")


def mm(a, b):
    return lax.dot_general(a, b, (((1,), (0,)), ((), ())), preferred_element_type=F32)


def mm_nt(a, b):
    return lax.dot_general(a, b, (((1,), (1,)), ((), ())), preferred_element_type=F32)


def mm_tn(a, b):
    return lax.dot_general(a, b, (((0,), (0,)), ((), ())), preferred_element_type=F32)


class Sizes:
    def __init__(self, text, layout, rd, ld, cols, lcols, dp):
        self.seq = text.shape[1]
        self.rows = self.seq // 2
        self.d = text.shape[2]
        self.ld = layout.shape[2]
        self.width = self.d + self.ld
        self.rd = rd
        self.lr = ld
        self.dp = dp
        self.quarter = cols
        self.lquarter = lcols
        self.heads = cols // HEAD
        self.block = rd + ld // GROUPS
        self.vblock = self.block + 16
        self.part = ld // GROUPS
        self.xs = dp // 2
        self.masks = 4 if self.xs == 2 else 2


def call(body, out_shapes, *args, scratch=(), meta=None, us=4):
    places = [pl.BlockSpec(memory_space=pltpu.VMEM)] * len(args)
    if meta is not None:
        args = (meta,) + args
        places = [pl.BlockSpec(memory_space=pltpu.SMEM)] + places
    return pl.pallas_call(
        body,
        out_shape=list(out_shapes),
        in_specs=places,
        out_specs=[pl.BlockSpec(memory_space=pltpu.VMEM)] * len(out_shapes),
        scratch_shapes=list(scratch),
        compiler_params=pltpu.CompilerParams(vmem_limit_bytes=56 * 2**20),
        cost_estimate=pl.CostEstimate(flops=int(us * 2.3e9), bytes_accessed=1000, transcendentals=0),
    )(*args)


def sds(shape, dtype):
    return jax.ShapeDtypeStruct(shape, dtype)


def text_w(w, h, z, lo=0, hi=None):
    return jnp.concatenate(
        [w[r % 2][r // 2, w[2](h), : z.rd, lo:hi] for r in range(z.dp)], axis=0
    )


def layout_w(w, h, z, lo=0, hi=None):
    width = w[0].shape[-1] // GROUPS
    hi = width if hi is None else hi
    pieces = []
    for r in range(z.dp):
        for k in range(GROUPS):
            rows = slice(z.rd, z.rd + z.part)
            pieces.append(w[r % 2][r // 2, w[2](h), rows, width * k + lo : width * k + hi])
    return jnp.concatenate(pieces, axis=0)


def alone(h):
    return h


def first_of_two(h):
    return 2 * h


def second_of_two(h):
    return 2 * h + 1


class Pick:
    def __init__(self, refs, core, piece):
        self.refs, self.core, self.piece = refs, core, piece
        self.shape = refs[core].shape

    def __getitem__(self, at):
        x, h, rows, cols = at
        if len(self.refs) == 4:
            return self.refs[2 * h + self.core][x, self.piece, rows, cols]
        return self.refs[self.core][x, 2 * h + self.piece, rows, cols]


def feed_forward(refs):
    return tuple((Pick(refs, 0, p), Pick(refs, 1, p), alone) for p in range(2))


def put_grads(g, h, text, layout, z):
    width = g[0].shape[-1] // GROUPS
    low = layout.astype(BF)
    pad = width - low.shape[-1]
    low = jnp.concatenate([low, jnp.zeros((low.shape[0], pad), BF)], axis=1)
    text = text.astype(BF)
    at = g[2](h)
    for r in range(z.dp):
        ref, x = g[r % 2], r // 2
        ref[x, at, : z.rd, :] = text[z.rd * r : z.rd * (r + 1)]
        for k in range(GROUPS):
            base = z.lr * r + z.part * k
            ref[x, at, z.rd : z.block, width * k : width * (k + 1)] = low[base : base + z.part]


def natural(pieces, m, z):
    out = []
    for d in range(z.dp):
        value = pieces[d]
        for other in range(1, z.masks):
            value = jnp.where(m == other, pieces[d ^ other], value)
        out.append(value)
    return jnp.concatenate(out, axis=1)


def norm_stats(resid):
    center = resid - jnp.mean(resid, axis=-1, keepdims=True)
    factor = lax.rsqrt(jnp.mean(center * center, axis=-1, keepdims=True) + 1e-05)
    return center * factor, factor


def norm_both(resid, z):
    nt, ft = norm_stats(resid[:, : z.d])
    nl, fl = norm_stats(resid[:, z.d :])
    return jnp.concatenate([nt, nl], axis=1), ft, fl


def norm_back(grad, normed, factor, gain):
    scaled = grad * gain
    return factor * (
        scaled
        - jnp.mean(scaled, axis=-1, keepdims=True)
        - normed * jnp.mean(scaled * normed, axis=-1, keepdims=True)
    )


def norm_back_both(grad, normed, ft, fl, gain, z):
    gt = norm_back(grad[:, : z.d], normed[:, : z.d], ft, gain[:, : z.d])
    gl = norm_back(grad[:, z.d :], normed[:, z.d :], fl, gain[:, z.d :])
    return jnp.concatenate([gt, gl], axis=1)


def small_rows(w, h, z):
    return [w[r % 2][r // 2, h, z.block : z.vblock, :].astype(F32) for r in range(z.dp)]


def qkv_body(z, fused, meta_ref, *refs):
    if fused:
        (hid_ref, own_ref, rec_ref, prev_ref, ws_ref, wc_ref,
         r_ref, x_ref, q_ref, kv_ref, vec_ref, ut_ref, ul_ref) = refs
        vec = prev_ref[...]
        resid = (
            hid_ref[...].astype(F32) + own_ref[...].astype(F32) + rec_ref[...].astype(F32) + vec[4:5]
        )
        r_ref[...] = resid
        normed, _, _ = norm_both(resid, z)
        x = (normed * vec[1:2] + vec[5:6]).astype(BF)
        x_ref[...] = x
    else:
        x_ref, far_ref, ws_ref, wc_ref, q_ref, kv_ref, kvr_ref, vec_ref, ut_ref, ul_ref = refs
        x = x_ref[...]
    w = (ws_ref, wc_ref, alone)
    mask = meta_ref[1]
    lane = 4 * SLOT
    small = small_rows(w, 0, z)
    vec_ref[:, : z.d] = jnp.concatenate([s[:, : z.rd] for s in small], axis=1)
    vec_ref[:, z.d :] = jnp.concatenate([s[:, lane : lane + z.lr] for s in small], axis=1)
    xt, xl = x[:, : z.d], x[:, z.d :]
    n, m = z.quarter, z.lquarter
    zeros = jnp.zeros((z.rows, SLOT - HEAD - LHEAD), BF)
    hb, lb, ub, vb = n // z.dp, m // z.dp, 4 * n // z.dp, 4 * m // z.dp

    def project(xt, xl, first, out_ref):
        yt = mm(xt, text_w(w, h, z, n * first, 3 * n)) + bt[:, n * first :]
        yl = mm(xl, layout_w(w, h, z, m * first, 3 * m)) + bl[:, m * first :]
        yt = yt.astype(BF)
        yl = yl.astype(BF)
        for s in range(first, 3):
            for j in range(z.heads):
                lo, llo = n * (s - first) + HEAD * j, m * (s - first) + LHEAD * j
                a = yt[:, lo : lo + HEAD]
                b = yl[:, llo : llo + LHEAD]
                if s == 0:
                    a = a * BF(HEAD**-0.5)
                    b = b * BF(LHEAD**-0.5)
                slot = jnp.concatenate([a, b, zeros], axis=1)
                head = z.heads * h + j
                if s == 0:
                    q_ref[head] = slot
                else:
                    out_ref[2 * z.heads * (s - 1) + head] = slot

    for h in range(2):
        small = small_rows(w, h, z)
        rows = lambda i, lo, size: natural([s[i : i + 1, lo : lo + size] for s in small], mask, z)
        ut_ref[h] = rows(8, 0, ub)
        ul_ref[h] = rows(8, lane, vb)
        bt = jnp.concatenate([rows(6, 0, hb), jnp.zeros((1, n), F32), rows(7, 0, hb)], axis=1)
        bl = jnp.concatenate(
            [rows(6, lane, lb), jnp.zeros((1, m), F32), rows(7, lane, lb)], axis=1
        )
        project(xt, xl, 0, kv_ref)
        if not fused:
            far = far_ref[...]
            project(far[:, : z.d], far[:, z.d :], 1, kvr_ref)


def attend_body(z, q_ref, own_ref, rec_ref, mask_ref, ws_ref, wc_ref, a_ref, c_ref, p_ref, s_ref):
    w = (ws_ref, wc_ref, alone)
    count = 2 * z.heads
    m0 = mask_ref[0:1, : z.rows] > 0
    m1 = mask_ref[0:1, z.rows :] > 0

    def head(j, carry):
        q = q_ref[j]
        s0 = jnp.where(m0, mm_nt(q, own_ref[j]), -1000000000.0)
        s1 = jnp.where(m1, mm_nt(q, rec_ref[j]), -1000000000.0)
        top = jnp.maximum(
            jnp.max(s0, axis=-1, keepdims=True), jnp.max(s1, axis=-1, keepdims=True)
        )
        e0 = jnp.exp(s0 - top)
        e1 = jnp.exp(s1 - top)
        inv = 1.0 / (jnp.sum(e0, axis=-1, keepdims=True) + jnp.sum(e1, axis=-1, keepdims=True))
        p0 = (e0 * inv).astype(BF)
        p1 = (e1 * inv).astype(BF)
        p_ref[j, :, : z.rows] = p0
        p_ref[j, :, z.rows :] = p1
        s_ref[j] = (mm(p0, own_ref[count + j]) + mm(p1, rec_ref[count + j])).astype(BF)
        return carry

    lax.fori_loop(0, count, head, 0, unroll=True)
    n, m = z.quarter, z.lquarter
    at = al = None
    for h in range(2):
        heads = [s_ref[z.heads * h + j] for j in range(z.heads)]
        ct = jnp.concatenate([s[:, :HEAD] for s in heads], axis=1)
        cl = jnp.concatenate([s[:, HEAD : HEAD + LHEAD] for s in heads], axis=1)
        c_ref[h, :, :n] = ct
        c_ref[h, :, 2 * SLOT : 2 * SLOT + m] = cl
        pt = mm_nt(ct, text_w(w, h, z, 3 * n, 4 * n))
        pll = mm_nt(cl, layout_w(w, h, z, 3 * m, 4 * m))
        at = pt if at is None else at + pt
        al = pll if al is None else al + pll
    a_ref[:, : z.d] = at.astype(BF)
    a_ref[:, z.d :] = al.astype(BF)


def gelu_parts(u):
    cdf = 0.5 * (1.0 + lax.erf(u * 0.7071067811865476))
    slope = cdf + u * jnp.exp(-0.5 * u * u) * 0.3989422804014327
    return (u * cdf).astype(BF), slope.astype(BF)


def forward_body(
    z, x_ref, own_ref, rec_ref, vec_ref, bt_ref, bl_ref, *refs
):
    r_ref, hid_ref, gt_ref, gl_ref, st_ref, sl_ref, f_ref = refs[-7:]
    up, down = feed_forward(refs[:-7])
    lw = 4 * z.lquarter
    vec = vec_ref[...]
    resid = x_ref[...].astype(F32) + own_ref[...].astype(F32) + rec_ref[...].astype(F32) + vec[2:3]
    r_ref[...] = resid
    normed, _, _ = norm_both(resid, z)
    hid = (normed * vec[0:1] + vec[3:4]).astype(BF)
    hid_ref[...] = hid
    ht, hl = hid[:, : z.d], hid[:, z.d :]
    ft = fl = None
    for h in range(2):
        g, s = gelu_parts(mm(ht, text_w(up, h, z)) + bt_ref[h])
        gt_ref[h] = g
        st_ref[h] = s
        p = mm_nt(g, text_w(down, h, z))
        ft = p if ft is None else ft + p
        g, s = gelu_parts(mm(hl, layout_w(up, h, z, 0, lw)) + bl_ref[h])
        gl_ref[h] = g
        sl_ref[h] = s
        p = mm_nt(g, layout_w(down, h, z, 0, lw))
        fl = p if fl is None else fl + p
    f_ref[:, : z.d] = ft.astype(BF)
    f_ref[:, z.d :] = fl.astype(BF)


def col_sum(value):
    return jnp.sum(value, axis=0, keepdims=True)


def tail_body(z, fused, *refs):
    if fused == "last":
        hid_ref, own_ref, rec_ref, go_ref, vec_ref, st_ref, sl_ref = refs[:7]
        ws = refs[7:-9]
        out_ref, d2_ref, df_ref, dut_ref, dul_ref, dh_ref, vg_ref, gbt_ref, gbl_ref = refs[-9:]
        vec = vec_ref[...]
        resid = (
            hid_ref[...].astype(F32) + own_ref[...].astype(F32) + rec_ref[...].astype(F32) + vec[4:5]
        )
        normed, ft, fl = norm_both(resid, z)
        out_ref[...] = (normed * vec[1:2] + vec[5:6]).astype(BF)
        go = go_ref[...].astype(F32)
    else:
        r_ref, d1_ref, own_ref, rec_ref, vec_ref, st_ref, sl_ref = refs[:7]
        ws = refs[7:-9]
        dx_ref, d2_ref, df_ref, dut_ref, dul_ref, dh_ref, vg_ref, gbt_ref, gbl_ref = refs[-9:]
        vec = vec_ref[...]
        normed, ft, fl = norm_both(r_ref[...], z)
        low = (d1_ref[...] + own_ref[...].astype(F32) + rec_ref[...].astype(F32)).astype(BF)
        dx_ref[...] = low
        go = low.astype(F32)
    up, down = feed_forward(ws)
    lw = 4 * z.lquarter
    d2 = norm_back_both(go, normed, ft, fl, vec[1:2], z)
    d2_ref[...] = d2
    df = d2.astype(BF)
    df_ref[...] = df
    vg_ref[0:1] = col_sum(go * normed)
    vg_ref[1:2] = col_sum(go)
    vg_ref[2:3] = col_sum(df.astype(F32))
    vg_ref[3:8] = jnp.zeros((5, z.width), F32)
    dft, dfl = df[:, : z.d], df[:, z.d :]
    ht = hl = None
    for h in range(2):
        du = (mm(dft, text_w(down, h, z)) * st_ref[h].astype(F32)).astype(BF)
        dut_ref[h] = du
        gbt_ref[h] = col_sum(du.astype(F32))
        p = mm_nt(du, text_w(up, h, z))
        ht = p if ht is None else ht + p
        du = (mm(dfl, layout_w(down, h, z, 0, lw)) * sl_ref[h].astype(F32)).astype(BF)
        dul_ref[h] = du
        gbl_ref[h] = col_sum(du.astype(F32))
        p = mm_nt(du, layout_w(up, h, z, 0, lw))
        hl = p if hl is None else hl + p
    dh_ref[:, : z.d] = ht.astype(BF)
    dh_ref[:, z.d :] = hl.astype(BF)


def ffn_grads_body(z, hid_ref, df_ref, gt_ref, gl_ref, dut_ref, dul_ref, g_ref, h_ref):
    one, two = (g_ref, h_ref, first_of_two), (g_ref, h_ref, second_of_two)
    hid, df = hid_ref[...], df_ref[...]
    for h in range(2):
        put_grads(one, h, mm_tn(hid[:, : z.d], dut_ref[h]), mm_tn(hid[:, z.d :], dul_ref[h]), z)
        put_grads(two, h, mm_tn(df[:, : z.d], gt_ref[h]), mm_tn(df[:, z.d :], gl_ref[h]), z)


def attend_back_body(
    z, d2_ref, own_ref, rec_ref, r_ref, vec_ref, ws_ref, wc_ref, c_ref, q_ref, kv_ref, kvr_ref, p_ref, mask_ref,
    d1_ref, da_ref, dq_ref, dkv_ref, dkvr_ref, vg_ref, dc_ref, dd_ref,
):
    count = 2 * z.heads
    w = (ws_ref, wc_ref, alone)
    vec = vec_ref[...]
    dh = d2_ref[...] + own_ref[...].astype(F32) + rec_ref[...].astype(F32)
    normed, ft, fl = norm_both(r_ref[...], z)
    d1 = norm_back_both(dh, normed, ft, fl, vec[0:1], z)
    d1_ref[...] = d1
    da = d1.astype(BF)
    da_ref[...] = da
    vg_ref[0:1] = col_sum(dh * normed)
    vg_ref[1:2] = col_sum(dh)
    vg_ref[2:3] = col_sum(da.astype(F32))
    vg_ref[3:8] = jnp.zeros((5, z.width), F32)
    n, m = z.quarter, z.lquarter
    zeros = jnp.zeros((z.rows, SLOT - HEAD - LHEAD), BF)
    for h in range(2):
        dct = mm(da[:, : z.d], text_w(w, h, z, 3 * n, 4 * n)).astype(BF)
        dcl = mm(da[:, z.d :], layout_w(w, h, z, 3 * m, 4 * m)).astype(BF)
        for j in range(z.heads):
            a = dct[:, HEAD * j : HEAD * (j + 1)]
            b = dcl[:, LHEAD * j : LHEAD * (j + 1)]
            dc_ref[z.heads * h + j] = jnp.concatenate([a, b, zeros], axis=1)
            ct = c_ref[h, :, HEAD * j : HEAD * (j + 1)].astype(F32)
            cl = c_ref[h, :, 2 * SLOT + LHEAD * j : 2 * SLOT + LHEAD * (j + 1)].astype(F32)
            dt = jnp.sum(a.astype(F32) * ct, axis=-1, keepdims=True)
            dl = jnp.sum(b.astype(F32) * cl, axis=-1, keepdims=True)
            dd_ref[z.heads * h + j, :, 0:1] = dt
            dd_ref[z.heads * h + j, :, 1:2] = dt + dl
    lane = lax.broadcasted_iota(jnp.int32, (z.rows, SLOT), 1)
    text_lane = lane < HEAD
    scale = jnp.where(text_lane, HEAD**-0.5, LHEAD**-0.5)
    mask = mask_ref[...]
    masks = (mask[:, : z.rows], mask[:, z.rows :])

    def head(j, carry):
        dc = dc_ref[j]
        dct = jnp.where(text_lane, dc, jnp.zeros_like(dc))
        q = q_ref[j]
        dt = dd_ref[j, :, 0:1]
        ds = dd_ref[j, :, 1:2]
        dq_t = dq_s = None
        for i, (k_ref, o_ref) in enumerate(((kv_ref, dkv_ref), (kvr_ref, dkvr_ref))):
            k = k_ref[j]
            v = k_ref[count + j]
            prob = p_ref[j, :, z.rows * i : z.rows * (i + 1)]
            pm = jnp.where(masks[i] > 0, prob.astype(F32), 0.0)
            st = (pm * (mm_nt(dct, v) - dt)).astype(BF)
            ss = (pm * (mm_nt(dc, v) - ds)).astype(BF)
            a = mm(st, k)
            b = mm(ss, k)
            dq_t = a if dq_t is None else dq_t + a
            dq_s = b if dq_s is None else dq_s + b
            dk = jnp.where(text_lane, mm_tn(st, q), mm_tn(ss, q))
            o_ref[j] = dk.astype(BF)
            o_ref[count + j] = mm_tn(prob, dc).astype(BF)
        dq_ref[j] = (jnp.where(text_lane, dq_t, dq_s) * scale).astype(BF)
        return carry

    lax.fori_loop(0, count, head, 0, unroll=True)


def input_back_body(z, dq_ref, dkv_ref, rec_ref, ws_ref, wc_ref, yt_ref, yl_ref, dx_ref, gbt_ref, gbl_ref):
    count = 2 * z.heads
    w = (ws_ref, wc_ref, alone)
    n, m = z.quarter, z.lquarter
    xt = xl = None
    for h in range(2):
        ts, ls = [], []
        for s in range(3):
            for j in range(z.heads):
                head = z.heads * h + j
                if s == 0:
                    slot = dq_ref[head]
                else:
                    at = count * (s - 1) + head
                    slot = (dkv_ref[at].astype(F32) + rec_ref[at].astype(F32)).astype(BF)
                ts.append(slot[:, :HEAD])
                ls.append(slot[:, HEAD : HEAD + LHEAD])
        yt = jnp.concatenate(ts, axis=1)
        yl = jnp.concatenate(ls, axis=1)
        yt_ref[h] = yt
        yl_ref[h] = yl
        gbt_ref[h] = col_sum(yt.astype(F32))
        gbl_ref[h] = col_sum(yl.astype(F32))
        p = mm_nt(yt, text_w(w, h, z, 0, 3 * n))
        xt = p if xt is None else xt + p
        p = mm_nt(yl, layout_w(w, h, z, 0, 3 * m))
        xl = p if xl is None else xl + p
    dx_ref[:, : z.d] = xt.astype(BF)
    dx_ref[:, z.d :] = xl.astype(BF)


def input_grads_body(
    z, meta_ref, x_ref, da_ref, c_ref, yt_ref, yl_ref, va_ref, vb_ref, bt_ref, bl_ref, ut_ref, ul_ref,
    g_ref, h_ref, s_ref,
):
    g = (g_ref, h_ref, alone)
    x, da = x_ref[...], da_ref[...]
    n, m = z.quarter, z.lquarter
    va, vb = va_ref[...], vb_ref[...]
    mask = meta_ref[1]
    rows = (vb[0:1], va[0:1], vb[2:3], vb[1:2], va[2:3], va[1:2])
    lane = 4 * SLOT
    s_ref[...] = jnp.zeros_like(s_ref)

    def relative(value, size):
        parts = [value[:, size * d : size * (d + 1)] for d in range(z.dp)]
        out = []
        for r in range(z.dp):
            v = parts[r]
            for other in range(1, z.masks):
                v = jnp.where(mask == other, parts[r ^ other], v)
            out.append(v)
        return out

    for h in range(2):
        ct = c_ref[h, :, :n]
        cl = c_ref[h, :, 2 * SLOT : 2 * SLOT + m]
        text = jnp.concatenate(
            [mm_tn(x[:, : z.d], yt_ref[h]), mm_tn(da[:, : z.d], ct)], axis=1
        )
        layout = jnp.concatenate(
            [mm_tn(x[:, z.d :], yl_ref[h]), mm_tn(da[:, z.d :], cl)], axis=1
        )
        put_grads(g, h, text, layout, z)
        bt, bl, ut, ul = bt_ref[h], bl_ref[h], ut_ref[h], ul_ref[h]
        entries = [
            (6, 0, relative(bt[:, :n], n // z.dp)),
            (7, 0, relative(bt[:, 2 * n :], n // z.dp)),
            (6, lane, relative(bl[:, :m], m // z.dp)),
            (7, lane, relative(bl[:, 2 * m :], m // z.dp)),
            (8, 0, relative(ut, 4 * n // z.dp)),
            (8, lane, relative(ul, 4 * m // z.dp)),
        ]
        for r in range(z.dp):
            for i, row in enumerate(rows):
                s_ref[i : i + 1, : z.rd] = row[:, z.rd * r : z.rd * (r + 1)]
                s_ref[i : i + 1, lane : lane + z.lr] = row[
                    :, z.d + z.lr * r : z.d + z.lr * (r + 1)
                ]
            for at, lo, values in entries:
                s_ref[at : at + 1, lo : lo + values[r].shape[1]] = values[r]
            g[r % 2][r // 2, h, z.block : z.vblock, :] = s_ref[...].astype(BF)


def put_pack(out_ref, text, layout, z):
    out_ref[: z.rd, :] = text.astype(BF)
    width = out_ref.shape[-1] // GROUPS
    low = layout.astype(BF)
    low = jnp.concatenate([low, jnp.zeros((low.shape[0], width - low.shape[1]), BF)], axis=1)
    for k in range(GROUPS):
        out_ref[z.rd : z.block, width * k : width * (k + 1)] = low[z.part * k : z.part * (k + 1)]


def pack_first_body(
    z, ti_ref, to_ref, li_ref, lo_ref, tg_ref, lg_ref, ts_ref, ls_ref, tb_ref, lb_ref, tu_ref, lu_ref,
    out_ref, s_ref,
):
    text = jnp.concatenate([ti_ref[0, 0], ti_ref[0, 1], ti_ref[0, 2], to_ref[0].T], axis=1)
    layout = jnp.concatenate([li_ref[0, 0], li_ref[0, 1], li_ref[0, 2], lo_ref[0].T], axis=1)
    put_pack(out_ref, text, layout, z)
    s_ref[...] = jnp.zeros_like(s_ref)
    for lane, refs in ((0, (tg_ref, ts_ref, tb_ref)), (4 * SLOT, (lg_ref, ls_ref, lb_ref))):
        at = 0
        for ref in refs:
            count, width = ref.shape[1], ref.shape[2]
            s_ref[at : at + count, lane : lane + width] = ref[0]
            at += count
    s_ref[8:9, : tu_ref.shape[1]] = tu_ref[...]
    s_ref[8:9, 4 * SLOT : 4 * SLOT + lu_ref.shape[1]] = lu_ref[...]
    out_ref[z.block : z.vblock, :] = s_ref[...].astype(BF)


def pack_rest_body(z, tu_ref, lu_ref, td_ref, ld_ref, out_ref):
    put_pack(out_ref.at[0], tu_ref[0], lu_ref[0], z)
    put_pack(out_ref.at[1], td_ref[0], ld_ref[0], z)


def take_layout(total, cols, z):
    width = total.shape[-1] // GROUPS
    return jnp.concatenate(
        [total[z.rd : z.block, width * k : width * k + cols] for k in range(GROUPS)], axis=0
    )


def final_sum(refs):
    return sum(r[...].astype(F32) for r in refs)


def finish_first_body(z, *refs):
    (ti_ref, tb_ref, to_ref, tg_ref, ts_ref, tu_ref,
     li_ref, lb_ref, lo_ref, lg_ref, ls_ref, lu_ref) = refs[2:]
    total = final_sum(refs[:2])[0]
    n, m = z.quarter, z.lquarter
    layout = take_layout(total, 4 * m, z)
    for s in range(3):
        ti_ref[0, s] = total[: z.rd, n * s : n * (s + 1)]
        li_ref[0, s] = layout[:, m * s : m * (s + 1)]
    to_ref[0] = total[: z.rd, 3 * n :].T
    lo_ref[0] = layout[:, 3 * m :].T
    rows = total[z.block : z.vblock]
    for lane, group in ((0, (tg_ref, ts_ref, tb_ref)), (4 * SLOT, (lg_ref, ls_ref, lb_ref))):
        at = 0
        for ref in group:
            count, width = ref.shape[1], ref.shape[2]
            ref[0] = rows[at : at + count, lane : lane + width]
            at += count
    tu_ref[...] = rows[8:9, : tu_ref.shape[1]]
    lu_ref[...] = rows[8:9, 4 * SLOT : 4 * SLOT + lu_ref.shape[1]]


def finish_body(z, *refs):
    total = final_sum(refs[:2])
    for p in range(2):
        t_ref, l_ref = refs[2 + 2 * p : 4 + 2 * p]
        t_ref[0] = total[p, : z.rd]
        l_ref[0] = take_layout(total[p], 4 * z.lquarter, z)


def entry_body(z, meta_ref, t_ref, l_ref, tc_ref, lc_ref, mask_ref, own_ref, send_ref):
    y, c = meta_ref[0], meta_ref[2]
    row = jnp.where(y == 0, mask_ref[0:1, :], mask_ref[1:2, :]).astype(F32)
    left, right = row[:, : z.rows], row[:, z.rows :]
    for ref, half in ((own_ref, c), (send_ref, 1 - c)):
        for i, (text, layout) in enumerate(((t_ref, l_ref), (t_ref, l_ref), (tc_ref, lc_ref))):
            part = 1 - half if i == 1 else half
            rows = pl.ds(pl.multiple_of(part * z.rows, z.rows), z.rows)
            out = slice(z.rows * i, z.rows * (i + 1))
            ref[out, : z.d] = text[y, rows, :]
            ref[out, z.d :] = layout[y, :, rows].astype(F32).T.astype(BF)
        near = jnp.where(half == 0, left, right)
        far = jnp.where(half == 0, right, left)
        low = jnp.concatenate([near, far, jnp.zeros((1, z.width - z.seq), F32)], axis=1)
        ref[3 * z.rows :, :] = jnp.broadcast_to(low, (16, z.width)).astype(BF)


def ordered(value, m, z):
    text = [value[:, z.rd * r : z.rd * (r + 1)] for r in range(z.dp)]
    layout = [value[:, z.d + z.lr * r : z.d + z.lr * (r + 1)] for r in range(z.dp)]
    return jnp.concatenate([natural(text, m, z), natural(layout, m, z)], axis=1)


def settle_body(z, meta_ref, own_ref, got_ref, x_ref, far_ref, cot_ref, out_ref):
    mine = meta_ref[3] == 1
    mask = meta_ref[1]
    step = z.rows // 4

    def chunk(k, carry):
        rows = pl.ds(pl.multiple_of(k * step, step), step)
        for i, ref in enumerate((x_ref, far_ref, cot_ref)):
            at = pl.ds(pl.multiple_of(z.rows * i + k * step, step), step)
            ref[rows, :] = ordered(jnp.where(mine, own_ref[at, :], got_ref[at, :]), mask, z)
        return carry

    lax.fori_loop(0, 4, chunk, 0)
    last = slice(3 * z.rows, 3 * z.rows + 16)
    row = jnp.where(mine, own_ref[last, : z.seq], got_ref[last, : z.seq])
    out_ref[...] = row.astype(F32)[0:1]


def exit_body(z, summed, meta_ref, *refs):
    if summed:
        d_ref, own_ref, rec_ref, b_ref, here_ref, part_ref, send_ref, far_ref = refs
    else:
        a_ref, b_ref, here_ref, part_ref, send_ref, far_ref = refs
    first = meta_ref[0] == 0
    low = meta_ref[4] == 0
    mask = meta_ref[1]
    half = z.rows // 2
    pieces = 1 if summed else 4
    step = z.rows // pieces

    def chunk(k, carry):
        rows = pl.ds(pl.multiple_of(k * step, step), step) if pieces > 1 else slice(None)
        two = b_ref[rows, :]
        if summed:
            one = d_ref[rows, :] + own_ref[rows, :].astype(F32) + rec_ref[rows, :].astype(F32)
            one = one.astype(BF)
        else:
            one = a_ref[rows, :]
        here_ref[rows, :] = ordered(jnp.where(first, one, two), mask, z)
        send_ref[rows, :] = ordered(jnp.where(first, two, one), mask, z)
        return carry

    lax.fori_loop(0, pieces, chunk, 0)
    part_ref[...] = jnp.where(low, here_ref[:half, :], here_ref[half:, :])
    far_ref[...] = jnp.where(low, send_ref[:half, :], send_ref[half:, :])


def sort_body(z, meta_ref, here_ref, got_ref, b_ref, d_ref, far_ref, keep_ref, send_ref):
    mine = meta_ref[3] == 1
    low = meta_ref[4] == 0
    half = z.rows // 2
    for i, (same_ref, near_ref) in enumerate(((here_ref, b_ref), (got_ref, d_ref))):
        beyond = far_ref[half * i : half * (i + 1), :]
        for k in range(2):
            rows = slice(half * k, half * (k + 1))
            other = jnp.where(low == (k == 0), near_ref[...], beyond)
            same = same_ref[rows, :]
            rows = slice(z.rows * i + half * k, z.rows * i + half * (k + 1))
            keep_ref[rows, :] = jnp.where(mine, same, other)
            send_ref[rows, :] = jnp.where(mine, other, same)
    send_ref[2 * z.rows :, :] = jnp.zeros((16, z.width), BF)


def place_body(z, meta_ref, keep_ref, got_ref, t_ref, l_ref):
    y, c = meta_ref[0], meta_ref[2]
    for i in range(2):
        page = y if i == 0 else 1 - y
        for ref, half in ((keep_ref, c), (got_ref, 1 - c)):
            rows = pl.ds(pl.multiple_of(half * z.rows, z.rows), z.rows)
            value = ref[z.rows * i : z.rows * (i + 1), :]
            t_ref[0, page, rows, :] = value[:, : z.d]
            l_ref[0, page, :, rows] = value[:, z.d :].astype(F32).T.astype(BF)


def swap(value, axis):
    return lax.ppermute(value, axis, [(0, 1), (1, 0)])


def after(value, *others):
    return lax.optimization_barrier((value,) + others)[0]


def together(*values):
    return lax.optimization_barrier(values)


def swap_both(value):
    return lax.ppermute(value, ("y", "h"), [(0, 3), (1, 2), (2, 1), (3, 0)])


def join_rows(*parts):
    return jnp.concatenate(parts + (jnp.zeros((16, parts[0].shape[1]), BF),), axis=0)


def join_blocks(parts, got):
    own = jnp.stack([jnp.concatenate(parts), jnp.concatenate(got)])
    return own, swap(own, "c")


def gather_blocks(parts, x_size, *token):
    if x_size == 2:
        return join_blocks(parts, [after(swap(v, "x"), *token) for v in parts])
    else:
        own = lax.all_gather(jnp.concatenate(parts), "x", axis=0)
    return own, swap(own, "c")


def add_low(*terms):
    total = terms[0].astype(F32)
    for term in terms[1:]:
        total = total + term.astype(F32)
    return total.astype(BF)


class Reduce:
    def __init__(self, keep, send, x_size, *token):
        self.keep, self.x_size = keep, x_size
        half = keep.shape[1] // 2
        self.rows = (slice(half, None), slice(0, half), slice(None))
        self.got = swap(after(send, *token) if token else send, "c")
        self.far = {}

    def x_step(self, part, *token):
        got, rows = after(self.got, *token), self.rows[part]
        if self.x_size == 2:
            total = add_low(self.keep[1, rows], got[1, rows])
            self.far[part] = swap(total, "x")
        else:
            total = add_low(self.keep[:, rows], got[:, rows])
            self.far[part] = lax.psum_scatter(total, "x", scatter_dimension=0, tiled=False)
        return total

    def near(self, part, *token):
        rows = self.rows[part]
        if part in self.far:
            far = after(self.far[part], *token)
        else:
            far = after(self.far[2], *token)[rows]
        if self.x_size == 2:
            far = add_low(self.keep[0, rows], self.got[0, rows], far)
        return far


class Finish:
    def __init__(self, y):
        self.y, self.here, self.cross = y, {}, {}

    def y_step(self, part, first, second):
        self.here[part] = jnp.where(self.y == 0, first, second)
        self.cross[part] = swap(jnp.where(self.y == 0, second, first), "y")
        return self.here[part]

    def sum_of(self, part, *token):
        if part in self.here:
            return add_low(self.here[part], after(self.cross[part], *token))
        half = self.here[2].shape[0] // 2
        rows = slice(half, None) if part == 0 else slice(0, half)
        return add_low(self.here[2][rows], after(self.cross[2], *token)[rows])

    def h_step(self, *token):
        other = self.sum_of(0, *token)
        self.last = swap(other, "h")
        return other

    def close(self, *token):
        self.own = self.sum_of(1, *token)
        return self.own

    def terms(self, *token):
        return (self.own, after(self.last, *token))


def per_device(
    text_in, layout_in, token_mask, text_cotangent, layout_cotangent,
    t_in, t_hb, t_out, t_gain, t_shift, t_up, t_ub, t_down,
    l_in, l_hb, l_out, l_gain, l_shift, l_up, l_ub, l_down,
):
    x_size = lax.axis_size("x")
    y, x, c, h, l = (lax.axis_index(a) for a in ALL)
    z = Sizes(
        text_in, layout_in, t_in.shape[2], l_in.shape[2], t_in.shape[3], l_in.shape[3], 2 * x_size
    )
    order = 2 * x + c if x_size == 2 else c
    meta = jnp.stack([y, order, c, (c == h).astype(jnp.int32), l, 0 * y, 0 * y, 0 * y])
    bind = functools.partial
    cols = t_up.shape[2]

    R, W, Q, M = z.rows, z.width, 4 * z.quarter, 4 * z.lquarter
    nh = 2 * z.heads
    flip = lambda v: jnp.swapaxes(v, -1, -2)

    (first,) = call(
        bind(pack_first_body, z), [sds((z.vblock, cols), BF)],
        t_in, t_out, l_in, l_out, t_gain, l_gain, t_shift, l_shift, t_hb, l_hb, t_ub, l_ub,
        scratch=[pltpu.VMEM((16, cols), F32)],
    )
    (rest,) = call(
        bind(pack_rest_body, z), [sds((2, z.block, cols), BF)],
        after(t_up, first), l_up, flip(t_down), flip(l_down), us=10,
    )
    own, send = call(
        bind(entry_body, z), [sds((3 * R + 16, W), BF)] * 2,
        after(text_in, rest), flip(layout_in), text_cotangent, flip(layout_cotangent), token_mask,
        meta=meta, us=10,
    )
    first = first[None]

    first_h = swap(first, "h")
    first_y = after(swap(first, "y"), rest, own)
    pick = lambda index, mine, across: jnp.where(y == index, mine, across)
    a0 = pick(0, first, first_y)
    rest_h = swap(after(rest, a0), "h")
    got = after(swap(send, "c"), a0)
    x0, far0, cot, mask = call(
        bind(settle_body, z), [sds((R, W), BF)] * 3 + [sds((1, z.seq), F32)], own, got, meta=meta, us=10,
    )
    first_h = after(first_h, x0)
    rest_y = after(swap(rest, "y"), first_h)
    f0 = pick(0, rest, rest_y)
    first_hy = swap(first_h, "y")
    rest_h = after(rest_h, first_h, f0)
    a1 = pick(0, first_h, after(first_hy, rest_h))
    parts_hy = [swap(rest_h[p : p + 1], "y") for p in range(2)]
    if x_size == 2:
        far_a = [swap(a0, "x"), swap(a1, "x")]
        far_f0 = swap(f0, "x")
        far_a[0] = after(far_a[0], far_a[1], far_f0, *parts_hy)
        weights = [[join_blocks([a0, a1], far_a)], []]
    else:
        weights = [[gather_blocks([a0, a1], x_size)], []]
    tokens = weights[0][0][0]
    f1 = pick(0, rest_h[0:1], after(parts_hy[0], tokens))
    f2 = pick(0, rest_h[1:2], after(parts_hy[1], tokens))
    x0 = after(x0, f1, f2)

    q_shapes = [sds((nh, R, SLOT), BF), sds((2 * nh, R, SLOT), BF)]
    v_shapes = [sds((16, W), F32), sds((2, 1, Q), F32), sds((2, 1, M), F32)]
    saved = []
    inner = None
    for index in range(2):
        w0 = weights[index][0]
        if index == 0:
            q, kv, kvr, vec, ut, ul = call(
                bind(qkv_body, z, False), q_shapes + q_shapes[1:] + v_shapes, x0, far0, *w0, meta=meta
            )
            xin = x0
        else:
            r2, xin, q, kv, vec, ut, ul = call(
                bind(qkv_body, z, True),
                [sds((R, W), F32), sds((R, W), BF)] + q_shapes + v_shapes,
                *inner, saved[0]["vec"], *w0, meta=meta,
            )
            saved[0]["r2"] = r2
            kvr = swap(kv, "c")
        a, ctx, prob = call(
            bind(attend_body, z),
            [sds((R, W), BF), sds((2, R, 3 * SLOT), BF), sds((nh, R, z.seq), BF)],
            q, kv, kvr, mask, *w0, scratch=[pltpu.VMEM((nh, R, SLOT), BF)], us=8,
        )
        ar = swap(a, "l")
        if index == 0:
            if x_size == 2:
                got = [after(swap(v, "x"), a) for v in (f1, f2)]
                weights[0].append(join_blocks([f0, f1, f2], [far_f0] + got))
            else:
                weights[0].append(gather_blocks([f0, f1, f2], x_size))
            token = weights[0][1][0]
            second = jnp.concatenate([pick(1, first, first_y), pick(1, after(first_h, token), first_hy)])
            got = swap(second, "x") if x_size == 2 else None
            if x_size == 2:
                ar = after(ar, got)
                weights[1].append(join_blocks([second], [got]))
            else:
                weights[1].append(gather_blocks([second], x_size))
            halves = [
                pick(1, after(rest, token), rest_y),
                jnp.concatenate(
                    [pick(1, after(rest_h, token)[p : p + 1], parts_hy[p]) for p in range(2)]
                ),
            ]
        if index == 1:
            if x_size == 2:
                far1 = swap(halves[1], "x")
                far1, ar = together(far1, ar)
                weights[1].append(near_blocks + join_blocks(halves[1:], [far1]))
            else:
                weights[1].append(gather_blocks(halves, x_size))
        r1, hid, gt, gl, st, sl, f = call(
            bind(forward_body, z),
            [sds((R, W), F32), sds((R, W), BF), sds((2, R, Q), BF), sds((2, R, M), BF),
             sds((2, R, Q), BF), sds((2, R, M), BF), sds((R, W), BF)],
            xin, a, ar, vec, ut, ul, *weights[index][1], us=6,
        )
        fr = swap(f, "l")
        if index == 0 and x_size == 2:
            far_half = swap(after(halves[0], ar), "x")
            fr = after(fr, far_half)
            near_blocks = join_blocks(halves[:1], [far_half])
        inner = (hid, f, fr)
        saved.append(dict(x=xin, q=q, kv=kv, kvr=kvr, ctx=ctx, prob=prob, r1=r1, hid=hid, gt=gt,
                          gl=gl, st=st, sl=sl, vec=vec))

    gshape = sds((x_size, 4, z.block, cols), BF)
    vshape = sds((x_size, 2, z.vblock, cols), BF)

    def tail(index, *args):
        keep = saved[index]
        shapes = [sds((R, W), BF), sds((R, W), F32), sds((R, W), BF), sds((2, R, Q), BF),
                  sds((2, R, M), BF), sds((R, W), BF), sds((8, W), F32), sds((2, 1, Q), F32),
                  sds((2, 1, M), F32)]
        return call(
            bind(tail_body, z, "last" if index == 1 else "mid"), shapes,
            *args, keep["vec"], keep["st"], keep["sl"], *weights[index][1], us=7,
        )

    def ffn_grads(index, df, dut, dul, *token):
        keep = saved[index]
        g, s = call(
            bind(ffn_grads_body, z), [gshape] * 2,
            keep["hid"], df, keep["gt"], keep["gl"], dut, dul, us=6,
        )
        return Reduce(g, s, x_size, *token)

    def attend_back(index, d2, dh, dhr):
        keep = saved[index]
        return call(
            bind(attend_back_body, z),
            [sds((R, W), F32), sds((R, W), BF), q_shapes[0], q_shapes[1], q_shapes[1], sds((8, W), F32)],
            d2, dh, dhr, keep["r1"], keep["vec"], *weights[index][0], keep["ctx"], keep["q"],
            keep["kv"], keep["kvr"], keep["prob"], mask,
            scratch=[pltpu.VMEM((nh, R, SLOT), BF), pltpu.VMEM((nh, R, SLOT), F32)], us=14,
        )

    def input_back(index, dq, dkv, back):
        return call(
            bind(input_back_body, z),
            [sds((2, R, 3 * z.quarter), BF), sds((2, R, 3 * z.lquarter), BF), sds((R, W), BF),
             sds((2, 1, 3 * z.quarter), F32), sds((2, 1, 3 * z.lquarter), F32)],
            dq, dkv, back, *weights[index][0],
        )

    def input_grads(index, *args):
        keep = saved[index]
        g0, s0 = call(
            bind(input_grads_body, z), [vshape] * 2, keep["x"], args[0], keep["ctx"], *args[1:],
            scratch=[pltpu.VMEM((16, cols), F32)], meta=meta,
        )
        return Reduce(g0, s0, x_size)

    def leave(summed, *args):
        return call(
            bind(exit_body, z, summed),
            [sds((R, W), BF), sds((R // 2, W), BF), sds((R, W), BF), sds((R // 2, W), BF)], *args,
            meta=meta,
        )

    out, d2, df, dut, dul, dh, va, gut, gul = tail(1, *inner, cot)
    dhr = swap(dh, "l")
    r1f = ffn_grads(1, df, dut, dul, dhr)
    here, part, send, send_far = leave(False, xin, after(out, r1f.keep))
    d1, da, dq, dkv, dkvr, vb = attend_back(1, d2, dh, after(dhr, r1f.keep, here))
    back = swap(dkvr, "c")
    s0 = r1f.x_step(0, vb)
    yt, yl, dxp, gbt, gbl = input_back(1, dq, dkv, after(back, s0))
    dxr = swap(dxp, "l")
    r10 = input_grads(1, da, yt, yl, va, vb, gbt, gbl, gut, gul)
    got, near = swap(after(send, dxp), "y"), swap(after(part, dxp), "h")
    n0 = r1f.near(0, r10.keep)
    s1 = r1f.x_step(1, n0)
    near = after(near, s1)
    got = after(got, near)

    dx1, d2, df, dut, dul, dh, va, gut, gul = tail(
        0, saved[0]["r2"], d1, dxp, after(dxr, r10.keep, n0, s1, got)
    )
    dhr = swap(dh, "l")
    r0f = ffn_grads(0, df, dut, dul)
    n1 = r1f.near(1, r0f.keep)
    s10 = r10.x_step(2, n1)
    far = swap_both(after(send_far, dhr))
    d1, da, dq, dkv, dkvr, vb = attend_back(0, d2, dh, after(dhr, r0f.keep, s10, n1))
    back = swap(dkvr, "c")
    n10 = r10.near(2, vb)
    far = after(far, n10)
    s0 = r0f.x_step(0, n10)
    low = join_rows(near, far)
    yt, yl, dxp, gbt, gbl = input_back(0, dq, dkv, after(back, s0, low))
    dxr = swap(dxp, "l")
    r00 = input_grads(0, da, yt, yl, va, vb, gbt, gbl, gut, gul)
    rest, first = Finish(y), Finish(y)
    y0 = rest.y_step(0, r0f.near(0, r00.keep), n0)
    dxr = after(dxr, y0)

    def sort(here, got, near, far, low):
        kept, sent = call(
            bind(sort_body, z), [sds((2 * R, W), BF), sds((2 * R + 16, W), BF)],
            here, got, near, far, low, meta=meta,
        )
        return kept, swap(sent, "c")

    def place(kept, sent):
        shape = layout_in.shape
        t, l_ = call(
            bind(place_body, z),
            [sds((1,) + text_in.shape, BF), sds((1, shape[0], shape[2], shape[1]), BF)],
            kept, sent, meta=meta,
        )
        return t, flip(l_)

    low = swap(after(low, dxr), "l")
    dhere, dpart, dsend, dsend_far = leave(True, d1, dxp, after(dxr, r00.keep), dx1)
    dgot, dnear, dfar = swap(dsend, "y"), swap(dpart, "h"), swap_both(dsend_far)
    other = rest.sum_of(0, dhere)
    r00.x_step(2, other)
    dgot, dnear, dfar, low, r00.far[2] = together(dgot, dnear, dfar, low, r00.far[2])
    dlow = swap(join_rows(dnear, dfar), "l")
    rest.last = swap(after(other, dlow), "h")
    r0f.x_step(1, dgot)
    first.y_step(2, r00.near(2, dgot), n10)
    dlow, r0f.far[1], first.cross[2] = together(dlow, r0f.far[1], first.cross[2])
    h1 = first.h_step()
    yf = rest.y_step(1, r0f.near(1), n1)
    dkept, dsent = sort(dhere, dgot, dnear, dfar, after(dlow, h1, yf))
    kept, sent = sort(here, got, near, far, after(low, dkept))
    own1 = first.close(kept)
    dx_t, dx_l = place(dkept, after(dsent, own1))
    res_t, res_l = place(kept, after(sent, dx_t))
    own2 = rest.close(res_t)
    like = lambda *arrays: [sds(v.shape, F32) for v in arrays]
    g_tup, g_lup, g_tdn, g_ldn = call(
        bind(finish_body, z), like(t_up, l_up, flip(t_down), flip(l_down)), *rest.terms(own2)
    )
    g_ti, g_tb, g_to, g_tg, g_ts, g_tu, g_li, g_lb, g_lo, g_lg, g_ls, g_lu = call(
        bind(finish_first_body, z),
        like(t_in, t_hb, t_out, t_gain, t_shift, t_ub, l_in, l_hb, l_out, l_gain, l_shift, l_ub),
        *first.terms(g_tup),
    )
    return (
        res_t, res_l, dx_t, dx_l,
        g_ti, g_tb, g_to, g_tg, g_ts, g_tup, g_tu, flip(g_tdn),
        g_li, g_lb, g_lo, g_lg, g_ls, g_lup, g_lu, flip(g_ldn),
    )


def solution(mesh):
    section, dp, tensor = (mesh.shape[a] for a in ("section", "dp", "tensor"))
    fine = Mesh(mesh.devices.reshape(section, dp // 2, 2, 2, tensor // 2), ALL)
    d, t = ("x", "c"), ("h", "l")
    weights = (
        P("y", None, d, t),
        P("y", None, t + d),
        P("y", t, d),
        P("y", None, d),
        P("y", None, d),
        P("y", d, t),
        P("y", t + d),
        P("y", t, d),
    ) * 2
    pages = (P(d, None, None), P(d, None, None))
    return jax.shard_map(
        per_device,
        mesh=fine,
        in_specs=pages + (P(d, None),) + pages + weights,
        out_specs=(P("y", d, None, None),) * 4 + weights,
        check_vma=False,
    )
```

```python
import functools

import jax
import jax.numpy as jnp
from jax import lax
from jax.experimental import pallas as pl
from jax.experimental.pallas import tpu as pltpu
from jax.sharding import Mesh, PartitionSpec as P

BF = jnp.bfloat16
F32 = jnp.float32
HEAD = 64
LHEAD = 16
SLOT = 128
GROUPS = 3
ALL = ("y", "x", "c", "h", "l")


def mm(a, b):
    return lax.dot_general(a, b, (((1,), (0,)), ((), ())), preferred_element_type=F32)


def mm_nt(a, b):
    return lax.dot_general(a, b, (((1,), (1,)), ((), ())), preferred_element_type=F32)


def mm_tn(a, b):
    return lax.dot_general(a, b, (((0,), (0,)), ((), ())), preferred_element_type=F32)


class Sizes:
    def __init__(self, text, layout, rd, ld, cols, lcols, dp):
        self.seq = text.shape[1]
        self.rows = self.seq // 2
        self.d = text.shape[2]
        self.ld = layout.shape[2]
        self.width = self.d + self.ld
        self.rd = rd
        self.lr = ld
        self.dp = dp
        self.quarter = cols
        self.lquarter = lcols
        self.heads = cols // HEAD
        self.block = rd + ld // GROUPS
        self.vblock = self.block + 16
        self.part = ld // GROUPS
        self.xs = dp // 2
        self.masks = 4 if self.xs == 2 else 2


def call(body, out_shapes, *args, scratch=(), meta=None, us=4):
    places = [pl.BlockSpec(memory_space=pltpu.VMEM)] * len(args)
    if meta is not None:
        args = (meta,) + args
        places = [pl.BlockSpec(memory_space=pltpu.SMEM)] + places
    return pl.pallas_call(
        body,
        out_shape=list(out_shapes),
        in_specs=places,
        out_specs=[pl.BlockSpec(memory_space=pltpu.VMEM)] * len(out_shapes),
        scratch_shapes=list(scratch),
        compiler_params=pltpu.CompilerParams(vmem_limit_bytes=56 * 2**20),
        cost_estimate=pl.CostEstimate(flops=int(us * 2.3e9), bytes_accessed=1000, transcendentals=0),
    )(*args)


def sds(shape, dtype):
    return jax.ShapeDtypeStruct(shape, dtype)


def text_w(w, h, z, lo=0, hi=None):
    return jnp.concatenate(
        [w[r % 2][r // 2, w[2](h), : z.rd, lo:hi] for r in range(z.dp)], axis=0
    )


def layout_w(w, h, z, lo=0, hi=None):
    width = w[0].shape[-1] // GROUPS
    hi = width if hi is None else hi
    pieces = []
    for r in range(z.dp):
        for k in range(GROUPS):
            rows = slice(z.rd, z.rd + z.part)
            pieces.append(w[r % 2][r // 2, w[2](h), rows, width * k + lo : width * k + hi])
    return jnp.concatenate(pieces, axis=0)


def alone(h):
    return h


def first_of_two(h):
    return 2 * h


def second_of_two(h):
    return 2 * h + 1


class Pick:
    def __init__(self, refs, core, piece):
        self.refs, self.core, self.piece = refs, core, piece
        self.shape = refs[core].shape

    def __getitem__(self, at):
        x, h, rows, cols = at
        if len(self.refs) == 4:
            return self.refs[2 * h + self.core][x, self.piece, rows, cols]
        return self.refs[self.core][x, 2 * h + self.piece, rows, cols]


def feed_forward(refs):
    return tuple((Pick(refs, 0, p), Pick(refs, 1, p), alone) for p in range(2))


def put_grads(g, h, text, layout, z):
    width = g[0].shape[-1] // GROUPS
    low = layout.astype(BF)
    pad = width - low.shape[-1]
    low = jnp.concatenate([low, jnp.zeros((low.shape[0], pad), BF)], axis=1)
    text = text.astype(BF)
    at = g[2](h)
    for r in range(z.dp):
        ref, x = g[r % 2], r // 2
        ref[x, at, : z.rd, :] = text[z.rd * r : z.rd * (r + 1)]
        for k in range(GROUPS):
            base = z.lr * r + z.part * k
            ref[x, at, z.rd : z.block, width * k : width * (k + 1)] = low[base : base + z.part]


def natural(pieces, m, z):
    out = []
    for d in range(z.dp):
        value = pieces[d]
        for other in range(1, z.masks):
            value = jnp.where(m == other, pieces[d ^ other], value)
        out.append(value)
    return jnp.concatenate(out, axis=1)


def norm_stats(resid):
    center = resid - jnp.mean(resid, axis=-1, keepdims=True)
    factor = lax.rsqrt(jnp.mean(center * center, axis=-1, keepdims=True) + 1e-05)
    return center * factor, factor


def norm_both(resid, z):
    nt, ft = norm_stats(resid[:, : z.d])
    nl, fl = norm_stats(resid[:, z.d :])
    return jnp.concatenate([nt, nl], axis=1), ft, fl


def norm_back(grad, normed, factor, gain):
    scaled = grad * gain
    return factor * (
        scaled
        - jnp.mean(scaled, axis=-1, keepdims=True)
        - normed * jnp.mean(scaled * normed, axis=-1, keepdims=True)
    )


def norm_back_both(grad, normed, ft, fl, gain, z):
    gt = norm_back(grad[:, : z.d], normed[:, : z.d], ft, gain[:, : z.d])
    gl = norm_back(grad[:, z.d :], normed[:, z.d :], fl, gain[:, z.d :])
    return jnp.concatenate([gt, gl], axis=1)


def small_rows(w, h, z):
    return [w[r % 2][r // 2, h, z.block : z.vblock, :].astype(F32) for r in range(z.dp)]


def qkv_body(z, fused, meta_ref, *refs):
    if fused:
        (hid_ref, own_ref, rec_ref, prev_ref, ws_ref, wc_ref,
         r_ref, x_ref, q_ref, kv_ref, vec_ref, ut_ref, ul_ref) = refs
        vec = prev_ref[...]
        resid = (
            hid_ref[...].astype(F32) + own_ref[...].astype(F32) + rec_ref[...].astype(F32) + vec[4:5]
        )
        r_ref[...] = resid
        normed, _, _ = norm_both(resid, z)
        x = (normed * vec[1:2] + vec[5:6]).astype(BF)
        x_ref[...] = x
    else:
        x_ref, far_ref, ws_ref, wc_ref, q_ref, kv_ref, kvr_ref, vec_ref, ut_ref, ul_ref = refs
        x = x_ref[...]
    w = (ws_ref, wc_ref, alone)
    mask = meta_ref[1]
    lane = 4 * SLOT
    small = small_rows(w, 0, z)
    vec_ref[:, : z.d] = jnp.concatenate([s[:, : z.rd] for s in small], axis=1)
    vec_ref[:, z.d :] = jnp.concatenate([s[:, lane : lane + z.lr] for s in small], axis=1)
    xt, xl = x[:, : z.d], x[:, z.d :]
    n, m = z.quarter, z.lquarter
    zeros = jnp.zeros((z.rows, SLOT - HEAD - LHEAD), BF)
    hb, lb, ub, vb = n // z.dp, m // z.dp, 4 * n // z.dp, 4 * m // z.dp

    def project(xt, xl, first, out_ref):
        yt = mm(xt, text_w(w, h, z, n * first, 3 * n)) + bt[:, n * first :]
        yl = mm(xl, layout_w(w, h, z, m * first, 3 * m)) + bl[:, m * first :]
        yt = yt.astype(BF)
        yl = yl.astype(BF)
        for s in range(first, 3):
            for j in range(z.heads):
                lo, llo = n * (s - first) + HEAD * j, m * (s - first) + LHEAD * j
                a = yt[:, lo : lo + HEAD]
                b = yl[:, llo : llo + LHEAD]
                if s == 0:
                    a = a * BF(HEAD**-0.5)
                    b = b * BF(LHEAD**-0.5)
                slot = jnp.concatenate([a, b, zeros], axis=1)
                head = z.heads * h + j
                if s == 0:
                    q_ref[head] = slot
                else:
                    out_ref[2 * z.heads * (s - 1) + head] = slot

    for h in range(2):
        small = small_rows(w, h, z)
        rows = lambda i, lo, size: natural([s[i : i + 1, lo : lo + size] for s in small], mask, z)
        ut_ref[h] = rows(8, 0, ub)
        ul_ref[h] = rows(8, lane, vb)
        bt = jnp.concatenate([rows(6, 0, hb), jnp.zeros((1, n), F32), rows(7, 0, hb)], axis=1)
        bl = jnp.concatenate(
            [rows(6, lane, lb), jnp.zeros((1, m), F32), rows(7, lane, lb)], axis=1
        )
        project(xt, xl, 0, kv_ref)
        if not fused:
            far = far_ref[...]
            project(far[:, : z.d], far[:, z.d :], 1, kvr_ref)


def attend_body(z, q_ref, own_ref, rec_ref, mask_ref, ws_ref, wc_ref, a_ref, c_ref, p_ref, s_ref):
    w = (ws_ref, wc_ref, alone)
    count = 2 * z.heads
    m0 = mask_ref[0:1, : z.rows] > 0
    m1 = mask_ref[0:1, z.rows :] > 0

    def head(j, carry):
        q = q_ref[j]
        s0 = jnp.where(m0, mm_nt(q, own_ref[j]), -1000000000.0)
        s1 = jnp.where(m1, mm_nt(q, rec_ref[j]), -1000000000.0)
        top = jnp.maximum(
            jnp.max(s0, axis=-1, keepdims=True), jnp.max(s1, axis=-1, keepdims=True)
        )
        e0 = jnp.exp(s0 - top)
        e1 = jnp.exp(s1 - top)
        inv = 1.0 / (jnp.sum(e0, axis=-1, keepdims=True) + jnp.sum(e1, axis=-1, keepdims=True))
        p0 = (e0 * inv).astype(BF)
        p1 = (e1 * inv).astype(BF)
        p_ref[j, :, : z.rows] = p0
        p_ref[j, :, z.rows :] = p1
        s_ref[j] = (mm(p0, own_ref[count + j]) + mm(p1, rec_ref[count + j])).astype(BF)
        return carry

    lax.fori_loop(0, count, head, 0, unroll=True)
    n, m = z.quarter, z.lquarter
    at = al = None
    for h in range(2):
        heads = [s_ref[z.heads * h + j] for j in range(z.heads)]
        ct = jnp.concatenate([s[:, :HEAD] for s in heads], axis=1)
        cl = jnp.concatenate([s[:, HEAD : HEAD + LHEAD] for s in heads], axis=1)
        c_ref[h, :, :n] = ct
        c_ref[h, :, 2 * SLOT : 2 * SLOT + m] = cl
        pt = mm_nt(ct, text_w(w, h, z, 3 * n, 4 * n))
        pll = mm_nt(cl, layout_w(w, h, z, 3 * m, 4 * m))
        at = pt if at is None else at + pt
        al = pll if al is None else al + pll
    a_ref[:, : z.d] = at.astype(BF)
    a_ref[:, z.d :] = al.astype(BF)


def gelu_parts(u):
    cdf = 0.5 * (1.0 + lax.erf(u * 0.7071067811865476))
    slope = cdf + u * jnp.exp(-0.5 * u * u) * 0.3989422804014327
    return (u * cdf).astype(BF), slope.astype(BF)


def forward_body(
    z, x_ref, own_ref, rec_ref, vec_ref, bt_ref, bl_ref, *refs
):
    r_ref, hid_ref, gt_ref, gl_ref, st_ref, sl_ref, f_ref = refs[-7:]
    up, down = feed_forward(refs[:-7])
    lw = 4 * z.lquarter
    vec = vec_ref[...]
    resid = x_ref[...].astype(F32) + own_ref[...].astype(F32) + rec_ref[...].astype(F32) + vec[2:3]
    r_ref[...] = resid
    normed, _, _ = norm_both(resid, z)
    hid = (normed * vec[0:1] + vec[3:4]).astype(BF)
    hid_ref[...] = hid
    ht, hl = hid[:, : z.d], hid[:, z.d :]
    ft = fl = None
    for h in range(2):
        g, s = gelu_parts(mm(ht, text_w(up, h, z)) + bt_ref[h])
        gt_ref[h] = g
        st_ref[h] = s
        p = mm_nt(g, text_w(down, h, z))
        ft = p if ft is None else ft + p
        g, s = gelu_parts(mm(hl, layout_w(up, h, z, 0, lw)) + bl_ref[h])
        gl_ref[h] = g
        sl_ref[h] = s
        p = mm_nt(g, layout_w(down, h, z, 0, lw))
        fl = p if fl is None else fl + p
    f_ref[:, : z.d] = ft.astype(BF)
    f_ref[:, z.d :] = fl.astype(BF)


def col_sum(value):
    return jnp.sum(value, axis=0, keepdims=True)


def tail_body(z, fused, *refs):
    if fused == "last":
        hid_ref, own_ref, rec_ref, go_ref, vec_ref, st_ref, sl_ref = refs[:7]
        ws = refs[7:-9]
        out_ref, d2_ref, df_ref, dut_ref, dul_ref, dh_ref, vg_ref, gbt_ref, gbl_ref = refs[-9:]
        vec = vec_ref[...]
        resid = (
            hid_ref[...].astype(F32) + own_ref[...].astype(F32) + rec_ref[...].astype(F32) + vec[4:5]
        )
        normed, ft, fl = norm_both(resid, z)
        out_ref[...] = (normed * vec[1:2] + vec[5:6]).astype(BF)
        go = go_ref[...].astype(F32)
    else:
        r_ref, d1_ref, own_ref, rec_ref, vec_ref, st_ref, sl_ref = refs[:7]
        ws = refs[7:-9]
        dx_ref, d2_ref, df_ref, dut_ref, dul_ref, dh_ref, vg_ref, gbt_ref, gbl_ref = refs[-9:]
        vec = vec_ref[...]
        normed, ft, fl = norm_both(r_ref[...], z)
        low = (d1_ref[...] + own_ref[...].astype(F32) + rec_ref[...].astype(F32)).astype(BF)
        dx_ref[...] = low
        go = low.astype(F32)
    up, down = feed_forward(ws)
    lw = 4 * z.lquarter
    d2 = norm_back_both(go, normed, ft, fl, vec[1:2], z)
    d2_ref[...] = d2
    df = d2.astype(BF)
    df_ref[...] = df
    vg_ref[0:1] = col_sum(go * normed)
    vg_ref[1:2] = col_sum(go)
    vg_ref[2:3] = col_sum(df.astype(F32))
    vg_ref[3:8] = jnp.zeros((5, z.width), F32)
    dft, dfl = df[:, : z.d], df[:, z.d :]
    ht = hl = None
    for h in range(2):
        du = (mm(dft, text_w(down, h, z)) * st_ref[h].astype(F32)).astype(BF)
        dut_ref[h] = du
        gbt_ref[h] = col_sum(du.astype(F32))
        p = mm_nt(du, text_w(up, h, z))
        ht = p if ht is None else ht + p
        du = (mm(dfl, layout_w(down, h, z, 0, lw)) * sl_ref[h].astype(F32)).astype(BF)
        dul_ref[h] = du
        gbl_ref[h] = col_sum(du.astype(F32))
        p = mm_nt(du, layout_w(up, h, z, 0, lw))
        hl = p if hl is None else hl + p
    dh_ref[:, : z.d] = ht.astype(BF)
    dh_ref[:, z.d :] = hl.astype(BF)


def ffn_grads_body(z, hid_ref, df_ref, gt_ref, gl_ref, dut_ref, dul_ref, g_ref, h_ref):
    one, two = (g_ref, h_ref, first_of_two), (g_ref, h_ref, second_of_two)
    hid, df = hid_ref[...], df_ref[...]

    def quarter(h, carry):
        put_grads(one, h, mm_tn(hid[:, : z.d], dut_ref[h]), mm_tn(hid[:, z.d :], dul_ref[h]), z)
        put_grads(two, h, mm_tn(df[:, : z.d], gt_ref[h]), mm_tn(df[:, z.d :], gl_ref[h]), z)
        return carry

    lax.fori_loop(0, 2, quarter, 0)


def attend_back_body(
    z, d2_ref, own_ref, rec_ref, r_ref, vec_ref, ws_ref, wc_ref, c_ref, q_ref, kv_ref, kvr_ref, p_ref, mask_ref,
    d1_ref, da_ref, dq_ref, dkv_ref, dkvr_ref, vg_ref, dc_ref, dd_ref,
):
    count = 2 * z.heads
    w = (ws_ref, wc_ref, alone)
    vec = vec_ref[...]
    dh = d2_ref[...] + own_ref[...].astype(F32) + rec_ref[...].astype(F32)
    normed, ft, fl = norm_both(r_ref[...], z)
    d1 = norm_back_both(dh, normed, ft, fl, vec[0:1], z)
    d1_ref[...] = d1
    da = d1.astype(BF)
    da_ref[...] = da
    vg_ref[0:1] = col_sum(dh * normed)
    vg_ref[1:2] = col_sum(dh)
    vg_ref[2:3] = col_sum(da.astype(F32))
    vg_ref[3:8] = jnp.zeros((5, z.width), F32)
    n, m = z.quarter, z.lquarter
    zeros = jnp.zeros((z.rows, SLOT - HEAD - LHEAD), BF)
    for h in range(2):
        dct = mm(da[:, : z.d], text_w(w, h, z, 3 * n, 4 * n)).astype(BF)
        dcl = mm(da[:, z.d :], layout_w(w, h, z, 3 * m, 4 * m)).astype(BF)
        for j in range(z.heads):
            a = dct[:, HEAD * j : HEAD * (j + 1)]
            b = dcl[:, LHEAD * j : LHEAD * (j + 1)]
            dc_ref[z.heads * h + j] = jnp.concatenate([a, b, zeros], axis=1)
            ct = c_ref[h, :, HEAD * j : HEAD * (j + 1)].astype(F32)
            cl = c_ref[h, :, 2 * SLOT + LHEAD * j : 2 * SLOT + LHEAD * (j + 1)].astype(F32)
            dt = jnp.sum(a.astype(F32) * ct, axis=-1, keepdims=True)
            dl = jnp.sum(b.astype(F32) * cl, axis=-1, keepdims=True)
            dd_ref[z.heads * h + j, :, 0:1] = dt
            dd_ref[z.heads * h + j, :, 1:2] = dt + dl
    lane = lax.broadcasted_iota(jnp.int32, (z.rows, SLOT), 1)
    text_lane = lane < HEAD
    scale = jnp.where(text_lane, HEAD**-0.5, LHEAD**-0.5)
    mask = mask_ref[...]
    masks = (mask[:, : z.rows].astype(BF), mask[:, z.rows :].astype(BF))

    def head(j, carry):
        dc = dc_ref[j]
        dct = jnp.where(text_lane, dc, jnp.zeros_like(dc))
        q = q_ref[j]
        dt = dd_ref[j, :, 0:1]
        ds = dd_ref[j, :, 1:2]
        dq_t = dq_s = None
        for i, (k_ref, o_ref) in enumerate(((kv_ref, dkv_ref), (kvr_ref, dkvr_ref))):
            k = k_ref[j]
            v = k_ref[count + j]
            prob = p_ref[j, :, z.rows * i : z.rows * (i + 1)]
            pm = prob * masks[i]
            st = pm * (mm_nt(dct, v) - dt).astype(BF)
            ss = pm * (mm_nt(dc, v) - ds).astype(BF)
            a = mm(st, k)
            b = mm(ss, k)
            dq_t = a if dq_t is None else dq_t + a
            dq_s = b if dq_s is None else dq_s + b
            dk = jnp.where(text_lane, mm_tn(st, q), mm_tn(ss, q))
            o_ref[j] = dk.astype(BF)
            o_ref[count + j] = mm_tn(prob, dc).astype(BF)
        dq_ref[j] = (jnp.where(text_lane, dq_t, dq_s) * scale).astype(BF)
        return carry

    lax.fori_loop(0, count, head, 0, unroll=True)


def input_back_body(z, dq_ref, dkv_ref, rec_ref, ws_ref, wc_ref, yt_ref, yl_ref, dx_ref, gbt_ref, gbl_ref):
    count = 2 * z.heads
    w = (ws_ref, wc_ref, alone)
    n, m = z.quarter, z.lquarter
    xt = xl = None
    for h in range(2):
        ts, ls = [], []
        for s in range(3):
            for j in range(z.heads):
                head = z.heads * h + j
                if s == 0:
                    slot = dq_ref[head]
                else:
                    at = count * (s - 1) + head
                    slot = (dkv_ref[at].astype(F32) + rec_ref[at].astype(F32)).astype(BF)
                ts.append(slot[:, :HEAD])
                ls.append(slot[:, HEAD : HEAD + LHEAD])
        yt = jnp.concatenate(ts, axis=1)
        yl = jnp.concatenate(ls, axis=1)
        yt_ref[h] = yt
        yl_ref[h] = yl
        gbt_ref[h] = col_sum(yt.astype(F32))
        gbl_ref[h] = col_sum(yl.astype(F32))
        p = mm_nt(yt, text_w(w, h, z, 0, 3 * n))
        xt = p if xt is None else xt + p
        p = mm_nt(yl, layout_w(w, h, z, 0, 3 * m))
        xl = p if xl is None else xl + p
    dx_ref[:, : z.d] = xt.astype(BF)
    dx_ref[:, z.d :] = xl.astype(BF)


def input_grads_body(
    z, meta_ref, x_ref, da_ref, c_ref, yt_ref, yl_ref, va_ref, vb_ref, bt_ref, bl_ref, ut_ref, ul_ref,
    g_ref, h_ref, s_ref,
):
    g = (g_ref, h_ref, alone)
    x, da = x_ref[...], da_ref[...]
    n, m = z.quarter, z.lquarter
    va, vb = va_ref[...], vb_ref[...]
    mask = meta_ref[1]
    rows = (vb[0:1], va[0:1], vb[2:3], vb[1:2], va[2:3], va[1:2])
    lane = 4 * SLOT
    s_ref[...] = jnp.zeros_like(s_ref)

    def relative(value, size):
        parts = [value[:, size * d : size * (d + 1)] for d in range(z.dp)]
        out = []
        for r in range(z.dp):
            v = parts[r]
            for other in range(1, z.masks):
                v = jnp.where(mask == other, parts[r ^ other], v)
            out.append(v)
        return out

    def quarter(h, carry):
        ct = c_ref[h, :, :n]
        cl = c_ref[h, :, 2 * SLOT : 2 * SLOT + m]
        text = jnp.concatenate(
            [mm_tn(x[:, : z.d], yt_ref[h]), mm_tn(da[:, : z.d], ct)], axis=1
        )
        layout = jnp.concatenate(
            [mm_tn(x[:, z.d :], yl_ref[h]), mm_tn(da[:, z.d :], cl)], axis=1
        )
        put_grads(g, h, text, layout, z)
        bt, bl, ut, ul = bt_ref[h], bl_ref[h], ut_ref[h], ul_ref[h]
        entries = [
            (6, 0, relative(bt[:, :n], n // z.dp)),
            (7, 0, relative(bt[:, 2 * n :], n // z.dp)),
            (6, lane, relative(bl[:, :m], m // z.dp)),
            (7, lane, relative(bl[:, 2 * m :], m // z.dp)),
            (8, 0, relative(ut, 4 * n // z.dp)),
            (8, lane, relative(ul, 4 * m // z.dp)),
        ]
        for r in range(z.dp):
            for i, row in enumerate(rows):
                s_ref[i : i + 1, : z.rd] = row[:, z.rd * r : z.rd * (r + 1)]
                s_ref[i : i + 1, lane : lane + z.lr] = row[
                    :, z.d + z.lr * r : z.d + z.lr * (r + 1)
                ]
            for at, lo, values in entries:
                s_ref[at : at + 1, lo : lo + values[r].shape[1]] = values[r]
            g[r % 2][r // 2, h, z.block : z.vblock, :] = s_ref[...].astype(BF)
        return carry

    lax.fori_loop(0, 2, quarter, 0)


def put_pack(out_ref, text, layout, z):
    out_ref[: z.rd, :] = text.astype(BF)
    width = out_ref.shape[-1] // GROUPS
    low = layout.astype(BF)
    low = jnp.concatenate([low, jnp.zeros((low.shape[0], width - low.shape[1]), BF)], axis=1)
    for k in range(GROUPS):
        out_ref[z.rd : z.block, width * k : width * (k + 1)] = low[z.part * k : z.part * (k + 1)]


def pack_first_body(
    z, ti_ref, to_ref, li_ref, lo_ref, tg_ref, lg_ref, ts_ref, ls_ref, tb_ref, lb_ref, tu_ref, lu_ref,
    out_ref, s_ref,
):
    text = jnp.concatenate([ti_ref[0, 0], ti_ref[0, 1], ti_ref[0, 2], to_ref[0].T], axis=1)
    layout = jnp.concatenate([li_ref[0, 0], li_ref[0, 1], li_ref[0, 2], lo_ref[0].T], axis=1)
    put_pack(out_ref, text, layout, z)
    s_ref[...] = jnp.zeros_like(s_ref)
    for lane, refs in ((0, (tg_ref, ts_ref, tb_ref)), (4 * SLOT, (lg_ref, ls_ref, lb_ref))):
        at = 0
        for ref in refs:
            count, width = ref.shape[1], ref.shape[2]
            s_ref[at : at + count, lane : lane + width] = ref[0]
            at += count
    s_ref[8:9, : tu_ref.shape[1]] = tu_ref[...]
    s_ref[8:9, 4 * SLOT : 4 * SLOT + lu_ref.shape[1]] = lu_ref[...]
    out_ref[z.block : z.vblock, :] = s_ref[...].astype(BF)


def pack_rest_body(z, tu_ref, lu_ref, td_ref, ld_ref, out_ref):
    put_pack(out_ref.at[0], tu_ref[0], lu_ref[0], z)
    put_pack(out_ref.at[1], td_ref[0], ld_ref[0], z)


def take_layout(total, cols, z):
    width = total.shape[-1] // GROUPS
    return jnp.concatenate(
        [total[z.rd : z.block, width * k : width * k + cols] for k in range(GROUPS)], axis=0
    )


def final_sum(refs):
    return sum(r[...].astype(F32) for r in refs)


def finish_first_body(z, *refs):
    (ti_ref, tb_ref, to_ref, tg_ref, ts_ref, tu_ref,
     li_ref, lb_ref, lo_ref, lg_ref, ls_ref, lu_ref) = refs[2:]
    total = final_sum(refs[:2])[0]
    n, m = z.quarter, z.lquarter
    layout = take_layout(total, 4 * m, z)
    for s in range(3):
        ti_ref[0, s] = total[: z.rd, n * s : n * (s + 1)]
        li_ref[0, s] = layout[:, m * s : m * (s + 1)]
    to_ref[0] = total[: z.rd, 3 * n :].T
    lo_ref[0] = layout[:, 3 * m :].T
    rows = total[z.block : z.vblock]
    for lane, group in ((0, (tg_ref, ts_ref, tb_ref)), (4 * SLOT, (lg_ref, ls_ref, lb_ref))):
        at = 0
        for ref in group:
            count, width = ref.shape[1], ref.shape[2]
            ref[0] = rows[at : at + count, lane : lane + width]
            at += count
    tu_ref[...] = rows[8:9, : tu_ref.shape[1]]
    lu_ref[...] = rows[8:9, 4 * SLOT : 4 * SLOT + lu_ref.shape[1]]


def finish_body(z, *refs):
    total = final_sum(refs[:2])
    for p in range(2):
        t_ref, l_ref = refs[2 + 2 * p : 4 + 2 * p]
        t_ref[0] = total[p, : z.rd]
        l_ref[0] = take_layout(total[p], 4 * z.lquarter, z)


def entry_body(z, meta_ref, t_ref, l_ref, tc_ref, lc_ref, mask_ref, own_ref, send_ref):
    y, c = meta_ref[0], meta_ref[2]
    row = jnp.where(y == 0, mask_ref[0:1, :], mask_ref[1:2, :]).astype(F32)
    left, right = row[:, : z.rows], row[:, z.rows :]
    for ref, half in ((own_ref, c), (send_ref, 1 - c)):
        for i, (text, layout) in enumerate(((t_ref, l_ref), (t_ref, l_ref), (tc_ref, lc_ref))):
            part = 1 - half if i == 1 else half
            rows = pl.ds(pl.multiple_of(part * z.rows, z.rows), z.rows)
            out = slice(z.rows * i, z.rows * (i + 1))
            ref[out, : z.d] = text[y, rows, :]
            ref[out, z.d :] = layout[y, :, rows].astype(F32).T.astype(BF)
        near = jnp.where(half == 0, left, right)
        far = jnp.where(half == 0, right, left)
        low = jnp.concatenate([near, far, jnp.zeros((1, z.width - z.seq), F32)], axis=1)
        ref[3 * z.rows :, :] = jnp.broadcast_to(low, (16, z.width)).astype(BF)


def ordered(value, m, z):
    text = [value[:, z.rd * r : z.rd * (r + 1)] for r in range(z.dp)]
    layout = [value[:, z.d + z.lr * r : z.d + z.lr * (r + 1)] for r in range(z.dp)]
    return jnp.concatenate([natural(text, m, z), natural(layout, m, z)], axis=1)


def settle_body(z, meta_ref, own_ref, got_ref, x_ref, far_ref, cot_ref, out_ref):
    mine = meta_ref[3] == 1
    mask = meta_ref[1]
    step = z.rows // 4

    def chunk(k, carry):
        rows = pl.ds(pl.multiple_of(k * step, step), step)
        for i, ref in enumerate((x_ref, far_ref, cot_ref)):
            at = pl.ds(pl.multiple_of(z.rows * i + k * step, step), step)
            ref[rows, :] = ordered(jnp.where(mine, own_ref[at, :], got_ref[at, :]), mask, z)
        return carry

    lax.fori_loop(0, 4, chunk, 0)
    last = slice(3 * z.rows, 3 * z.rows + 16)
    row = jnp.where(mine, own_ref[last, : z.seq], got_ref[last, : z.seq])
    out_ref[...] = row.astype(F32)[0:1]


def exit_body(z, summed, meta_ref, *refs):
    if summed:
        d_ref, own_ref, rec_ref, b_ref, here_ref, part_ref, send_ref, far_ref = refs
    else:
        a_ref, b_ref, here_ref, part_ref, send_ref, far_ref = refs
    first = meta_ref[0] == 0
    low = meta_ref[4] == 0
    mask = meta_ref[1]
    half = z.rows // 2
    pieces = 1 if summed else 4
    step = z.rows // pieces

    def chunk(k, carry):
        rows = pl.ds(pl.multiple_of(k * step, step), step) if pieces > 1 else slice(None)
        two = b_ref[rows, :]
        if summed:
            one = d_ref[rows, :] + own_ref[rows, :].astype(F32) + rec_ref[rows, :].astype(F32)
            one = one.astype(BF)
        else:
            one = a_ref[rows, :]
        here_ref[rows, :] = ordered(jnp.where(first, one, two), mask, z)
        send_ref[rows, :] = ordered(jnp.where(first, two, one), mask, z)
        return carry

    lax.fori_loop(0, pieces, chunk, 0)
    part_ref[...] = jnp.where(low, here_ref[:half, :], here_ref[half:, :])
    far_ref[...] = jnp.where(low, send_ref[:half, :], send_ref[half:, :])


def sort_body(z, meta_ref, here_ref, got_ref, b_ref, d_ref, far_ref, keep_ref, send_ref):
    mine = meta_ref[3] == 1
    low = meta_ref[4] == 0
    half = z.rows // 2
    for i, (same_ref, near_ref) in enumerate(((here_ref, b_ref), (got_ref, d_ref))):
        beyond = far_ref[half * i : half * (i + 1), :]
        for k in range(2):
            rows = slice(half * k, half * (k + 1))
            other = jnp.where(low == (k == 0), near_ref[...], beyond)
            same = same_ref[rows, :]
            rows = slice(z.rows * i + half * k, z.rows * i + half * (k + 1))
            keep_ref[rows, :] = jnp.where(mine, same, other)
            send_ref[rows, :] = jnp.where(mine, other, same)
    send_ref[2 * z.rows :, :] = jnp.zeros((16, z.width), BF)


def place_body(z, meta_ref, keep_ref, got_ref, t_ref, l_ref):
    y, c = meta_ref[0], meta_ref[2]
    for i in range(2):
        page = y if i == 0 else 1 - y
        for ref, half in ((keep_ref, c), (got_ref, 1 - c)):
            rows = pl.ds(pl.multiple_of(half * z.rows, z.rows), z.rows)
            value = ref[z.rows * i : z.rows * (i + 1), :]
            t_ref[0, page, rows, :] = value[:, : z.d]
            l_ref[0, page, :, rows] = value[:, z.d :].astype(F32).T.astype(BF)


def swap(value, axis):
    return lax.ppermute(value, axis, [(0, 1), (1, 0)])


def after(value, *others):
    return lax.optimization_barrier((value,) + others)[0]


def together(*values):
    return lax.optimization_barrier(values)


def swap_both(value):
    return lax.ppermute(value, ("y", "h"), [(0, 3), (1, 2), (2, 1), (3, 0)])


def join_rows(*parts):
    return jnp.concatenate(parts + (jnp.zeros((16, parts[0].shape[1]), BF),), axis=0)


def join_blocks(parts, got):
    own = jnp.stack([jnp.concatenate(parts), jnp.concatenate(got)])
    return own, swap(own, "c")


def gather_blocks(parts, x_size, *token):
    if x_size == 2:
        return join_blocks(parts, [after(swap(v, "x"), *token) for v in parts])
    else:
        own = lax.all_gather(jnp.concatenate(parts), "x", axis=0)
    return own, swap(own, "c")


def add_low(*terms):
    total = terms[0].astype(F32)
    for term in terms[1:]:
        total = total + term.astype(F32)
    return total.astype(BF)


class Reduce:
    def __init__(self, keep, send, x_size, *token):
        self.keep, self.x_size = keep, x_size
        half = keep.shape[1] // 2
        self.rows = (slice(half, None), slice(0, half), slice(None))
        self.got = swap(after(send, *token) if token else send, "c")
        self.far = {}

    def x_step(self, part, *token):
        got, rows = after(self.got, *token), self.rows[part]
        if self.x_size == 2:
            total = add_low(self.keep[1, rows], got[1, rows])
            self.far[part] = swap(total, "x")
        else:
            total = add_low(self.keep[:, rows], got[:, rows])
            self.far[part] = lax.psum_scatter(total, "x", scatter_dimension=0, tiled=False)
        return total

    def near(self, part, *token):
        rows = self.rows[part]
        if part in self.far:
            far = after(self.far[part], *token)
        else:
            far = after(self.far[2], *token)[rows]
        if self.x_size == 2:
            far = add_low(self.keep[0, rows], self.got[0, rows], far)
        return far


class Finish:
    def __init__(self, y):
        self.y, self.here, self.cross = y, {}, {}

    def y_step(self, part, first, second):
        self.here[part] = jnp.where(self.y == 0, first, second)
        self.cross[part] = swap(jnp.where(self.y == 0, second, first), "y")
        return self.here[part]

    def sum_of(self, part, *token):
        if part in self.here:
            return add_low(self.here[part], after(self.cross[part], *token))
        half = self.here[2].shape[0] // 2
        rows = slice(half, None) if part == 0 else slice(0, half)
        return add_low(self.here[2][rows], after(self.cross[2], *token)[rows])

    def h_step(self, *token):
        other = self.sum_of(0, *token)
        self.last = swap(other, "h")
        return other

    def close(self, *token):
        self.own = self.sum_of(1, *token)
        return self.own

    def terms(self, *token):
        return (self.own, after(self.last, *token))


def per_device(
    text_in, layout_in, token_mask, text_cotangent, layout_cotangent,
    t_in, t_hb, t_out, t_gain, t_shift, t_up, t_ub, t_down,
    l_in, l_hb, l_out, l_gain, l_shift, l_up, l_ub, l_down,
):
    x_size = lax.axis_size("x")
    y, x, c, h, l = (lax.axis_index(a) for a in ALL)
    z = Sizes(
        text_in, layout_in, t_in.shape[2], l_in.shape[2], t_in.shape[3], l_in.shape[3], 2 * x_size
    )
    order = 2 * x + c if x_size == 2 else c
    meta = jnp.stack([y, order, c, (c == h).astype(jnp.int32), l, 0 * y, 0 * y, 0 * y])
    bind = functools.partial
    cols = t_up.shape[2]

    R, W, Q, M = z.rows, z.width, 4 * z.quarter, 4 * z.lquarter
    nh = 2 * z.heads
    flip = lambda v: jnp.swapaxes(v, -1, -2)

    (first,) = call(
        bind(pack_first_body, z), [sds((z.vblock, cols), BF)],
        t_in, t_out, l_in, l_out, t_gain, l_gain, t_shift, l_shift, t_hb, l_hb, t_ub, l_ub,
        scratch=[pltpu.VMEM((16, cols), F32)],
    )
    (rest,) = call(
        bind(pack_rest_body, z), [sds((2, z.block, cols), BF)],
        after(t_up, first), l_up, flip(t_down), flip(l_down), us=10,
    )
    own, send = call(
        bind(entry_body, z), [sds((3 * R + 16, W), BF)] * 2,
        after(text_in, rest), flip(layout_in), text_cotangent, flip(layout_cotangent), token_mask,
        meta=meta, us=10,
    )
    first = first[None]

    first_h = swap(first, "h")
    first_y = after(swap(first, "y"), rest, own)
    pick = lambda index, mine, across: jnp.where(y == index, mine, across)
    a0 = pick(0, first, first_y)
    rest_h = swap(after(rest, a0), "h")
    got = after(swap(send, "c"), a0)
    x0, far0, cot, mask = call(
        bind(settle_body, z), [sds((R, W), BF)] * 3 + [sds((1, z.seq), F32)], own, got, meta=meta, us=10,
    )
    first_h = after(first_h, x0)
    rest_y = after(swap(rest, "y"), first_h)
    f0 = pick(0, rest, rest_y)
    first_hy = swap(first_h, "y")
    rest_h = after(rest_h, first_h, f0)
    a1 = pick(0, first_h, after(first_hy, rest_h))
    parts_hy = [swap(rest_h[p : p + 1], "y") for p in range(2)]
    if x_size == 2:
        far_a = [swap(a0, "x"), swap(a1, "x")]
        far_f0 = swap(f0, "x")
        far_a[0] = after(far_a[0], far_a[1], far_f0, *parts_hy)
        weights = [[join_blocks([a0, a1], far_a)], []]
    else:
        weights = [[gather_blocks([a0, a1], x_size)], []]
    tokens = weights[0][0][0]
    f1 = pick(0, rest_h[0:1], after(parts_hy[0], tokens))
    f2 = pick(0, rest_h[1:2], after(parts_hy[1], tokens))
    x0 = after(x0, f1, f2)

    q_shapes = [sds((nh, R, SLOT), BF), sds((2 * nh, R, SLOT), BF)]
    v_shapes = [sds((16, W), F32), sds((2, 1, Q), F32), sds((2, 1, M), F32)]
    saved = []
    inner = None
    for index in range(2):
        w0 = weights[index][0]
        if index == 0:
            q, kv, kvr, vec, ut, ul = call(
                bind(qkv_body, z, False), q_shapes + q_shapes[1:] + v_shapes, x0, far0, *w0, meta=meta
            )
            xin = x0
        else:
            r2, xin, q, kv, vec, ut, ul = call(
                bind(qkv_body, z, True),
                [sds((R, W), F32), sds((R, W), BF)] + q_shapes + v_shapes,
                *inner, saved[0]["vec"], *w0, meta=meta,
            )
            saved[0]["r2"] = r2
            kvr = swap(kv, "c")
        a, ctx, prob = call(
            bind(attend_body, z),
            [sds((R, W), BF), sds((2, R, 3 * SLOT), BF), sds((nh, R, z.seq), BF)],
            q, kv, kvr, mask, *w0, scratch=[pltpu.VMEM((nh, R, SLOT), BF)], us=8,
        )
        ar = swap(a, "l")
        if index == 0:
            if x_size == 2:
                got = [after(swap(v, "x"), a) for v in (f1, f2)]
                weights[0].append(join_blocks([f0, f1, f2], [far_f0] + got))
            else:
                weights[0].append(gather_blocks([f0, f1, f2], x_size))
            token = weights[0][1][0]
            second = jnp.concatenate([pick(1, first, first_y), pick(1, after(first_h, token), first_hy)])
            got = swap(second, "x") if x_size == 2 else None
            if x_size == 2:
                ar = after(ar, got)
                weights[1].append(join_blocks([second], [got]))
            else:
                weights[1].append(gather_blocks([second], x_size))
            halves = [
                pick(1, after(rest, token), rest_y),
                jnp.concatenate(
                    [pick(1, after(rest_h, token)[p : p + 1], parts_hy[p]) for p in range(2)]
                ),
            ]
        if index == 1:
            if x_size == 2:
                far1 = swap(halves[1], "x")
                far1, ar = together(far1, ar)
                weights[1].append(near_blocks + join_blocks(halves[1:], [far1]))
            else:
                weights[1].append(gather_blocks(halves, x_size))
        r1, hid, gt, gl, st, sl, f = call(
            bind(forward_body, z),
            [sds((R, W), F32), sds((R, W), BF), sds((2, R, Q), BF), sds((2, R, M), BF),
             sds((2, R, Q), BF), sds((2, R, M), BF), sds((R, W), BF)],
            xin, a, ar, vec, ut, ul, *weights[index][1], us=6,
        )
        fr = swap(f, "l")
        if index == 0 and x_size == 2:
            far_half = swap(after(halves[0], ar), "x")
            fr = after(fr, far_half)
            near_blocks = join_blocks(halves[:1], [far_half])
        inner = (hid, f, fr)
        saved.append(dict(x=xin, q=q, kv=kv, kvr=kvr, ctx=ctx, prob=prob, r1=r1, hid=hid, gt=gt,
                          gl=gl, st=st, sl=sl, vec=vec))

    gshape = sds((x_size, 4, z.block, cols), BF)
    vshape = sds((x_size, 2, z.vblock, cols), BF)

    def tail(index, *args):
        keep = saved[index]
        shapes = [sds((R, W), BF), sds((R, W), F32), sds((R, W), BF), sds((2, R, Q), BF),
                  sds((2, R, M), BF), sds((R, W), BF), sds((8, W), F32), sds((2, 1, Q), F32),
                  sds((2, 1, M), F32)]
        return call(
            bind(tail_body, z, "last" if index == 1 else "mid"), shapes,
            *args, keep["vec"], keep["st"], keep["sl"], *weights[index][1], us=7,
        )

    def ffn_grads(index, df, dut, dul, *token):
        keep = saved[index]
        g, s = call(
            bind(ffn_grads_body, z), [gshape] * 2,
            keep["hid"], df, keep["gt"], keep["gl"], dut, dul, us=6,
        )
        return Reduce(g, s, x_size, *token)

    def attend_back(index, d2, dh, dhr):
        keep = saved[index]
        return call(
            bind(attend_back_body, z),
            [sds((R, W), F32), sds((R, W), BF), q_shapes[0], q_shapes[1], q_shapes[1], sds((8, W), F32)],
            d2, dh, dhr, keep["r1"], keep["vec"], *weights[index][0], keep["ctx"], keep["q"],
            keep["kv"], keep["kvr"], keep["prob"], mask,
            scratch=[pltpu.VMEM((nh, R, SLOT), BF), pltpu.VMEM((nh, R, SLOT), F32)], us=14,
        )

    def input_back(index, dq, dkv, back):
        return call(
            bind(input_back_body, z),
            [sds((2, R, 3 * z.quarter), BF), sds((2, R, 3 * z.lquarter), BF), sds((R, W), BF),
             sds((2, 1, 3 * z.quarter), F32), sds((2, 1, 3 * z.lquarter), F32)],
            dq, dkv, back, *weights[index][0],
        )

    def input_grads(index, *args):
        keep = saved[index]
        g0, s0 = call(
            bind(input_grads_body, z), [vshape] * 2, keep["x"], args[0], keep["ctx"], *args[1:],
            scratch=[pltpu.VMEM((16, cols), F32)], meta=meta,
        )
        return Reduce(g0, s0, x_size)

    def leave(summed, *args):
        return call(
            bind(exit_body, z, summed),
            [sds((R, W), BF), sds((R // 2, W), BF), sds((R, W), BF), sds((R // 2, W), BF)], *args,
            meta=meta,
        )

    out, d2, df, dut, dul, dh, va, gut, gul = tail(1, *inner, cot)
    dhr = swap(dh, "l")
    r1f = ffn_grads(1, df, dut, dul, dhr)
    here, part, send, send_far = leave(False, xin, after(out, r1f.keep))
    d1, da, dq, dkv, dkvr, vb = attend_back(1, d2, dh, after(dhr, r1f.keep, here))
    back = swap(dkvr, "c")
    s0 = r1f.x_step(0, vb)
    yt, yl, dxp, gbt, gbl = input_back(1, dq, dkv, after(back, s0))
    dxr = swap(dxp, "l")
    r10 = input_grads(1, da, yt, yl, va, vb, gbt, gbl, gut, gul)
    got, near = swap(after(send, dxp), "y"), swap(after(part, dxp), "h")
    n0 = r1f.near(0, r10.keep)
    s1 = r1f.x_step(1, n0)
    near = after(near, s1)
    got = after(got, near)

    dx1, d2, df, dut, dul, dh, va, gut, gul = tail(
        0, saved[0]["r2"], d1, dxp, after(dxr, r10.keep, n0, s1, got)
    )
    dhr = swap(dh, "l")
    r0f = ffn_grads(0, df, dut, dul)
    n1 = r1f.near(1, r0f.keep)
    s10 = r10.x_step(2, n1)
    far = swap_both(after(send_far, dhr))
    d1, da, dq, dkv, dkvr, vb = attend_back(0, d2, dh, after(dhr, r0f.keep, s10, n1))
    back = swap(dkvr, "c")
    n10 = r10.near(2, vb)
    far = after(far, n10)
    s0 = r0f.x_step(0, n10)
    low = join_rows(near, far)
    yt, yl, dxp, gbt, gbl = input_back(0, dq, dkv, after(back, s0, low))
    dxr = swap(dxp, "l")
    r00 = input_grads(0, da, yt, yl, va, vb, gbt, gbl, gut, gul)
    rest, first = Finish(y), Finish(y)
    y0 = rest.y_step(0, r0f.near(0, r00.keep), n0)
    dxr = after(dxr, y0)

    def sort(here, got, near, far, low):
        kept, sent = call(
            bind(sort_body, z), [sds((2 * R, W), BF), sds((2 * R + 16, W), BF)],
            here, got, near, far, low, meta=meta,
        )
        return kept, swap(sent, "c")

    def place(kept, sent):
        shape = layout_in.shape
        t, l_ = call(
            bind(place_body, z),
            [sds((1,) + text_in.shape, BF), sds((1, shape[0], shape[2], shape[1]), BF)],
            kept, sent, meta=meta,
        )
        return t, flip(l_)

    low = swap(after(low, dxr), "l")
    dhere, dpart, dsend, dsend_far = leave(True, d1, dxp, after(dxr, r00.keep), dx1)
    dgot, dnear, dfar = swap(dsend, "y"), swap(dpart, "h"), swap_both(dsend_far)
    other = rest.sum_of(0, dhere)
    r00.x_step(2, other)
    dgot, dnear, dfar, low, r00.far[2] = together(dgot, dnear, dfar, low, r00.far[2])
    dlow = swap(join_rows(dnear, dfar), "l")
    rest.last = swap(after(other, dlow), "h")
    r0f.x_step(1, dgot)
    first.y_step(2, r00.near(2, dgot), n10)
    dlow, r0f.far[1], first.cross[2] = together(dlow, r0f.far[1], first.cross[2])
    h1 = first.h_step()
    yf = rest.y_step(1, r0f.near(1), n1)
    dkept, dsent = sort(dhere, dgot, dnear, dfar, after(dlow, h1, yf))
    kept, sent = sort(here, got, near, far, after(low, dkept))
    own1 = first.close(kept)
    dx_t, dx_l = place(dkept, after(dsent, own1))
    res_t, res_l = place(kept, after(sent, dx_t))
    own2 = rest.close(res_t)
    like = lambda *arrays: [sds(v.shape, F32) for v in arrays]
    g_tup, g_lup, g_tdn, g_ldn = call(
        bind(finish_body, z), like(t_up, l_up, flip(t_down), flip(l_down)), *rest.terms(own2)
    )
    g_ti, g_tb, g_to, g_tg, g_ts, g_tu, g_li, g_lb, g_lo, g_lg, g_ls, g_lu = call(
        bind(finish_first_body, z),
        like(t_in, t_hb, t_out, t_gain, t_shift, t_ub, l_in, l_hb, l_out, l_gain, l_shift, l_ub),
        *first.terms(g_tup),
    )
    return (
        res_t, res_l, dx_t, dx_l,
        g_ti, g_tb, g_to, g_tg, g_ts, g_tup, g_tu, flip(g_tdn),
        g_li, g_lb, g_lo, g_lg, g_ls, g_lup, g_lu, flip(g_ldn),
    )


def solution(mesh):
    section, dp, tensor = (mesh.shape[a] for a in ("section", "dp", "tensor"))
    fine = Mesh(mesh.devices.reshape(section, dp // 2, 2, 2, tensor // 2), ALL)
    d, t = ("x", "c"), ("h", "l")
    weights = (
        P("y", None, d, t),
        P("y", None, t + d),
        P("y", t, d),
        P("y", None, d),
        P("y", None, d),
        P("y", d, t),
        P("y", t + d),
        P("y", t, d),
    ) * 2
    pages = (P(d, None, None), P(d, None, None))
    return jax.shard_map(
        per_device,
        mesh=fine,
        in_specs=pages + (P(d, None),) + pages + weights,
        out_specs=(P("y", d, None, None),) * 4 + weights,
        check_vma=False,
    )
```

```python
import functools

import jax
import jax.numpy as jnp
from jax import lax
from jax.experimental import pallas as pl
from jax.experimental.pallas import tpu as pltpu
from jax.sharding import Mesh, PartitionSpec as P

BF = jnp.bfloat16
F32 = jnp.float32
HEAD = 64
LHEAD = 16
SLOT = 128
GROUPS = 3
ALL = ("y", "x", "c", "h", "l")


def mm(a, b):
    return lax.dot_general(a, b, (((1,), (0,)), ((), ())), preferred_element_type=F32)


def mm_nt(a, b):
    return lax.dot_general(a, b, (((1,), (1,)), ((), ())), preferred_element_type=F32)


def mm_tn(a, b):
    return lax.dot_general(a, b, (((0,), (0,)), ((), ())), preferred_element_type=F32)


class Sizes:
    def __init__(self, text, layout, rd, ld, cols, lcols, dp):
        self.seq = text.shape[1]
        self.rows = self.seq // 2
        self.d = text.shape[2]
        self.ld = layout.shape[2]
        self.width = self.d + self.ld
        self.rd = rd
        self.lr = ld
        self.dp = dp
        self.quarter = cols
        self.lquarter = lcols
        self.heads = cols // HEAD
        self.block = rd + ld // GROUPS
        self.vblock = self.block + 16
        self.part = ld // GROUPS
        self.xs = dp // 2
        self.masks = 4 if self.xs == 2 else 2


def call(body, out_shapes, *args, scratch=(), meta=None, us=4):
    places = [pl.BlockSpec(memory_space=pltpu.VMEM)] * len(args)
    if meta is not None:
        args = (meta,) + args
        places = [pl.BlockSpec(memory_space=pltpu.SMEM)] + places
    return pl.pallas_call(
        body,
        out_shape=list(out_shapes),
        in_specs=places,
        out_specs=[pl.BlockSpec(memory_space=pltpu.VMEM)] * len(out_shapes),
        scratch_shapes=list(scratch),
        compiler_params=pltpu.CompilerParams(vmem_limit_bytes=56 * 2**20),
        cost_estimate=pl.CostEstimate(flops=int(us * 8e9), bytes_accessed=1000, transcendentals=0),
    )(*args)


def sds(shape, dtype):
    return jax.ShapeDtypeStruct(shape, dtype)


def text_w(w, h, z, lo=0, hi=None):
    return jnp.concatenate(
        [w[r % 2][r // 2, w[2](h), : z.rd, lo:hi] for r in range(z.dp)], axis=0
    )


def layout_w(w, h, z, lo=0, hi=None):
    width = w[0].shape[-1] // GROUPS
    hi = width if hi is None else hi
    pieces = []
    for r in range(z.dp):
        for k in range(GROUPS):
            rows = slice(z.rd, z.rd + z.part)
            pieces.append(w[r % 2][r // 2, w[2](h), rows, width * k + lo : width * k + hi])
    return jnp.concatenate(pieces, axis=0)


def alone(h):
    return h


def first_of_two(h):
    return 2 * h


def second_of_two(h):
    return 2 * h + 1


class Pick:
    def __init__(self, refs, core, piece):
        self.refs, self.core, self.piece = refs, core, piece
        self.shape = refs[core].shape

    def __getitem__(self, at):
        x, h, rows, cols = at
        if len(self.refs) == 4:
            return self.refs[2 * h + self.core][x, self.piece, rows, cols]
        return self.refs[self.core][x, 2 * h + self.piece, rows, cols]


def feed_forward(refs):
    return tuple((Pick(refs, 0, p), Pick(refs, 1, p), alone) for p in range(2))


def put_grads(g, h, text, layout, z):
    width = g[0].shape[-1] // GROUPS
    low = layout.astype(BF)
    pad = width - low.shape[-1]
    low = jnp.concatenate([low, jnp.zeros((low.shape[0], pad), BF)], axis=1)
    text = text.astype(BF)
    at = g[2](h)
    for r in range(z.dp):
        ref, x = g[r % 2], r // 2
        ref[x, at, : z.rd, :] = text[z.rd * r : z.rd * (r + 1)]
        for k in range(GROUPS):
            base = z.lr * r + z.part * k
            ref[x, at, z.rd : z.block, width * k : width * (k + 1)] = low[base : base + z.part]


def natural(pieces, m, z):
    out = []
    for d in range(z.dp):
        value = pieces[d]
        for other in range(1, z.masks):
            value = jnp.where(m == other, pieces[d ^ other], value)
        out.append(value)
    return jnp.concatenate(out, axis=1)


def norm_stats(resid):
    center = resid - jnp.mean(resid, axis=-1, keepdims=True)
    factor = lax.rsqrt(jnp.mean(center * center, axis=-1, keepdims=True) + 1e-05)
    return center * factor, factor


def norm_both(resid, z):
    nt, ft = norm_stats(resid[:, : z.d])
    nl, fl = norm_stats(resid[:, z.d :])
    return jnp.concatenate([nt, nl], axis=1), ft, fl


def norm_back(grad, normed, factor, gain):
    scaled = grad * gain
    return factor * (
        scaled
        - jnp.mean(scaled, axis=-1, keepdims=True)
        - normed * jnp.mean(scaled * normed, axis=-1, keepdims=True)
    )


def norm_back_both(grad, normed, ft, fl, gain, z):
    gt = norm_back(grad[:, : z.d], normed[:, : z.d], ft, gain[:, : z.d])
    gl = norm_back(grad[:, z.d :], normed[:, z.d :], fl, gain[:, z.d :])
    return jnp.concatenate([gt, gl], axis=1)


def small_rows(w, h, z):
    return [w[r % 2][r // 2, h, z.block : z.vblock, :].astype(F32) for r in range(z.dp)]


def qkv_body(z, fused, meta_ref, *refs):
    if fused:
        (hid_ref, own_ref, rec_ref, prev_ref, ws_ref, wc_ref,
         r_ref, x_ref, q_ref, kv_ref, vec_ref, ut_ref, ul_ref) = refs
        vec = prev_ref[...]
        resid = (
            hid_ref[...].astype(F32) + own_ref[...].astype(F32) + rec_ref[...].astype(F32) + vec[4:5]
        )
        r_ref[...] = resid
        normed, _, _ = norm_both(resid, z)
        x = (normed * vec[1:2] + vec[5:6]).astype(BF)
        x_ref[...] = x
    else:
        x_ref, far_ref, ws_ref, wc_ref, q_ref, kv_ref, kvr_ref, vec_ref, ut_ref, ul_ref = refs
        x = x_ref[...]
    w = (ws_ref, wc_ref, alone)
    mask = meta_ref[1]
    lane = 4 * SLOT
    small = small_rows(w, 0, z)
    vec_ref[:, : z.d] = jnp.concatenate([s[:, : z.rd] for s in small], axis=1)
    vec_ref[:, z.d :] = jnp.concatenate([s[:, lane : lane + z.lr] for s in small], axis=1)
    xt, xl = x[:, : z.d], x[:, z.d :]
    n, m = z.quarter, z.lquarter
    zeros = jnp.zeros((z.rows, SLOT - HEAD - LHEAD), BF)
    hb, lb, ub, vb = n // z.dp, m // z.dp, 4 * n // z.dp, 4 * m // z.dp

    def project(xt, xl, first, out_ref):
        yt = mm(xt, text_w(w, h, z, n * first, 3 * n)) + bt[:, n * first :]
        yl = mm(xl, layout_w(w, h, z, m * first, 3 * m)) + bl[:, m * first :]
        yt = yt.astype(BF)
        yl = yl.astype(BF)
        for s in range(first, 3):
            for j in range(z.heads):
                lo, llo = n * (s - first) + HEAD * j, m * (s - first) + LHEAD * j
                a = yt[:, lo : lo + HEAD]
                b = yl[:, llo : llo + LHEAD]
                if s == 0:
                    a = a * BF(HEAD**-0.5)
                    b = b * BF(LHEAD**-0.5)
                slot = jnp.concatenate([a, b, zeros], axis=1)
                head = z.heads * h + j
                if s == 0:
                    q_ref[head] = slot
                else:
                    out_ref[2 * z.heads * (s - 1) + head] = slot

    for h in range(2):
        small = small_rows(w, h, z)
        rows = lambda i, lo, size: natural([s[i : i + 1, lo : lo + size] for s in small], mask, z)
        ut_ref[h] = rows(8, 0, ub)
        ul_ref[h] = rows(8, lane, vb)
        bt = jnp.concatenate([rows(6, 0, hb), jnp.zeros((1, n), F32), rows(7, 0, hb)], axis=1)
        bl = jnp.concatenate(
            [rows(6, lane, lb), jnp.zeros((1, m), F32), rows(7, lane, lb)], axis=1
        )
        project(xt, xl, 0, kv_ref)
        if not fused:
            far = far_ref[...]
            project(far[:, : z.d], far[:, z.d :], 1, kvr_ref)


def attend_body(z, q_ref, own_ref, rec_ref, mask_ref, ws_ref, wc_ref, a_ref, c_ref, p_ref, s_ref):
    w = (ws_ref, wc_ref, alone)
    count = 2 * z.heads
    m0 = mask_ref[0:1, : z.rows] > 0
    m1 = mask_ref[0:1, z.rows :] > 0

    def head(j, carry):
        q = q_ref[j]
        s0 = jnp.where(m0, mm_nt(q, own_ref[j]), -1000000000.0)
        s1 = jnp.where(m1, mm_nt(q, rec_ref[j]), -1000000000.0)
        top = jnp.maximum(
            jnp.max(s0, axis=-1, keepdims=True), jnp.max(s1, axis=-1, keepdims=True)
        )
        e0 = jnp.exp(s0 - top)
        e1 = jnp.exp(s1 - top)
        inv = 1.0 / (jnp.sum(e0, axis=-1, keepdims=True) + jnp.sum(e1, axis=-1, keepdims=True))
        p0 = (e0 * inv).astype(BF)
        p1 = (e1 * inv).astype(BF)
        p_ref[j, :, : z.rows] = p0
        p_ref[j, :, z.rows :] = p1
        s_ref[j] = (mm(p0, own_ref[count + j]) + mm(p1, rec_ref[count + j])).astype(BF)
        return carry

    lax.fori_loop(0, count, head, 0, unroll=True)
    n, m = z.quarter, z.lquarter
    at = al = None
    for h in range(2):
        heads = [s_ref[z.heads * h + j] for j in range(z.heads)]
        ct = jnp.concatenate([s[:, :HEAD] for s in heads], axis=1)
        cl = jnp.concatenate([s[:, HEAD : HEAD + LHEAD] for s in heads], axis=1)
        c_ref[h, :, :n] = ct
        c_ref[h, :, 2 * SLOT : 2 * SLOT + m] = cl
        pt = mm_nt(ct, text_w(w, h, z, 3 * n, 4 * n))
        pll = mm_nt(cl, layout_w(w, h, z, 3 * m, 4 * m))
        at = pt if at is None else at + pt
        al = pll if al is None else al + pll
    a_ref[:, : z.d] = at.astype(BF)
    a_ref[:, z.d :] = al.astype(BF)


def gelu_parts(u):
    cdf = 0.5 * (1.0 + lax.erf(u * 0.7071067811865476))
    slope = cdf + u * jnp.exp(-0.5 * u * u) * 0.3989422804014327
    return (u * cdf).astype(BF), slope.astype(BF)


def forward_body(
    z, x_ref, own_ref, rec_ref, vec_ref, bt_ref, bl_ref, *refs
):
    r_ref, hid_ref, gt_ref, gl_ref, st_ref, sl_ref, f_ref = refs[-7:]
    up, down = feed_forward(refs[:-7])
    lw = 4 * z.lquarter
    vec = vec_ref[...]
    resid = x_ref[...].astype(F32) + own_ref[...].astype(F32) + rec_ref[...].astype(F32) + vec[2:3]
    r_ref[...] = resid
    normed, _, _ = norm_both(resid, z)
    hid = (normed * vec[0:1] + vec[3:4]).astype(BF)
    hid_ref[...] = hid
    ht, hl = hid[:, : z.d], hid[:, z.d :]
    ft = fl = None
    for h in range(2):
        g, s = gelu_parts(mm(ht, text_w(up, h, z)) + bt_ref[h])
        gt_ref[h] = g
        st_ref[h] = s
        p = mm_nt(g, text_w(down, h, z))
        ft = p if ft is None else ft + p
        g, s = gelu_parts(mm(hl, layout_w(up, h, z, 0, lw)) + bl_ref[h])
        gl_ref[h] = g
        sl_ref[h] = s
        p = mm_nt(g, layout_w(down, h, z, 0, lw))
        fl = p if fl is None else fl + p
    f_ref[:, : z.d] = ft.astype(BF)
    f_ref[:, z.d :] = fl.astype(BF)


def col_sum(value):
    return jnp.sum(value, axis=0, keepdims=True)


def tail_body(z, fused, *refs):
    if fused == "last":
        hid_ref, own_ref, rec_ref, go_ref, vec_ref, st_ref, sl_ref = refs[:7]
        ws = refs[7:-9]
        out_ref, d2_ref, df_ref, dut_ref, dul_ref, dh_ref, vg_ref, gbt_ref, gbl_ref = refs[-9:]
        vec = vec_ref[...]
        resid = (
            hid_ref[...].astype(F32) + own_ref[...].astype(F32) + rec_ref[...].astype(F32) + vec[4:5]
        )
        normed, ft, fl = norm_both(resid, z)
        out_ref[...] = (normed * vec[1:2] + vec[5:6]).astype(BF)
        go = go_ref[...].astype(F32)
    else:
        r_ref, d1_ref, own_ref, rec_ref, vec_ref, st_ref, sl_ref = refs[:7]
        ws = refs[7:-9]
        dx_ref, d2_ref, df_ref, dut_ref, dul_ref, dh_ref, vg_ref, gbt_ref, gbl_ref = refs[-9:]
        vec = vec_ref[...]
        normed, ft, fl = norm_both(r_ref[...], z)
        low = (d1_ref[...] + own_ref[...].astype(F32) + rec_ref[...].astype(F32)).astype(BF)
        dx_ref[...] = low
        go = low.astype(F32)
    up, down = feed_forward(ws)
    lw = 4 * z.lquarter
    d2 = norm_back_both(go, normed, ft, fl, vec[1:2], z)
    d2_ref[...] = d2
    df = d2.astype(BF)
    df_ref[...] = df
    vg_ref[0:1] = col_sum(go * normed)
    vg_ref[1:2] = col_sum(go)
    vg_ref[2:3] = col_sum(df.astype(F32))
    vg_ref[3:8] = jnp.zeros((5, z.width), F32)
    dft, dfl = df[:, : z.d], df[:, z.d :]
    ht = hl = None
    for h in range(2):
        du = (mm(dft, text_w(down, h, z)) * st_ref[h].astype(F32)).astype(BF)
        dut_ref[h] = du
        gbt_ref[h] = col_sum(du.astype(F32))
        p = mm_nt(du, text_w(up, h, z))
        ht = p if ht is None else ht + p
        du = (mm(dfl, layout_w(down, h, z, 0, lw)) * sl_ref[h].astype(F32)).astype(BF)
        dul_ref[h] = du
        gbl_ref[h] = col_sum(du.astype(F32))
        p = mm_nt(du, layout_w(up, h, z, 0, lw))
        hl = p if hl is None else hl + p
    dh_ref[:, : z.d] = ht.astype(BF)
    dh_ref[:, z.d :] = hl.astype(BF)


def ffn_grads_body(z, hid_ref, df_ref, gt_ref, gl_ref, dut_ref, dul_ref, g_ref, h_ref):
    one, two = (g_ref, h_ref, first_of_two), (g_ref, h_ref, second_of_two)
    hid, df = hid_ref[...], df_ref[...]
    for h in range(2):
        put_grads(one, h, mm_tn(hid[:, : z.d], dut_ref[h]), mm_tn(hid[:, z.d :], dul_ref[h]), z)
        put_grads(two, h, mm_tn(df[:, : z.d], gt_ref[h]), mm_tn(df[:, z.d :], gl_ref[h]), z)


def attend_back_body(
    z, d2_ref, own_ref, rec_ref, r_ref, vec_ref, ws_ref, wc_ref, c_ref, q_ref, kv_ref, kvr_ref, p_ref, mask_ref,
    d1_ref, da_ref, dq_ref, dkv_ref, dkvr_ref, vg_ref, dc_ref, dd_ref,
):
    count = 2 * z.heads
    w = (ws_ref, wc_ref, alone)
    vec = vec_ref[...]
    dh = d2_ref[...] + own_ref[...].astype(F32) + rec_ref[...].astype(F32)
    normed, ft, fl = norm_both(r_ref[...], z)
    d1 = norm_back_both(dh, normed, ft, fl, vec[0:1], z)
    d1_ref[...] = d1
    da = d1.astype(BF)
    da_ref[...] = da
    vg_ref[0:1] = col_sum(dh * normed)
    vg_ref[1:2] = col_sum(dh)
    vg_ref[2:3] = col_sum(da.astype(F32))
    vg_ref[3:8] = jnp.zeros((5, z.width), F32)
    n, m = z.quarter, z.lquarter
    zeros = jnp.zeros((z.rows, SLOT - HEAD - LHEAD), BF)
    for h in range(2):
        dct = mm(da[:, : z.d], text_w(w, h, z, 3 * n, 4 * n)).astype(BF)
        dcl = mm(da[:, z.d :], layout_w(w, h, z, 3 * m, 4 * m)).astype(BF)
        for j in range(z.heads):
            a = dct[:, HEAD * j : HEAD * (j + 1)]
            b = dcl[:, LHEAD * j : LHEAD * (j + 1)]
            dc_ref[z.heads * h + j] = jnp.concatenate([a, b, zeros], axis=1)
            ct = c_ref[h, :, HEAD * j : HEAD * (j + 1)].astype(F32)
            cl = c_ref[h, :, 2 * SLOT + LHEAD * j : 2 * SLOT + LHEAD * (j + 1)].astype(F32)
            dt = jnp.sum(a.astype(F32) * ct, axis=-1, keepdims=True)
            dl = jnp.sum(b.astype(F32) * cl, axis=-1, keepdims=True)
            dd_ref[z.heads * h + j, :, 0:1] = dt
            dd_ref[z.heads * h + j, :, 1:2] = dt + dl
    lane = lax.broadcasted_iota(jnp.int32, (z.rows, SLOT), 1)
    text_lane = lane < HEAD
    scale = jnp.where(text_lane, HEAD**-0.5, LHEAD**-0.5)
    mask = mask_ref[...]
    masks = (mask[:, : z.rows], mask[:, z.rows :])

    def head(j, carry):
        dc = dc_ref[j]
        dct = jnp.where(text_lane, dc, jnp.zeros_like(dc))
        q = q_ref[j]
        dt = dd_ref[j, :, 0:1]
        ds = dd_ref[j, :, 1:2]
        dq_t = dq_s = None
        for i, (k_ref, o_ref) in enumerate(((kv_ref, dkv_ref), (kvr_ref, dkvr_ref))):
            k = k_ref[j]
            v = k_ref[count + j]
            prob = p_ref[j, :, z.rows * i : z.rows * (i + 1)]
            pm = jnp.where(masks[i] > 0, prob.astype(F32), 0.0)
            st = (pm * (mm_nt(dct, v) - dt)).astype(BF)
            ss = (pm * (mm_nt(dc, v) - ds)).astype(BF)
            a = mm(st, k)
            b = mm(ss, k)
            dq_t = a if dq_t is None else dq_t + a
            dq_s = b if dq_s is None else dq_s + b
            dk = jnp.where(text_lane, mm_tn(st, q), mm_tn(ss, q))
            o_ref[j] = dk.astype(BF)
            o_ref[count + j] = mm_tn(prob, dc).astype(BF)
        dq_ref[j] = (jnp.where(text_lane, dq_t, dq_s) * scale).astype(BF)
        return carry

    lax.fori_loop(0, count, head, 0, unroll=True)


def input_back_body(z, dq_ref, dkv_ref, rec_ref, ws_ref, wc_ref, yt_ref, yl_ref, dx_ref, gbt_ref, gbl_ref):
    count = 2 * z.heads
    w = (ws_ref, wc_ref, alone)
    n, m = z.quarter, z.lquarter
    xt = xl = None
    for h in range(2):
        ts, ls = [], []
        for s in range(3):
            for j in range(z.heads):
                head = z.heads * h + j
                if s == 0:
                    slot = dq_ref[head]
                else:
                    at = count * (s - 1) + head
                    slot = (dkv_ref[at].astype(F32) + rec_ref[at].astype(F32)).astype(BF)
                ts.append(slot[:, :HEAD])
                ls.append(slot[:, HEAD : HEAD + LHEAD])
        yt = jnp.concatenate(ts, axis=1)
        yl = jnp.concatenate(ls, axis=1)
        yt_ref[h] = yt
        yl_ref[h] = yl
        gbt_ref[h] = col_sum(yt.astype(F32))
        gbl_ref[h] = col_sum(yl.astype(F32))
        p = mm_nt(yt, text_w(w, h, z, 0, 3 * n))
        xt = p if xt is None else xt + p
        p = mm_nt(yl, layout_w(w, h, z, 0, 3 * m))
        xl = p if xl is None else xl + p
    dx_ref[:, : z.d] = xt.astype(BF)
    dx_ref[:, z.d :] = xl.astype(BF)


def input_grads_body(
    z, meta_ref, x_ref, da_ref, c_ref, yt_ref, yl_ref, va_ref, vb_ref, bt_ref, bl_ref, ut_ref, ul_ref,
    g_ref, h_ref, s_ref,
):
    g = (g_ref, h_ref, alone)
    x, da = x_ref[...], da_ref[...]
    n, m = z.quarter, z.lquarter
    va, vb = va_ref[...], vb_ref[...]
    mask = meta_ref[1]
    rows = (vb[0:1], va[0:1], vb[2:3], vb[1:2], va[2:3], va[1:2])
    lane = 4 * SLOT
    s_ref[...] = jnp.zeros_like(s_ref)

    def relative(value, size):
        parts = [value[:, size * d : size * (d + 1)] for d in range(z.dp)]
        out = []
        for r in range(z.dp):
            v = parts[r]
            for other in range(1, z.masks):
                v = jnp.where(mask == other, parts[r ^ other], v)
            out.append(v)
        return out

    for h in range(2):
        ct = c_ref[h, :, :n]
        cl = c_ref[h, :, 2 * SLOT : 2 * SLOT + m]
        text = jnp.concatenate(
            [mm_tn(x[:, : z.d], yt_ref[h]), mm_tn(da[:, : z.d], ct)], axis=1
        )
        layout = jnp.concatenate(
            [mm_tn(x[:, z.d :], yl_ref[h]), mm_tn(da[:, z.d :], cl)], axis=1
        )
        put_grads(g, h, text, layout, z)
        bt, bl, ut, ul = bt_ref[h], bl_ref[h], ut_ref[h], ul_ref[h]
        entries = [
            (6, 0, relative(bt[:, :n], n // z.dp)),
            (7, 0, relative(bt[:, 2 * n :], n // z.dp)),
            (6, lane, relative(bl[:, :m], m // z.dp)),
            (7, lane, relative(bl[:, 2 * m :], m // z.dp)),
            (8, 0, relative(ut, 4 * n // z.dp)),
            (8, lane, relative(ul, 4 * m // z.dp)),
        ]
        for r in range(z.dp):
            for i, row in enumerate(rows):
                s_ref[i : i + 1, : z.rd] = row[:, z.rd * r : z.rd * (r + 1)]
                s_ref[i : i + 1, lane : lane + z.lr] = row[
                    :, z.d + z.lr * r : z.d + z.lr * (r + 1)
                ]
            for at, lo, values in entries:
                s_ref[at : at + 1, lo : lo + values[r].shape[1]] = values[r]
            g[r % 2][r // 2, h, z.block : z.vblock, :] = s_ref[...].astype(BF)


def put_pack(out_ref, text, layout, z):
    out_ref[: z.rd, :] = text.astype(BF)
    width = out_ref.shape[-1] // GROUPS
    low = layout.astype(BF)
    low = jnp.concatenate([low, jnp.zeros((low.shape[0], width - low.shape[1]), BF)], axis=1)
    for k in range(GROUPS):
        out_ref[z.rd : z.block, width * k : width * (k + 1)] = low[z.part * k : z.part * (k + 1)]


def pack_first_body(
    z, ti_ref, to_ref, li_ref, lo_ref, tg_ref, lg_ref, ts_ref, ls_ref, tb_ref, lb_ref, tu_ref, lu_ref,
    out_ref, s_ref,
):
    text = jnp.concatenate([ti_ref[0, 0], ti_ref[0, 1], ti_ref[0, 2], to_ref[0].T], axis=1)
    layout = jnp.concatenate([li_ref[0, 0], li_ref[0, 1], li_ref[0, 2], lo_ref[0].T], axis=1)
    put_pack(out_ref, text, layout, z)
    s_ref[...] = jnp.zeros_like(s_ref)
    for lane, refs in ((0, (tg_ref, ts_ref, tb_ref)), (4 * SLOT, (lg_ref, ls_ref, lb_ref))):
        at = 0
        for ref in refs:
            count, width = ref.shape[1], ref.shape[2]
            s_ref[at : at + count, lane : lane + width] = ref[0]
            at += count
    s_ref[8:9, : tu_ref.shape[1]] = tu_ref[...]
    s_ref[8:9, 4 * SLOT : 4 * SLOT + lu_ref.shape[1]] = lu_ref[...]
    out_ref[z.block : z.vblock, :] = s_ref[...].astype(BF)


def pack_rest_body(z, tu_ref, lu_ref, td_ref, ld_ref, out_ref):
    put_pack(out_ref.at[0], tu_ref[0], lu_ref[0], z)
    put_pack(out_ref.at[1], td_ref[0], ld_ref[0], z)


def take_layout(total, cols, z):
    width = total.shape[-1] // GROUPS
    return jnp.concatenate(
        [total[z.rd : z.block, width * k : width * k + cols] for k in range(GROUPS)], axis=0
    )


def final_sum(refs):
    return sum(r[...].astype(F32) for r in refs)


def finish_first_body(z, *refs):
    (ti_ref, tb_ref, to_ref, tg_ref, ts_ref, tu_ref,
     li_ref, lb_ref, lo_ref, lg_ref, ls_ref, lu_ref) = refs[2:]
    total = final_sum(refs[:2])[0]
    n, m = z.quarter, z.lquarter
    layout = take_layout(total, 4 * m, z)
    for s in range(3):
        ti_ref[0, s] = total[: z.rd, n * s : n * (s + 1)]
        li_ref[0, s] = layout[:, m * s : m * (s + 1)]
    to_ref[0] = total[: z.rd, 3 * n :].T
    lo_ref[0] = layout[:, 3 * m :].T
    rows = total[z.block : z.vblock]
    for lane, group in ((0, (tg_ref, ts_ref, tb_ref)), (4 * SLOT, (lg_ref, ls_ref, lb_ref))):
        at = 0
        for ref in group:
            count, width = ref.shape[1], ref.shape[2]
            ref[0] = rows[at : at + count, lane : lane + width]
            at += count
    tu_ref[...] = rows[8:9, : tu_ref.shape[1]]
    lu_ref[...] = rows[8:9, 4 * SLOT : 4 * SLOT + lu_ref.shape[1]]


def finish_body(z, *refs):
    total = final_sum(refs[:2])
    for p in range(2):
        t_ref, l_ref = refs[2 + 2 * p : 4 + 2 * p]
        t_ref[0] = total[p, : z.rd]
        l_ref[0] = take_layout(total[p], 4 * z.lquarter, z)


def entry_body(z, meta_ref, t_ref, l_ref, tc_ref, lc_ref, mask_ref, own_ref, send_ref):
    y, c = meta_ref[0], meta_ref[2]
    row = jnp.where(y == 0, mask_ref[0:1, :], mask_ref[1:2, :]).astype(F32)
    left, right = row[:, : z.rows], row[:, z.rows :]
    for ref, half in ((own_ref, c), (send_ref, 1 - c)):
        for i, (text, layout) in enumerate(((t_ref, l_ref), (t_ref, l_ref), (tc_ref, lc_ref))):
            part = 1 - half if i == 1 else half
            rows = pl.ds(pl.multiple_of(part * z.rows, z.rows), z.rows)
            out = slice(z.rows * i, z.rows * (i + 1))
            ref[out, : z.d] = text[y, rows, :]
            ref[out, z.d :] = layout[y, :, rows].astype(F32).T.astype(BF)
        near = jnp.where(half == 0, left, right)
        far = jnp.where(half == 0, right, left)
        low = jnp.concatenate([near, far, jnp.zeros((1, z.width - z.seq), F32)], axis=1)
        ref[3 * z.rows :, :] = jnp.broadcast_to(low, (16, z.width)).astype(BF)


def ordered(value, m, z):
    text = [value[:, z.rd * r : z.rd * (r + 1)] for r in range(z.dp)]
    layout = [value[:, z.d + z.lr * r : z.d + z.lr * (r + 1)] for r in range(z.dp)]
    return jnp.concatenate([natural(text, m, z), natural(layout, m, z)], axis=1)


def settle_body(z, meta_ref, own_ref, got_ref, x_ref, far_ref, cot_ref, out_ref):
    mine = meta_ref[3] == 1
    mask = meta_ref[1]
    step = z.rows // 4

    def chunk(k, carry):
        rows = pl.ds(pl.multiple_of(k * step, step), step)
        for i, ref in enumerate((x_ref, far_ref, cot_ref)):
            at = pl.ds(pl.multiple_of(z.rows * i + k * step, step), step)
            ref[rows, :] = ordered(jnp.where(mine, own_ref[at, :], got_ref[at, :]), mask, z)
        return carry

    lax.fori_loop(0, 4, chunk, 0)
    last = slice(3 * z.rows, 3 * z.rows + 16)
    row = jnp.where(mine, own_ref[last, : z.seq], got_ref[last, : z.seq])
    out_ref[...] = row.astype(F32)[0:1]


def exit_body(z, summed, meta_ref, *refs):
    if summed:
        d_ref, own_ref, rec_ref, b_ref, here_ref, part_ref, send_ref, far_ref = refs
    else:
        a_ref, b_ref, here_ref, part_ref, send_ref, far_ref = refs
    first = meta_ref[0] == 0
    low = meta_ref[4] == 0
    mask = meta_ref[1]
    half = z.rows // 2
    pieces = 1 if summed else 4
    step = z.rows // pieces

    def chunk(k, carry):
        rows = pl.ds(pl.multiple_of(k * step, step), step) if pieces > 1 else slice(None)
        two = b_ref[rows, :]
        if summed:
            one = d_ref[rows, :] + own_ref[rows, :].astype(F32) + rec_ref[rows, :].astype(F32)
            one = one.astype(BF)
        else:
            one = a_ref[rows, :]
        here_ref[rows, :] = ordered(jnp.where(first, one, two), mask, z)
        send_ref[rows, :] = ordered(jnp.where(first, two, one), mask, z)
        return carry

    lax.fori_loop(0, pieces, chunk, 0)
    part_ref[...] = jnp.where(low, here_ref[:half, :], here_ref[half:, :])
    far_ref[...] = jnp.where(low, send_ref[:half, :], send_ref[half:, :])


def sort_body(z, meta_ref, here_ref, got_ref, b_ref, d_ref, far_ref, keep_ref, send_ref):
    mine = meta_ref[3] == 1
    low = meta_ref[4] == 0
    half = z.rows // 2
    for i, (same_ref, near_ref) in enumerate(((here_ref, b_ref), (got_ref, d_ref))):
        beyond = far_ref[half * i : half * (i + 1), :]
        for k in range(2):
            rows = slice(half * k, half * (k + 1))
            other = jnp.where(low == (k == 0), near_ref[...], beyond)
            same = same_ref[rows, :]
            rows = slice(z.rows * i + half * k, z.rows * i + half * (k + 1))
            keep_ref[rows, :] = jnp.where(mine, same, other)
            send_ref[rows, :] = jnp.where(mine, other, same)
    send_ref[2 * z.rows :, :] = jnp.zeros((16, z.width), BF)


def place_body(z, meta_ref, keep_ref, got_ref, t_ref, l_ref):
    y, c = meta_ref[0], meta_ref[2]
    for i in range(2):
        page = y if i == 0 else 1 - y
        for ref, half in ((keep_ref, c), (got_ref, 1 - c)):
            rows = pl.ds(pl.multiple_of(half * z.rows, z.rows), z.rows)
            value = ref[z.rows * i : z.rows * (i + 1), :]
            t_ref[0, page, rows, :] = value[:, : z.d]
            l_ref[0, page, :, rows] = value[:, z.d :].astype(F32).T.astype(BF)


def swap(value, axis):
    return lax.ppermute(value, axis, [(0, 1), (1, 0)])


def after(value, *others):
    return lax.optimization_barrier((value,) + others)[0]


def together(*values):
    return lax.optimization_barrier(values)


def swap_both(value):
    return lax.ppermute(value, ("y", "h"), [(0, 3), (1, 2), (2, 1), (3, 0)])


def join_rows(*parts):
    return jnp.concatenate(parts + (jnp.zeros((16, parts[0].shape[1]), BF),), axis=0)


def join_blocks(parts, got):
    own = jnp.stack([jnp.concatenate(parts), jnp.concatenate(got)])
    return own, swap(own, "c")


def gather_blocks(parts, x_size, *token):
    if x_size == 2:
        return join_blocks(parts, [after(swap(v, "x"), *token) for v in parts])
    else:
        own = lax.all_gather(jnp.concatenate(parts), "x", axis=0)
    return own, swap(own, "c")


def add_low(*terms):
    total = terms[0].astype(F32)
    for term in terms[1:]:
        total = total + term.astype(F32)
    return total.astype(BF)


class Reduce:
    def __init__(self, keep, send, x_size, *token):
        self.keep, self.x_size = keep, x_size
        half = keep.shape[1] // 2
        self.rows = (slice(half, None), slice(0, half), slice(None))
        self.got = swap(after(send, *token) if token else send, "c")
        self.far = {}

    def x_step(self, part, *token):
        got, rows = after(self.got, *token), self.rows[part]
        if self.x_size == 2:
            total = add_low(self.keep[1, rows], got[1, rows])
            self.far[part] = swap(total, "x")
        else:
            total = add_low(self.keep[:, rows], got[:, rows])
            self.far[part] = lax.psum_scatter(total, "x", scatter_dimension=0, tiled=False)
        return total

    def near(self, part, *token):
        rows = self.rows[part]
        if part in self.far:
            far = after(self.far[part], *token)
        else:
            far = after(self.far[2], *token)[rows]
        if self.x_size == 2:
            far = add_low(self.keep[0, rows], self.got[0, rows], far)
        return far


class Finish:
    def __init__(self, y):
        self.y, self.here, self.cross = y, {}, {}

    def y_step(self, part, first, second):
        self.here[part] = jnp.where(self.y == 0, first, second)
        self.cross[part] = swap(jnp.where(self.y == 0, second, first), "y")
        return self.here[part]

    def sum_of(self, part, *token):
        if part in self.here:
            return add_low(self.here[part], after(self.cross[part], *token))
        half = self.here[2].shape[0] // 2
        rows = slice(half, None) if part == 0 else slice(0, half)
        return add_low(self.here[2][rows], after(self.cross[2], *token)[rows])

    def h_step(self, *token):
        other = self.sum_of(0, *token)
        self.last = swap(other, "h")
        return other

    def close(self, *token):
        self.own = self.sum_of(1, *token)
        return self.own

    def terms(self, *token):
        return (self.own, after(self.last, *token))


def per_device(
    text_in, layout_in, token_mask, text_cotangent, layout_cotangent,
    t_in, t_hb, t_out, t_gain, t_shift, t_up, t_ub, t_down,
    l_in, l_hb, l_out, l_gain, l_shift, l_up, l_ub, l_down,
):
    x_size = lax.axis_size("x")
    y, x, c, h, l = (lax.axis_index(a) for a in ALL)
    z = Sizes(
        text_in, layout_in, t_in.shape[2], l_in.shape[2], t_in.shape[3], l_in.shape[3], 2 * x_size
    )
    order = 2 * x + c if x_size == 2 else c
    meta = jnp.stack([y, order, c, (c == h).astype(jnp.int32), l, 0 * y, 0 * y, 0 * y])
    bind = functools.partial
    cols = t_up.shape[2]

    R, W, Q, M = z.rows, z.width, 4 * z.quarter, 4 * z.lquarter
    nh = 2 * z.heads
    flip = lambda v: jnp.swapaxes(v, -1, -2)

    (first,) = call(
        bind(pack_first_body, z), [sds((z.vblock, cols), BF)],
        t_in, t_out, l_in, l_out, t_gain, l_gain, t_shift, l_shift, t_hb, l_hb, t_ub, l_ub,
        scratch=[pltpu.VMEM((16, cols), F32)],
    )
    (rest,) = call(
        bind(pack_rest_body, z), [sds((2, z.block, cols), BF)],
        after(t_up, first), l_up, flip(t_down), flip(l_down), us=10,
    )
    own, send = call(
        bind(entry_body, z), [sds((3 * R + 16, W), BF)] * 2,
        after(text_in, rest), flip(layout_in), text_cotangent, flip(layout_cotangent), token_mask,
        meta=meta, us=10,
    )
    first = first[None]

    first_h = swap(first, "h")
    first_y = after(swap(first, "y"), rest, own)
    pick = lambda index, mine, across: jnp.where(y == index, mine, across)
    a0 = pick(0, first, first_y)
    rest_h = swap(after(rest, a0), "h")
    got = after(swap(send, "c"), a0)
    x0, far0, cot, mask = call(
        bind(settle_body, z), [sds((R, W), BF)] * 3 + [sds((1, z.seq), F32)], own, got, meta=meta, us=10,
    )
    first_h = after(first_h, x0)
    rest_y = after(swap(rest, "y"), first_h)
    f0 = pick(0, rest, rest_y)
    first_hy = swap(first_h, "y")
    rest_h = after(rest_h, first_h, f0)
    a1 = pick(0, first_h, after(first_hy, rest_h))
    parts_hy = [swap(rest_h[p : p + 1], "y") for p in range(2)]
    if x_size == 2:
        far_a = [swap(a0, "x"), swap(a1, "x")]
        far_f0 = swap(f0, "x")
        far_a[0] = after(far_a[0], far_a[1], far_f0, *parts_hy)
        weights = [[join_blocks([a0, a1], far_a)], []]
    else:
        weights = [[gather_blocks([a0, a1], x_size)], []]
    tokens = weights[0][0][0]
    f1 = pick(0, rest_h[0:1], after(parts_hy[0], tokens))
    f2 = pick(0, rest_h[1:2], after(parts_hy[1], tokens))
    x0 = after(x0, f1, f2)

    q_shapes = [sds((nh, R, SLOT), BF), sds((2 * nh, R, SLOT), BF)]
    v_shapes = [sds((16, W), F32), sds((2, 1, Q), F32), sds((2, 1, M), F32)]
    saved = []
    inner = None
    for index in range(2):
        w0 = weights[index][0]
        if index == 0:
            q, kv, kvr, vec, ut, ul = call(
                bind(qkv_body, z, False), q_shapes + q_shapes[1:] + v_shapes, x0, far0, *w0, meta=meta
            )
            xin = x0
        else:
            r2, xin, q, kv, vec, ut, ul = call(
                bind(qkv_body, z, True),
                [sds((R, W), F32), sds((R, W), BF)] + q_shapes + v_shapes,
                *inner, saved[0]["vec"], *w0, meta=meta,
            )
            saved[0]["r2"] = r2
            kvr = swap(kv, "c")
        a, ctx, prob = call(
            bind(attend_body, z),
            [sds((R, W), BF), sds((2, R, 3 * SLOT), BF), sds((nh, R, z.seq), BF)],
            q, kv, kvr, mask, *w0, scratch=[pltpu.VMEM((nh, R, SLOT), BF)], us=8,
        )
        ar = swap(a, "l")
        if index == 0:
            if x_size == 2:
                got = [after(swap(v, "x"), a) for v in (f1, f2)]
                weights[0].append(join_blocks([f0, f1, f2], [far_f0] + got))
            else:
                weights[0].append(gather_blocks([f0, f1, f2], x_size))
            token = weights[0][1][0]
            second = jnp.concatenate([pick(1, first, first_y), pick(1, after(first_h, token), first_hy)])
            got = swap(second, "x") if x_size == 2 else None
            if x_size == 2:
                ar = after(ar, got)
                weights[1].append(join_blocks([second], [got]))
            else:
                weights[1].append(gather_blocks([second], x_size))
            halves = [
                pick(1, after(rest, token), rest_y),
            ] + [pick(1, after(rest_h, token)[p : p + 1], parts_hy[p]) for p in range(2)]
        if index == 1:
            if x_size == 2:
                far2 = swap(halves[2], "x")
                far2, ar = together(far2, ar)
                weights[1].append(near_blocks + join_blocks(halves[1:], [far1, far2]))
            else:
                weights[1].append(gather_blocks(halves, x_size))
        r1, hid, gt, gl, st, sl, f = call(
            bind(forward_body, z),
            [sds((R, W), F32), sds((R, W), BF), sds((2, R, Q), BF), sds((2, R, M), BF),
             sds((2, R, Q), BF), sds((2, R, M), BF), sds((R, W), BF)],
            xin, a, ar, vec, ut, ul, *weights[index][1], us=6,
        )
        fr = swap(f, "l")
        if index == 0 and x_size == 2:
            far_half = swap(after(halves[0], ar), "x")
            far1 = swap(after(halves[1], ar), "x")
            far_half, far1, fr = together(far_half, far1, fr)
            near_blocks = join_blocks(halves[:1], [far_half])
        inner = (hid, f, fr)
        saved.append(dict(x=xin, q=q, kv=kv, kvr=kvr, ctx=ctx, prob=prob, r1=r1, hid=hid, gt=gt,
                          gl=gl, st=st, sl=sl, vec=vec))

    gshape = sds((x_size, 4, z.block, cols), BF)
    vshape = sds((x_size, 2, z.vblock, cols), BF)

    def tail(index, *args):
        keep = saved[index]
        shapes = [sds((R, W), BF), sds((R, W), F32), sds((R, W), BF), sds((2, R, Q), BF),
                  sds((2, R, M), BF), sds((R, W), BF), sds((8, W), F32), sds((2, 1, Q), F32),
                  sds((2, 1, M), F32)]
        return call(
            bind(tail_body, z, "last" if index == 1 else "mid"), shapes,
            *args, keep["vec"], keep["st"], keep["sl"], *weights[index][1], us=7,
        )

    def ffn_grads(index, df, dut, dul, *token):
        keep = saved[index]
        g, s = call(
            bind(ffn_grads_body, z), [gshape] * 2,
            keep["hid"], df, keep["gt"], keep["gl"], dut, dul, us=6,
        )
        return Reduce(g, s, x_size, *token)

    def attend_back(index, d2, dh, dhr):
        keep = saved[index]
        return call(
            bind(attend_back_body, z),
            [sds((R, W), F32), sds((R, W), BF), q_shapes[0], q_shapes[1], q_shapes[1], sds((8, W), F32)],
            d2, dh, dhr, keep["r1"], keep["vec"], *weights[index][0], keep["ctx"], keep["q"],
            keep["kv"], keep["kvr"], keep["prob"], mask,
            scratch=[pltpu.VMEM((nh, R, SLOT), BF), pltpu.VMEM((nh, R, SLOT), F32)], us=14,
        )

    def input_back(index, dq, dkv, back):
        return call(
            bind(input_back_body, z),
            [sds((2, R, 3 * z.quarter), BF), sds((2, R, 3 * z.lquarter), BF), sds((R, W), BF),
             sds((2, 1, 3 * z.quarter), F32), sds((2, 1, 3 * z.lquarter), F32)],
            dq, dkv, back, *weights[index][0],
        )

    def input_grads(index, *args):
        keep = saved[index]
        g0, s0 = call(
            bind(input_grads_body, z), [vshape] * 2, keep["x"], args[0], keep["ctx"], *args[1:],
            scratch=[pltpu.VMEM((16, cols), F32)], meta=meta,
        )
        return Reduce(g0, s0, x_size)

    def leave(summed, *args):
        return call(
            bind(exit_body, z, summed),
            [sds((R, W), BF), sds((R // 2, W), BF), sds((R, W), BF), sds((R // 2, W), BF)], *args,
            meta=meta,
        )

    out, d2, df, dut, dul, dh, va, gut, gul = tail(1, *inner, cot)
    dhr = swap(dh, "l")
    r1f = ffn_grads(1, df, dut, dul, dhr)
    here, part, send, send_far = leave(False, xin, after(out, r1f.keep))
    d1, da, dq, dkv, dkvr, vb = attend_back(1, d2, dh, after(dhr, r1f.keep, here))
    back = swap(dkvr, "c")
    s0 = r1f.x_step(0, vb)
    yt, yl, dxp, gbt, gbl = input_back(1, dq, dkv, after(back, s0))
    dxr = swap(dxp, "l")
    r10 = input_grads(1, da, yt, yl, va, vb, gbt, gbl, gut, gul)
    got, near = swap(after(send, dxp), "y"), swap(after(part, dxp), "h")
    n0 = r1f.near(0, r10.keep)
    s1 = r1f.x_step(1, n0)
    near = after(near, s1)
    got = after(got, near)

    dx1, d2, df, dut, dul, dh, va, gut, gul = tail(
        0, saved[0]["r2"], d1, dxp, after(dxr, r10.keep, n0, s1, got)
    )
    dhr = swap(dh, "l")
    r0f = ffn_grads(0, df, dut, dul)
    n1 = r1f.near(1, r0f.keep)
    s10 = r10.x_step(2, n1)
    far = swap_both(after(send_far, dhr))
    d1, da, dq, dkv, dkvr, vb = attend_back(0, d2, dh, after(dhr, r0f.keep, s10, n1))
    back = swap(dkvr, "c")
    n10 = r10.near(2, vb)
    far = after(far, n10)
    s0 = r0f.x_step(0, n10)
    low = join_rows(near, far)
    yt, yl, dxp, gbt, gbl = input_back(0, dq, dkv, after(back, s0, low))
    dxr = swap(dxp, "l")
    r00 = input_grads(0, da, yt, yl, va, vb, gbt, gbl, gut, gul)
    rest, first = Finish(y), Finish(y)
    y0 = rest.y_step(0, r0f.near(0, r00.keep), n0)
    dxr = after(dxr, y0)

    def sort(here, got, near, far, low):
        kept, sent = call(
            bind(sort_body, z), [sds((2 * R, W), BF), sds((2 * R + 16, W), BF)],
            here, got, near, far, low, meta=meta,
        )
        return kept, swap(sent, "c")

    def place(kept, sent):
        shape = layout_in.shape
        t, l_ = call(
            bind(place_body, z),
            [sds((1,) + text_in.shape, BF), sds((1, shape[0], shape[2], shape[1]), BF)],
            kept, sent, meta=meta,
        )
        return t, flip(l_)

    low = swap(after(low, dxr), "l")
    dhere, dpart, dsend, dsend_far = leave(True, d1, dxp, after(dxr, r00.keep), dx1)
    dgot, dnear, dfar = swap(dsend, "y"), swap(dpart, "h"), swap_both(dsend_far)
    other = rest.sum_of(0, dhere)
    r00.x_step(2, other)
    dgot, dnear, dfar, low, r00.far[2] = together(dgot, dnear, dfar, low, r00.far[2])
    dlow = swap(join_rows(dnear, dfar), "l")
    rest.last = swap(after(other, dlow), "h")
    r0f.x_step(1, dgot)
    first.y_step(2, r00.near(2, dgot), n10)
    dlow, r0f.far[1], first.cross[2] = together(dlow, r0f.far[1], first.cross[2])
    h1 = first.h_step()
    yf = rest.y_step(1, r0f.near(1), n1)
    dkept, dsent = sort(dhere, dgot, dnear, dfar, after(dlow, h1, yf))
    kept, sent = sort(here, got, near, far, after(low, dkept))
    own1 = first.close(kept)
    dx_t, dx_l = place(dkept, after(dsent, own1))
    res_t, res_l = place(kept, after(sent, dx_t))
    own2 = rest.close(res_t)
    like = lambda *arrays: [sds(v.shape, F32) for v in arrays]
    g_tup, g_lup, g_tdn, g_ldn = call(
        bind(finish_body, z), like(t_up, l_up, flip(t_down), flip(l_down)), *rest.terms(own2)
    )
    g_ti, g_tb, g_to, g_tg, g_ts, g_tu, g_li, g_lb, g_lo, g_lg, g_ls, g_lu = call(
        bind(finish_first_body, z),
        like(t_in, t_hb, t_out, t_gain, t_shift, t_ub, l_in, l_hb, l_out, l_gain, l_shift, l_ub),
        *first.terms(g_tup),
    )
    return (
        res_t, res_l, dx_t, dx_l,
        g_ti, g_tb, g_to, g_tg, g_ts, g_tup, g_tu, flip(g_tdn),
        g_li, g_lb, g_lo, g_lg, g_ls, g_lup, g_lu, flip(g_ldn),
    )


def solution(mesh):
    section, dp, tensor = (mesh.shape[a] for a in ("section", "dp", "tensor"))
    fine = Mesh(mesh.devices.reshape(section, dp // 2, 2, 2, tensor // 2), ALL)
    d, t = ("x", "c"), ("h", "l")
    weights = (
        P("y", None, d, t),
        P("y", None, t + d),
        P("y", t, d),
        P("y", None, d),
        P("y", None, d),
        P("y", d, t),
        P("y", t + d),
        P("y", t, d),
    ) * 2
    pages = (P(d, None, None), P(d, None, None))
    return jax.shard_map(
        per_device,
        mesh=fine,
        in_specs=pages + (P(d, None),) + pages + weights,
        out_specs=(P("y", d, None, None),) * 4 + weights,
        check_vma=False,
    )
```
